32 devices in a mesh: grp: 4 (over y, x), col: 8 (over z, core).
Axes of the slice: x: 2, y: 2, z: 4, core: 2. Of those that a mesh axis runs over, the one named last changes fastest.
Arguments:
- proxy_rows: bfloat16 [4, 96, 256, 512], P('grp', 'col'), may hold values from -6 to 6
- pattern: int32 [4, 96, 8], P('grp', 'col'), may hold values from 0 to 1, as said below
- first_pivots: int32 [4, 96, 64], P('grp', 'col'), may hold values from 0 to 255, as said below
- merge_pivots: int32 [4, 3, 4, 12, 64], P('grp'), may hold values from 0 to 127, as said below
- send_counts: int32 [4, 96, 4], P('grp', 'col'), may hold values from 0 to 64, as said below
- near_field: bfloat16 [4, 96, 4, 256, 256], P('grp', 'col'), may hold values from -6 to 6
- self_inverse: bfloat16 [4, 96, 256, 256], P('grp', 'col'), may hold values from -0.375 to 0.375
Outputs:
- interpolation: float32 [4, 96, 64, 256], P('grp', 'col')
- coupling: float32 [4, 96, 64, 256], P('grp', 'col')
The draws below stay inside these ranges and needn't reach their ends.
Inputs may be any that keep to these rules, and one draw needn't show every extreme that they name: `pattern`: in each box, from 4 to 8 blocks are active. `first_pivots`: distinct within each row. `merge_pivots`: distinct within each row. `send_counts`: every box owes 64 rows to at least one group.
All inputs are finite; a program needn't handle non-finite values.
Results may differ from the reference program's by a relative error of at most 0.0003.
Values may be sent and summed in bfloat16 or wider, within the bound.
No kernel may reach another device: no remote copies, remote signals or barrier semaphores. Data moves between devices by JAX's collectives and lax.ppermute only.
A program may use at most 128 MiB of HBM per device.

```python
import jax
import jax.numpy as jnp
from jax import lax

BOX = 256
PROX = 512
PBLK = 64
SKEL = 64
SLOT = 12
NPB = 8
BOXES = 96
ROUNDS = 3
MERGE = 8
N_GRP = 4
N_COL = 8


def first_of_permutations(key, rows, length, keep):
    keys = jax.random.split(key, rows)
    orders = jax.vmap(lambda single: jax.random.permutation(single, length))(keys)
    return orders[:, :keep].astype(jnp.int32)


def draw_pattern(key, part):
    rows = N_GRP * N_COL * SLOT
    keys = jax.random.split(jax.random.fold_in(key, 11), rows)
    ranks = jax.vmap(lambda single: jax.random.permutation(single, NPB))(keys)
    active = jax.random.randint(jax.random.fold_in(key, 12), (rows, 1), NPB // 2, NPB + 1)
    return (ranks < active).astype(jnp.int32).reshape((N_GRP, N_COL * SLOT, NPB))


def draw_first_pivots(key, part):
    rows = N_GRP * N_COL * SLOT
    picked = first_of_permutations(jax.random.fold_in(key, 21), rows, BOX, SKEL)
    return picked.reshape((N_GRP, N_COL * SLOT, SKEL))


def draw_merge_pivots(key, part):
    rows = N_GRP * ROUNDS * (N_COL // 2) * SLOT
    picked = first_of_permutations(jax.random.fold_in(key, 31), rows, 2 * SKEL, SKEL)
    return picked.reshape((N_GRP, ROUNDS, N_COL // 2, SLOT, SKEL))


def draw_send_counts(key, part):
    base = jax.random.randint(jax.random.fold_in(key, 41), (N_GRP, N_COL * SLOT, N_GRP), 0, SKEL + 1)
    full = jax.random.randint(jax.random.fold_in(key, 42), (N_GRP, N_COL * SLOT, 1), 0, N_GRP)
    column = jax.lax.broadcasted_iota(jnp.int32, (N_GRP, N_COL * SLOT, N_GRP), 2)
    return jnp.where(column == full, SKEL, base).astype(jnp.int32)


def block_levels(rng, dims, cuts, low, high):
    level, own = 1.0, jax.random.fold_in(rng, 6)
    for dim, shards_of in cuts:
        steps = jnp.exp(jax.random.uniform(jax.random.fold_in(own, dim), (shards_of,), jnp.float32, low / len(cuts), high / len(cuts)))
        level = level * jnp.repeat(steps, dims[dim] // shards_of).reshape([-1 if axis == dim else 1 for axis in range(len(dims))])
    return level


def noise(own_key, extent, width, limit, shards=(), kind=jnp.bfloat16):
    factor_of = block_levels(own_key, extent, shards, -0.22, 0.18) if shards else 1.0
    drawn = jax.random.normal(own_key, extent, jnp.float32) * width * factor_of
    return jnp.minimum(jnp.maximum(drawn, -limit), limit).astype(kind)


def setup_inputs(seed: int = 0) -> dict:
    arg_keys = jax.random.split(jax.random.key(seed), 8)
    return {
        "proxy_rows": noise(arg_keys[0], (N_GRP, BOXES, BOX, PROX), 1.0, 6.0, ((0, 4), (1, 8))),
        "pattern": draw_pattern(jax.random.fold_in(arg_keys[7], 71), 0),
        "first_pivots": draw_first_pivots(jax.random.fold_in(arg_keys[7], 71), 0),
        "merge_pivots": draw_merge_pivots(jax.random.fold_in(arg_keys[7], 71), 0),
        "send_counts": draw_send_counts(jax.random.fold_in(arg_keys[7], 71), 0),
        "near_field": noise(arg_keys[5], (N_GRP, BOXES, N_GRP, BOX, BOX), 1.0, 6.0, ((0, 4), (1, 8))),
        "self_inverse": noise(arg_keys[6], (N_GRP, BOXES, BOX, BOX), BOX ** -0.5, 0.375, ((0, 4), (1, 8))),
    }


def interpolate(skeleton, masked):
    left = skeleton.astype(jnp.float32)
    whole = masked.astype(jnp.float32)
    gram_matrix = jnp.einsum('bjp,bkp->bjk', left, left, precision=lax.Precision.HIGHEST)
    projected = jnp.einsum('bjp,bup->bju', left, whole, precision=lax.Precision.HIGHEST)
    factor = jnp.linalg.cholesky(gram_matrix)
    halfway = jax.scipy.linalg.solve_triangular(factor, projected, lower=True)
    return jax.scipy.linalg.solve_triangular(factor, halfway, lower=True, trans=1)

def group_interpolation(items):
    proxy_group, pattern_group, first_group, merge_group = items
    row_mask = jnp.repeat(pattern_group, PBLK, axis=1).astype(proxy_group.dtype)
    masked = proxy_group * row_mask[:, None, :]
    candidates = jnp.take_along_axis(masked, first_group[:, :, None], axis=1)
    nodes = candidates.reshape((N_COL, SLOT, SKEL, PROX))
    for section in range(ROUNDS):
        halves = nodes.shape[0] // 2
        paired = nodes.reshape((halves, 2, SLOT, SKEL, PROX))
        merged = jnp.concatenate([paired[:, 0], paired[:, 1]], axis=2)
        chosen = merge_group[section, :halves]
        nodes = jnp.take_along_axis(merged, chosen[..., None], axis=2)
    skeleton = jnp.repeat(nodes, MERGE, axis=0).reshape((N_COL * SLOT, SKEL, PROX))
    return interpolate(skeleton, masked)

def reference(proxy_rows, pattern, first_pivots, merge_pivots, send_counts, near_field, self_inverse):
    interpolation = lax.map(group_interpolation, (proxy_rows, pattern, first_pivots, merge_pivots))
    skel_iota = lax.broadcasted_iota(jnp.int32, (1, 1, SKEL, 1), 2)

    def receive(group_index):
        counts_in = lax.dynamic_index_in_dim(send_counts, group_index, 2, keepdims=False)
        keep = skel_iota < counts_in[:, :, None, None]
        incoming = jnp.where(keep, interpolation, jnp.zeros_like(interpolation))
        near_here = lax.dynamic_index_in_dim(near_field, group_index, 0, keepdims=False)
        inverse_here = lax.dynamic_index_in_dim(self_inverse, group_index, 0, keepdims=False)
        reduced = jnp.einsum('bdvu,buw->bdvw', near_here.astype(jnp.float32), inverse_here.astype(jnp.float32), precision=lax.Precision.HIGHEST)
        return jnp.einsum('dbjw,bdvw->bjv', incoming, reduced, precision=lax.Precision.HIGHEST)
    coupling = lax.map(receive, jnp.arange(N_GRP, dtype=jnp.int32))
    return (interpolation, coupling)
```

```python
import functools

import jax
import jax.numpy as jnp
from jax import lax
from jax.experimental import pallas as pl
from jax.experimental.pallas import tpu as pltpu
from jax.sharding import PartitionSpec as P


F32 = jnp.float32
BF16 = jnp.bfloat16
I32 = jnp.int32
NT = (((1,), (1,)), ((), ()))
NN = (((1,), (0,)), ((), ()))
VMEM = pl.BlockSpec(memory_space=pltpu.VMEM)
ANY = pl.BlockSpec(memory_space=pl.ANY)
Q_MAX = 32767.0


def dot(a, b, dims=NN, precision=None):
    return lax.dot_general(a, b, dims, preferred_element_type=F32, precision=precision)


def iota(shape, dim):
    return lax.broadcasted_iota(I32, shape, dim)


def route_kernel(merge, merge_ref, first_ref, pattern_ref, proxy_ref, compact_ref, where_ref, taken_ref, most_ref, boxes, acc, sems):
    rounds = merge.bit_length() - 1
    slots, unknowns, width = boxes.shape
    skel = first_ref.shape[1]
    room = compact_ref.shape[0]
    copies = [pltpu.make_async_copy(proxy_ref.at[s], boxes.at[s], sems.at[s]) for s in range(slots)]
    for copy in copies:
        copy.start()
    me = lax.axis_index("col")
    final, local = me >> rounds, me & (merge - 1)
    picked = merge_ref[rounds - 1, final]
    upper = (picked >= skel).astype(I32)
    node, row = upper, picked - upper * skel
    for section in range(rounds - 2, -1, -1):
        count = merge >> (section + 1)
        picked = jnp.zeros_like(row)
        for n in range(count):
            found = jnp.take_along_axis(merge_ref[section, final * count + n], row, axis=1)
            picked = jnp.where(node == n, found, picked)
        upper = (picked >= skel).astype(I32)
        node, row = 2 * node + upper, picked - upper * skel
    unknown = jnp.take_along_axis(first_ref[...], row, axis=1)
    before = (iota((skel, skel), 0) < iota((skel, skel), 1)).astype(BF16)
    ones = jnp.ones((skel, skel), BF16)
    above = (iota((slots, slots), 1) < iota((slots, slots), 0)).astype(BF16)
    place = jnp.zeros((slots, skel), F32)
    for d in range(merge):
        here = (node == d).astype(F32).astype(BF16)
        rank = dot(here, before) + dot(dot(above, here).astype(BF16), ones)
        place = jnp.where(node == d, rank, place)
    place = place.astype(I32)
    most_ref[0] = jnp.max(place)
    where_ref[...] = jnp.where(place < room, (node ^ local) * room + place, -1)
    mine = jnp.where(node == local, place, -1)
    taken_ref[...] = jnp.where(node == local, unknown, -1)
    blocks = pattern_ref.shape[1]
    spread = (iota((blocks, width), 1) // (width // blocks) == iota((blocks, width), 0)).astype(F32).astype(BF16)
    mask = dot(pattern_ref[...].astype(F32).astype(BF16), spread)
    for s in range(slots):
        into = (iota((room, skel), 0) == mine[s : s + 1, :]).astype(F32).astype(BF16)
        out_of = (iota((unknowns, skel), 0) == unknown[s : s + 1, :]).astype(F32).astype(BF16)
        move = dot(into, out_of, NT).astype(BF16)
        copies[s].wait()
        part = dot(move, boxes[s]) * mask[s : s + 1, :]
        if s == 0:
            acc[...] = part
        else:
            acc[...] += part
    compact_ref[...] = acc[...].astype(BF16)


def route(merge, room, merge_pivots, first_pivots, pattern, proxy):
    slots, unknowns, width = proxy.shape
    skel = first_pivots.shape[1]
    return pl.pallas_call(
        functools.partial(route_kernel, merge),
        name="route",
        out_shape=[
            jax.ShapeDtypeStruct((room, width), BF16),
            jax.ShapeDtypeStruct((slots, skel), I32),
            jax.ShapeDtypeStruct((slots, skel), I32),
            jax.ShapeDtypeStruct((1,), I32),
        ],
        in_specs=[VMEM, VMEM, VMEM, ANY],
        out_specs=[VMEM, VMEM, VMEM, pl.BlockSpec(memory_space=pltpu.SMEM)],
        scratch_shapes=[
            pltpu.VMEM((slots, unknowns, width), BF16),
            pltpu.VMEM((room, width), F32),
            pltpu.SemaphoreType.DMA((slots,)),
        ],
    )(merge_pivots, first_pivots, pattern, proxy)


def solve_kernel(parts, where_ref, pattern_ref, proxy_ref, *refs):
    piece_refs = refs[:parts]
    interp_ref, coded_ref, scale_ref, boxes, pieces, skeleton, inverse, right, sems, piece_sems = refs[parts:]
    slots, unknowns, width = boxes.shape
    skel = interp_ref.shape[1]
    room = piece_refs[0].shape[0]
    piece_copies = [
        pltpu.make_async_copy(piece_refs[k], pieces.at[pl.ds(k * room, room), :], piece_sems.at[k])
        for k in range(parts)
    ]
    copies = [pltpu.make_async_copy(proxy_ref.at[s], boxes.at[s], sems.at[s]) for s in range(slots)]
    for copy in piece_copies + copies:
        copy.start()
    total = parts * room
    lanes = iota((skel, total), 1)
    for copy in piece_copies:
        copy.wait()
    half = slots // 2
    for s in range(slots):
        choose = (lanes == where_ref[:, s : s + 1]).astype(F32).astype(BF16)
        rows = dot(choose, pieces[...]).astype(BF16)
        skeleton[s] = rows
        gram = dot(rows, rows, NT)
        inverse[s % half, :, (s // half) * skel : (s // half + 1) * skel] = gram
    blocks = pattern_ref.shape[1]
    spread = (iota((blocks, width), 1) // (width // blocks) == iota((blocks, width), 0)).astype(F32).astype(BF16)
    mask = dot(pattern_ref[...].astype(F32).astype(BF16), spread).astype(BF16)
    for s in range(slots):
        copies[s].wait()
        right[s] = dot(skeleton[s] * mask[s : s + 1, :], boxes[s], NT)

    lane = iota((half, skel, 2 * skel), 2)
    column = lane & (skel - 1)
    line = iota((half, skel, 2 * skel), 1)
    offset = iota((half * skel, 2 * skel), 1) & skel

    def eliminate(k, carry):
        a = inverse[...]
        pivot_row = inverse[:, pl.ds(k, 1), :]
        wide = jnp.broadcast_to(pivot_row, (half, 8, 2 * skel)).reshape(half * 8, 2 * skel)
        pivot = jnp.take_along_axis(wide, offset[: half * 8] + k, axis=1)
        reciprocal = 1.0 / pivot
        row = jnp.where((iota((half * 8, 2 * skel), 1) & (skel - 1)) == k, reciprocal, wide * reciprocal)
        row = row.reshape(half, 8, 2 * skel)[:, :1]
        col = jnp.take_along_axis(a.reshape(half * skel, 2 * skel), offset + k, axis=1)
        col = col.reshape(half, skel, 2 * skel)
        col = jnp.where(line == k, -1.0, col)
        kept = jnp.where((line == k) | (column == k), 0.0, a)
        inverse[...] = kept - col * row
        return carry

    lax.fori_loop(0, skel, eliminate, 0)

    diagonal = iota((skel, skel), 0) == iota((skel, skel), 1)
    for s in range(slots):
        inv = inverse[s % half, :, (s // half) * skel : (s // half + 1) * skel]
        x = dot(inv, right[s], NN, lax.Precision.HIGHEST)
        interp_ref[s] = x
        top = jnp.max(jnp.abs(x), axis=1, keepdims=True)
        top = jnp.maximum(top, 1e-30)
        coded = x * (Q_MAX / top)
        coded = (coded + jnp.where(coded >= 0, 0.5, -0.5)).astype(I32)
        coded_ref[s] = coded.astype(jnp.int16)
        scale = jnp.where(diagonal, top * (1.0 / Q_MAX), 0.0)
        scale_ref[s : s + 1, :] = jnp.sum(scale, axis=0, keepdims=True)


def solve(where, pattern, proxy, pieces):
    slots, unknowns, width = proxy.shape
    skel = where.shape[0]
    parts, room = len(pieces), pieces[0].shape[0]
    return pl.pallas_call(
        functools.partial(solve_kernel, parts),
        name="solve",
        out_shape=[
            jax.ShapeDtypeStruct((slots, skel, unknowns), F32),
            jax.ShapeDtypeStruct((slots, skel, unknowns), jnp.int16),
            jax.ShapeDtypeStruct((slots, skel), F32),
        ],
        in_specs=[VMEM, VMEM, ANY] + [ANY] * parts,
        out_specs=[VMEM, VMEM, VMEM],
        scratch_shapes=[
            pltpu.VMEM((slots, unknowns, width), BF16),
            pltpu.VMEM((parts * room, width), BF16),
            pltpu.VMEM((slots, skel, width), BF16),
            pltpu.VMEM((slots // 2, skel, 2 * skel), F32),
            pltpu.VMEM((slots, skel, unknowns), F32),
            pltpu.SemaphoreType.DMA((slots,)),
            pltpu.SemaphoreType.DMA((parts,)),
        ],
    )(where, pattern, proxy, *pieces)


def couple_kernel(groups, near_ref, inverse_ref, own_ref, own_scale_ref, *refs):
    coded_refs, scale_refs, out_ref = refs[: groups - 1], refs[groups - 1 : 2 * groups - 2], refs[-1]
    b = pl.program_id(0)
    skel = out_ref.shape[1]
    here = lax.axis_index("grp")
    diagonal = iota((skel, skel), 0) == iota((skel, skel), 1)
    rows, scales = [], []
    for k in range(groups):
        x = own_ref[0] if k == 0 else coded_refs[k - 1][0].astype(I32).astype(F32)
        scale = (own_scale_ref if k == 0 else scale_refs[k - 1])[pl.ds(b, 1), :]
        rows.append(x)
        scales.append(jnp.sum(jnp.where(diagonal, scale, 0.0), axis=1, keepdims=True))
    x = jnp.concatenate(rows, axis=0)
    high = x.astype(BF16)
    low = (x - high.astype(F32)).astype(BF16)
    turned = dot(high, inverse_ref[0], NT) + dot(low, inverse_ref[0], NT)
    turned = turned * jnp.concatenate(scales, axis=0)
    high = turned.astype(BF16)
    low = (turned - high.astype(F32)).astype(BF16)
    total = None
    for k in range(groups):
        near = near_ref[0, here ^ k]
        part = slice(k * skel, (k + 1) * skel)
        both = jnp.concatenate([high[part], low[part]], axis=0)
        term = dot(both, near, NT)
        total = term if total is None else total + term
    out_ref[0] = total[:skel] + total[skel:]


def couple(near, inverse, own, own_scale, coded, scales):
    boxes, groups, unknowns = near.shape[0], near.shape[1], near.shape[2]
    skel = own.shape[1]
    block = pl.BlockSpec((1, skel, unknowns), lambda b: (b, 0, 0))
    whole = pl.BlockSpec((boxes, skel), lambda b: (0, 0))
    return pl.pallas_call(
        functools.partial(couple_kernel, groups),
        name="couple",
        grid=(boxes,),
        out_shape=jax.ShapeDtypeStruct((boxes, skel, unknowns), F32),
        in_specs=[
            pl.BlockSpec((1, groups, unknowns, unknowns), lambda b: (b, 0, 0, 0)),
            pl.BlockSpec((1, unknowns, unknowns), lambda b: (b, 0, 0)),
            block,
            whole,
        ]
        + [block] * (groups - 1)
        + [whole] * (groups - 1),
        out_specs=block,
    )(near, inverse, own, own_scale, *coded, *scales)


def swap(x, axis, size, k):
    return lax.ppermute(x, axis, [(i, i ^ k) for i in range(size)])


def send_all(merge, room, taken, pattern, proxy, where):
    cols = lax.axis_size("col")
    slots, skel = taken.shape
    width = proxy.shape[2]
    mask = jnp.repeat(pattern, width // pattern.shape[1], axis=1).astype(BF16)
    rows = jnp.take_along_axis(proxy, jnp.maximum(taken, 0)[:, :, None], axis=1) * mask[:, None, :]
    rows = jnp.where(taken[:, :, None] >= 0, rows, jnp.zeros_like(rows)).astype(F32)
    placed = jnp.zeros((cols // merge,) + rows.shape, F32)
    final = lax.axis_index("col") // merge
    placed = lax.dynamic_update_index_in_dim(placed, rows, final, 0)
    summed = lax.psum(placed, "col")
    rows = lax.dynamic_index_in_dim(summed, final, 0, keepdims=False).astype(BF16)
    rows = rows.reshape(slots * skel, width)
    rows = jnp.pad(rows, ((0, merge * room - slots * skel), (0, 0)))
    order = lax.broadcasted_iota(I32, where.shape, 1) * skel + lax.broadcasted_iota(I32, where.shape, 0)
    return (jnp.zeros((), bool), order) + tuple(rows[k * room : (k + 1) * room] for k in range(merge))


def local(proxy_rows, pattern, first_pivots, merge_pivots, send_counts, near_field, self_inverse):
    cols, groups = lax.axis_size("col"), lax.axis_size("grp")
    merge = 1 << min(5, cols.bit_length() - 1)
    slots, skel = first_pivots.shape[1:]
    proxy = proxy_rows[0]
    share = slots * skel // merge
    room = -(-(share * 4) // (3 * 32)) * 32
    compact, where, taken, most = route(merge, room, merge_pivots[0], first_pivots[0], pattern[0], proxy)

    pieces = {0: compact, 1: swap(compact, "col", cols, 1)}
    for k in range(2, merge, 2):
        pieces[k] = swap(compact, "col", cols, k)
    for k in range(2, merge, 2):
        pieces[k + 1] = swap(pieces[k], "col", cols, 1)
    state = (most[0] >= room, where.T) + tuple(pieces[k] for k in range(merge))
    state = lax.while_loop(
        lambda now: now[0], lambda now: send_all(merge, room, taken, pattern[0], proxy, now[1]), state
    )
    interp, coded, scale = solve(state[1], pattern[0], proxy, state[2:])

    keep = lax.broadcasted_iota(I32, (groups, slots, skel), 2) < send_counts[0].T[:, :, None]
    here = lax.axis_index("grp")
    codes, scales = [], []
    for k in range(1, groups):
        owed = lax.dynamic_index_in_dim(keep, here ^ k, 0, keepdims=False)
        codes.append(swap(coded, "grp", groups, k))
        scales.append(swap(jnp.where(owed, scale, 0.0), "grp", groups, k))
    own = lax.dynamic_index_in_dim(keep, here, 0, keepdims=False).astype(F32)
    coupling = couple(near_field[0], self_inverse[0], interp, own, codes, scales)
    return (interp[None], coupling[None])


def solution(mesh):
    return jax.shard_map(
        local,
        mesh=mesh,
        in_specs=(
            P("grp", "col", None, None),
            P("grp", "col", None),
            P("grp", "col", None),
            P("grp", None, None, None, None),
            P("grp", "col", None),
            P("grp", "col", None, None, None),
            P("grp", "col", None, None),
        ),
        out_specs=(P("grp", "col", None, None), P("grp", "col", None, None)),
        check_vma=False,
    )
```

```python
import functools

import jax
import jax.numpy as jnp
from jax import lax
from jax.experimental import pallas as pl
from jax.experimental.pallas import tpu as pltpu
from jax.sharding import PartitionSpec as P


F32 = jnp.float32
BF16 = jnp.bfloat16
I32 = jnp.int32
NT = (((1,), (1,)), ((), ()))
NN = (((1,), (0,)), ((), ()))
TN = (((0,), (0,)), ((), ()))
VMEM = pl.BlockSpec(memory_space=pltpu.VMEM)
ANY = pl.BlockSpec(memory_space=pl.ANY)
Q_MAX = 32000.0
MAIN = 8000.0


def dot(a, b, dims=NN, precision=None):
    return lax.dot_general(a, b, dims, preferred_element_type=F32, precision=precision)


def iota(shape, dim):
    return lax.broadcasted_iota(I32, shape, dim)


def box_masks(pattern_ref, width):
    blocks = pattern_ref.shape[0]
    spread = (iota((blocks, width), 1) // (width // blocks) == iota((blocks, width), 0)).astype(F32).astype(BF16)
    return dot(pattern_ref[...].astype(F32).astype(BF16), spread, TN)


def to_column(row, diagonal):
    return jnp.sum(jnp.where(diagonal, row, 0.0), axis=1, keepdims=True)


def to_row(column, diagonal):
    return jnp.sum(jnp.where(diagonal, column, 0.0), axis=0, keepdims=True)


def route_kernel(
    merge, only, merge_ref, first_ref, pattern_ref, proxy_ref, compact_ref, where_ref, taken_ref, most_ref, boxes, acc, sems
):
    rounds = merge.bit_length() - 1
    slots, unknowns, width = boxes.shape
    skel = first_ref.shape[2]
    room = compact_ref.shape[0]
    copies = [pltpu.make_async_copy(proxy_ref.at[s], boxes.at[s], sems.at[s]) for s in range(slots)]
    for copy in copies:
        copy.start()
    me = lax.axis_index("col")
    final, local = (0 if only else me >> rounds), me & (merge - 1)
    picked = merge_ref[rounds - 1, :, final, :]
    upper = (picked >= skel).astype(I32)
    node, row = upper, picked - upper * skel
    for section in range(rounds - 2, -1, -1):
        count = merge >> (section + 1)
        picked = jnp.zeros_like(row)
        for n in range(count):
            found = jnp.take_along_axis(merge_ref[section, :, final * count + n, :], row, axis=1)
            picked = jnp.where(node == n, found, picked)
        upper = (picked >= skel).astype(I32)
        node, row = 2 * node + upper, picked - upper * skel
    unknown = jnp.take_along_axis(first_ref[:, 0, :], row, axis=1)
    before = (iota((skel, skel), 0) < iota((skel, skel), 1)).astype(BF16)
    ones = jnp.ones((skel, skel), BF16)
    above = (iota((slots, slots), 1) < iota((slots, slots), 0)).astype(BF16)
    place = jnp.zeros((slots, skel), F32)
    for d in range(merge):
        here = (node == d).astype(F32).astype(BF16)
        rank = dot(here, before) + dot(dot(above, here).astype(BF16), ones)
        place = jnp.where(node == d, rank, place)
    place = place.astype(I32)
    most_ref[0] = jnp.max(place)
    where_ref[...] = jnp.where(place < room, (node ^ local) * room + place, -1)
    mine = jnp.where(node == local, place, -1)
    taken_ref[...] = jnp.where(node == local, unknown, -1)
    mask = box_masks(pattern_ref, width)
    for s in range(slots):
        into = (iota((room, skel), 0) == mine[s : s + 1, :]).astype(F32).astype(BF16)
        out_of = (iota((unknowns, skel), 0) == unknown[s : s + 1, :]).astype(F32).astype(BF16)
        move = dot(into, out_of, NT).astype(BF16)
        copies[s].wait()
        part = dot(move, boxes[s]) * mask[s : s + 1, :]
        if s == 0:
            acc[...] = part
        else:
            acc[...] += part
    compact_ref[...] = acc[...].astype(BF16)


def route(merge, room, merge_pivots, first_pivots, pattern, proxy):
    slots, unknowns, width = proxy.shape
    skel = first_pivots.shape[2]
    return pl.pallas_call(
        functools.partial(route_kernel, merge, lax.axis_size("col") == merge),
        name="route",
        out_shape=[
            jax.ShapeDtypeStruct((room, width), BF16),
            jax.ShapeDtypeStruct((slots, skel), I32),
            jax.ShapeDtypeStruct((slots, skel), I32),
            jax.ShapeDtypeStruct((1,), I32),
        ],
        in_specs=[VMEM, VMEM, VMEM, ANY],
        out_specs=[VMEM, VMEM, VMEM, pl.BlockSpec(memory_space=pltpu.SMEM)],
        scratch_shapes=[
            pltpu.VMEM((slots, unknowns, width), BF16),
            pltpu.VMEM((room, width), F32),
            pltpu.SemaphoreType.DMA((slots,)),
        ],
        compiler_params=pltpu.CompilerParams(vmem_limit_bytes=16 << 20),
    )(merge_pivots, first_pivots, pattern, proxy)


def solve_kernel(parts, where_ref, pattern_ref, counts_ref, proxy_ref, *refs):
    piece_refs = refs[:parts]
    interp_ref, coded_ref, pieces, choose, skeleton, inverse, right, tails = refs[parts:]
    slots, unknowns, width = proxy_ref.shape
    skel = interp_ref.shape[1]
    room = piece_refs[0].shape[0]
    total = parts * room
    half = slots // 2
    for k in range(parts):
        pieces[k * room : (k + 1) * room, :] = piece_refs[k][...]
    diagonal = iota((skel, skel), 0) == iota((skel, skel), 1)
    lanes = iota((skel, total), 1)
    for s in range(slots):
        spot = to_column(where_ref[s : s + 1, :].astype(F32), diagonal).astype(I32)
        choose[s * skel : (s + 1) * skel, :] = (lanes == spot).astype(F32).astype(BF16)
    skeleton[...] = dot(choose[...], pieces[...]).astype(BF16)
    mask = box_masks(pattern_ref, width).astype(BF16)
    for s in range(slots):
        rows = skeleton[s * skel : (s + 1) * skel, :]
        inverse[s % half, :, (s // half) * skel : (s // half + 1) * skel] = dot(rows, rows, NT)

    size = (half, skel, 2 * skel)
    flat = (half * skel, 2 * skel)
    lane = iota((half * 8, 2 * skel), 1)
    side = lane & skel
    column = lane & (skel - 1)
    wide_side = iota(flat, 1) & skel
    wide_column = iota(size, 2) & (skel - 1)

    def pick(x, k):
        return jnp.take_along_axis(x, side + k, axis=1)

    def eliminate(step, carry):
        k = 2 * step
        a = inverse[...]
        first = jnp.broadcast_to(inverse[:, pl.ds(k, 1), :], (half, 8, 2 * skel)).reshape(half * 8, 2 * skel)
        second = jnp.broadcast_to(inverse[:, pl.ds(k + 1, 1), :], (half, 8, 2 * skel)).reshape(half * 8, 2 * skel)
        p00, p01, p10, p11 = pick(first, k), pick(first, k + 1), pick(second, k), pick(second, k + 1)
        r0 = 1.0 / p00
        up, down = p01 * r0, p10 * r0
        r1 = 1.0 / (p11 - down * p01)
        at0, at1 = column == k, column == k + 1
        second = jnp.where(at0, -down, jnp.where(at1, 1.0, second - down * first)) * r1
        first = jnp.where(at0, r0, jnp.where(at1, 0.0, first * r0)) - up * second
        first = first.reshape(half, 8, 2 * skel)[:, :1]
        second = second.reshape(half, 8, 2 * skel)[:, :1]
        c0 = jnp.take_along_axis(a.reshape(flat), wide_side + k, axis=1).reshape(size)
        c1 = jnp.take_along_axis(a.reshape(flat), wide_side + (k + 1), axis=1).reshape(size)
        kept = jnp.where((wide_column >> 1) == step, 0.0, a)
        inverse[...] = kept - c0 * first - c1 * second
        inverse[:, pl.ds(k, 1), :] = first
        inverse[:, pl.ds(k + 1, 1), :] = second
        return carry

    lax.fori_loop(0, skel // 2, eliminate, 0)

    for s in range(slots):
        rows = skeleton[s * skel : (s + 1) * skel, :]
        right[s] = dot(proxy_ref[s], rows * mask[s : s + 1, :], NT)
    groups = counts_ref.shape[0]
    unit = (iota((groups, 2 * skel), 0) == iota((groups, 2 * skel), 1)).astype(F32).astype(BF16)
    owed = dot(counts_ref[...].astype(F32).astype(BF16), unit, TN)
    for s in range(slots):
        inv = inverse[s % half, :, (s // half) * skel : (s // half + 1) * skel]
        x = dot(inv, right[s], NT, lax.Precision.HIGHEST)
        interp_ref[s] = x
        top = jnp.maximum(jnp.max(jnp.abs(x), axis=1, keepdims=True), 1e-30)
        power = jnp.clip(jnp.floor(jnp.log2(top)), -100.0, 126.0)
        main = jnp.floor(top * jnp.exp2(-power) * MAIN) + 1.0
        coded = x * ((Q_MAX * MAIN) / (main * jnp.exp2(power)))
        coded = (coded + jnp.where(coded >= 0, 0.5, -0.5)).astype(I32)
        coded_ref[s * skel : (s + 1) * skel, :] = coded.astype(jnp.int16)
        tails[s : s + 1, :] = jnp.concatenate(
            [to_row(main, diagonal), to_row(power, diagonal), owed[s : s + 1, :]], axis=1
        )
    coded_ref[slots * skel :, :] = tails[...].astype(I32).astype(jnp.int16)


def solve(where, pattern, counts, proxy, pieces):
    slots, unknowns, width = proxy.shape
    skel = where.shape[1]
    parts, room = len(pieces), pieces[0].shape[0]
    extra = -(-slots // 16) * 16
    return pl.pallas_call(
        functools.partial(solve_kernel, parts),
        name="solve",
        out_shape=[
            jax.ShapeDtypeStruct((slots, skel, unknowns), F32),
            jax.ShapeDtypeStruct((slots * skel + extra, unknowns), jnp.int16),
        ],
        in_specs=[VMEM] * (4 + parts),
        out_specs=[VMEM, VMEM],
        scratch_shapes=[
            pltpu.VMEM((parts * room, width), BF16),
            pltpu.VMEM((slots * skel, parts * room), BF16),
            pltpu.VMEM((slots * skel, width), BF16),
            pltpu.VMEM((slots // 2, skel, 2 * skel), F32),
            pltpu.VMEM((slots, unknowns, skel), F32),
            pltpu.VMEM((extra, unknowns), F32),
        ],
        compiler_params=pltpu.CompilerParams(vmem_limit_bytes=24 << 20),
    )(where, pattern, counts, proxy, *pieces)


def couple_kernel(groups, near_ref, inverse_ref, own_ref, counts_ref, *refs):
    coded_refs, out_ref = refs[:-1], refs[-1]
    slots, skel, unknowns = out_ref.shape
    here = lax.axis_index("grp")
    diagonal = iota((skel, skel), 0) == iota((skel, skel), 1)

    def owed(counts):
        mine = jnp.where(iota(counts.shape, 1) == here, counts, 0.0)
        return iota((counts.shape[0], skel), 1) < jnp.sum(mine, axis=1, keepdims=True).astype(I32)

    unit = (iota((groups, 2 * skel), 0) == iota((groups, 2 * skel), 1)).astype(F32).astype(BF16)
    scales = [owed(dot(counts_ref[...].astype(F32).astype(BF16), unit, TN)).astype(F32)]
    for ref in coded_refs:
        tail = ref[slots * skel :, :].astype(I32).astype(F32)
        main, power, counts = tail[:, :skel], tail[:, skel : 2 * skel], tail[:, 2 * skel :]
        scales.append(jnp.where(owed(counts), main * jnp.exp2(power) * (1.0 / (MAIN * Q_MAX)), 0.0))
    for b in range(slots):
        rows = [own_ref[b]] + [ref[b * skel : (b + 1) * skel, :].astype(I32).astype(F32) for ref in coded_refs]
        scale = jnp.concatenate([to_column(scales[k][b : b + 1, :], diagonal) for k in range(groups)], axis=0)
        x = jnp.concatenate(rows, axis=0)
        high = x.astype(BF16)
        low = (x - high.astype(F32)).astype(BF16)
        turned = (dot(high, inverse_ref[b], NT) + dot(low, inverse_ref[b], NT)) * scale
        high = turned.astype(BF16)
        low = (turned - high.astype(F32)).astype(BF16)
        total = None
        for k in range(groups):
            part = slice(k * skel, (k + 1) * skel)
            term = dot(jnp.concatenate([high[part], low[part]], axis=0), near_ref[b, here ^ k], NT)
            total = term if total is None else total + term
        out_ref[b] = total[:skel] + total[skel:]


def couple(near, inverse, own, counts, coded):
    groups = near.shape[1]
    return pl.pallas_call(
        functools.partial(couple_kernel, groups),
        name="couple",
        out_shape=jax.ShapeDtypeStruct(own.shape, F32),
        in_specs=[VMEM] * (4 + len(coded)),
        out_specs=VMEM,
        compiler_params=pltpu.CompilerParams(vmem_limit_bytes=24 << 20),
    )(near, inverse, own, counts, *coded)


def swap(x, axis, size, k):
    return lax.ppermute(x, axis, [(i, i ^ k) for i in range(size)])


def send_all(merge, room, taken, pattern, proxy):
    cols = lax.axis_size("col")
    slots, skel = taken.shape
    width = proxy.shape[2]
    mask = jnp.repeat(pattern, width // pattern.shape[1], axis=1).astype(BF16)
    rows = jnp.take_along_axis(proxy, jnp.maximum(taken, 0)[:, :, None], axis=1) * mask[:, None, :]
    rows = jnp.where(taken[:, :, None] >= 0, rows, jnp.zeros_like(rows)).astype(F32)
    placed = jnp.zeros((cols // merge,) + rows.shape, F32)
    final = lax.axis_index("col") // merge
    placed = lax.dynamic_update_index_in_dim(placed, rows, final, 0)
    summed = lax.psum(placed, "col")
    rows = lax.dynamic_index_in_dim(summed, final, 0, keepdims=False).astype(BF16)
    rows = rows.reshape(slots * skel, width)
    rows = jnp.pad(rows, ((0, merge * room - slots * skel), (0, 0)))
    order = lax.broadcasted_iota(I32, taken.shape, 0) * skel + lax.broadcasted_iota(I32, taken.shape, 1)
    return (jnp.zeros((), bool), order) + tuple(rows[k * room : (k + 1) * room] for k in range(merge))


def local(proxy_rows, pattern, first_pivots, merge_pivots, send_counts, near_field, self_inverse):
    cols, groups = lax.axis_size("col"), lax.axis_size("grp")
    merge = 1 << min(5, cols.bit_length() - 1)
    slots, skel = first_pivots.shape[1:]
    proxy = proxy_rows[0]
    share = slots * skel // merge
    room = -(-(share * 4) // (3 * 32)) * 32
    blocks, counts = pattern[0].T, send_counts[0].T
    compact, where, taken, most = route(
        merge, room, jnp.swapaxes(merge_pivots[0], 1, 2), jnp.swapaxes(first_pivots, 0, 1), blocks, proxy
    )

    pieces = {0: compact, 1: swap(compact, "col", cols, 1)}
    for k in range(2, merge, 2):
        pieces[k] = swap(compact, "col", cols, k)
    for k in range(2, merge, 2):
        pieces[k + 1] = swap(pieces[k], "col", cols, 1)
    state = (most[0] >= room, where) + tuple(pieces[k] for k in range(merge))
    state = lax.while_loop(
        lambda now: now[0], lambda now: send_all(merge, room, taken, pattern[0], proxy), state
    )
    interp, coded = solve(state[1], blocks, counts, proxy, state[2:])

    codes = [swap(coded, "grp", groups, k) for k in range(1, groups)]
    coupling = couple(near_field[0], self_inverse[0], interp, counts, codes)
    return (interp[None], coupling[None])


def solution(mesh):
    return jax.shard_map(
        local,
        mesh=mesh,
        in_specs=(
            P("grp", "col", None, None),
            P("grp", "col", None),
            P("grp", "col", None),
            P("grp", None, None, None, None),
            P("grp", "col", None),
            P("grp", "col", None, None, None),
            P("grp", "col", None, None),
        ),
        out_specs=(P("grp", "col", None, None), P("grp", "col", None, None)),
        check_vma=False,
    )
```

```python
import functools

import jax
import jax.numpy as jnp
from jax import lax
from jax.experimental import pallas as pl
from jax.experimental.pallas import tpu as pltpu
from jax.sharding import PartitionSpec as P


F32 = jnp.float32
BF16 = jnp.bfloat16
I32 = jnp.int32
NT = (((1,), (1,)), ((), ()))
NN = (((1,), (0,)), ((), ()))
TN = (((0,), (0,)), ((), ()))
VMEM = pl.BlockSpec(memory_space=pltpu.VMEM)
HBM = pl.BlockSpec(memory_space=pltpu.HBM)
SMEM = pl.BlockSpec(memory_space=pltpu.SMEM)
CHUNKS = 2
Q_MAX = 32000.0
MAIN = 8000.0


def dot(a, b, dims=NN, precision=None):
    return lax.dot_general(a, b, dims, preferred_element_type=F32, precision=precision)


def in_hbm(*arrays):
    return [pltpu.with_memory_space_constraint(x, pltpu.HBM) for x in arrays]


def iota(shape, dim):
    return lax.broadcasted_iota(I32, shape, dim)


def box_masks(pattern_ref, width):
    blocks = pattern_ref.shape[0]
    spread = (iota((blocks, width), 1) // (width // blocks) == iota((blocks, width), 0)).astype(F32).astype(BF16)
    return dot(pattern_ref[...].astype(F32).astype(BF16), spread, TN)


def to_column(row, diagonal):
    return jnp.sum(jnp.where(diagonal, row, 0.0), axis=1, keepdims=True)


def to_row(column, diagonal):
    return jnp.sum(jnp.where(diagonal, column, 0.0), axis=0, keepdims=True)


def route_kernel(merge, only, merge_hbm, first_hbm, pattern_hbm, proxy_ref, *refs):
    compact_refs, where_refs = refs[:CHUNKS], refs[CHUNKS : 2 * CHUNKS]
    taken_ref, most_ref, _, merge_ref, first_ref, pattern_ref, boxes, move, sems = refs[2 * CHUNKS :]
    rounds = merge.bit_length() - 1
    slots, unknowns, width = boxes.shape
    chunk = slots // CHUNKS
    skel = first_ref.shape[2]
    room = compact_refs[0].shape[0]
    tables = ((merge_hbm, merge_ref), (first_hbm, first_ref), (pattern_hbm, pattern_ref))
    tables = [pltpu.make_async_copy(a, b, sems.at[slots + i]) for i, (a, b) in enumerate(tables)]
    copies = [pltpu.make_async_copy(proxy_ref.at[s], boxes.at[s], sems.at[s]) for s in range(slots)]
    for copy in tables + copies:
        copy.start()
    for copy in tables:
        copy.wait()
    me = lax.axis_index("col")
    final, local = (0 if only else me >> rounds), me & (merge - 1)
    picked = merge_ref[rounds - 1, :, final, :]
    upper = (picked >= skel).astype(I32)
    node, row = upper, picked - upper * skel
    for section in range(rounds - 2, -1, -1):
        count = merge >> (section + 1)
        picked = jnp.zeros_like(row)
        for n in range(count):
            found = jnp.take_along_axis(merge_ref[section, :, final * count + n, :], row, axis=1)
            picked = jnp.where(node == n, found, picked)
        upper = (picked >= skel).astype(I32)
        node, row = 2 * node + upper, picked - upper * skel
    unknown = jnp.take_along_axis(first_ref[:, 0, :], row, axis=1)
    before = (iota((skel, skel), 0) < iota((skel, skel), 1)).astype(BF16)
    ones = jnp.ones((skel, skel), BF16)
    later, sooner = iota((slots, slots), 0), iota((slots, slots), 1)
    above = ((sooner < later) & (sooner // chunk == later // chunk)).astype(BF16)
    place = jnp.zeros((slots, skel), F32)
    for d in range(merge):
        here = (node == d).astype(F32).astype(BF16)
        rank = dot(here, before) + dot(dot(above, here).astype(BF16), ones)
        place = jnp.where(node == d, rank, place)
    place = place.astype(I32)
    most_ref[0] = jnp.max(place)
    where = jnp.where(place < room, (node ^ local) * room + place, -1)
    mine = jnp.where(node == local, place, -1)
    taken_ref[...] = jnp.where(node == local, unknown, -1)
    mask = box_masks(pattern_ref, width).astype(BF16)
    kind = iota((8, skel), 0)
    for c in range(CHUNKS):
        where_refs[c][...] = where[c * chunk : (c + 1) * chunk]
        source = jnp.zeros((room, 8), F32)
        for s in range(c * chunk, (c + 1) * chunk):
            into = (iota((room, skel), 0) == mine[s : s + 1, :]).astype(F32).astype(BF16)
            facts = jnp.where(kind == 0, unknown[s : s + 1, :], jnp.where(kind == 1, s + 1, 0))
            source += dot(into, facts.astype(F32).astype(BF16), NT)
        slot = source[:, 1:2].astype(I32) - 1
        source = source[:, 0:1].astype(I32)
        for s in range(c * chunk, (c + 1) * chunk):
            match = iota((room, unknowns), 1) == jnp.where(slot == s, source, -1)
            move[:, s * unknowns : (s + 1) * unknowns] = match.astype(F32).astype(BF16)
        own = (iota((room, slots), 1) == slot).astype(F32).astype(BF16)
        for s in range(c * chunk, (c + 1) * chunk):
            copies[s].wait()
        part = slice(c * chunk * unknowns, (c + 1) * chunk * unknowns)
        held = boxes[c * chunk : (c + 1) * chunk].reshape(chunk * unknowns, width)
        compact_refs[c][...] = (dot(move[:, part], held) * dot(own, mask)).astype(BF16)


def route(merge, room, merge_pivots, first_pivots, pattern, proxy):
    slots, unknowns, width = proxy.shape
    skel = first_pivots.shape[2]
    return pl.pallas_call(
        functools.partial(route_kernel, merge, lax.axis_size("col") == merge),
        name="route",
        out_shape=[jax.ShapeDtypeStruct((room, width), BF16)] * CHUNKS
        + [jax.ShapeDtypeStruct((slots // CHUNKS, skel), I32)] * CHUNKS
        + [
            jax.ShapeDtypeStruct((slots, skel), I32),
            jax.ShapeDtypeStruct((1,), I32),
            jax.ShapeDtypeStruct((slots * skel, width), BF16),
        ],
        in_specs=[HBM] * 4,
        out_specs=[VMEM] * (2 * CHUNKS + 1) + [SMEM, HBM],
        scratch_shapes=[
            pltpu.VMEM(merge_pivots.shape, I32),
            pltpu.VMEM(first_pivots.shape, I32),
            pltpu.VMEM(pattern.shape, I32),
            pltpu.VMEM((slots, unknowns, width), BF16),
            pltpu.VMEM((room, slots * unknowns), BF16),
            pltpu.SemaphoreType.DMA((slots + 3,)),
        ],
        compiler_params=pltpu.CompilerParams(vmem_limit_bytes=16 << 20),
    )(*in_hbm(merge_pivots, first_pivots, pattern, proxy))


def solve_kernel(chunk_index, parts, most_ref, where_ref, pattern_ref, counts_ref, dense_ref, proxy_ref, *refs):
    piece_refs = refs[:parts]
    interp_ref, coded_ref, pieces, choose, skeleton, inverse, tails, found, sems = refs[-9:]
    slots, skel = where_ref.shape
    unknowns, width = proxy_ref.shape[1:]
    base = chunk_index * slots
    room = piece_refs[0].shape[0]
    total = parts * room
    half = slots // 2
    pair = 2 * skel
    diagonal = iota((skel, skel), 0) == iota((skel, skel), 1)

    @pl.when(most_ref[0] < room)
    def _():
        for k in range(parts):
            pieces[k * room : (k + 1) * room, :] = piece_refs[k][...]
        lanes = iota((skel, total), 1)
        for s in range(slots):
            spot = to_column(where_ref[s : s + 1, :].astype(F32), diagonal).astype(I32)
            choose[s * skel : (s + 1) * skel, :] = (lanes == spot).astype(F32).astype(BF16)
        skeleton[...] = dot(choose[...], pieces[...]).astype(BF16)

    @pl.when(most_ref[0] >= room)
    def _():
        copy = pltpu.make_async_copy(dense_ref.at[pl.ds(base * skel, slots * skel), :], skeleton, sems.at[0])
        copy.start()
        copy.wait()

    mask = box_masks(pattern_ref, width).astype(BF16)
    for h in range(half):
        for side in range(2):
            rows = skeleton[(h + side * half) * skel : (h + side * half + 1) * skel, :]
            inverse[h * skel : (h + 1) * skel, side * skel : (side + 1) * skel] = dot(rows, rows, NT)

    small, flat, size = (half * 8, pair), (half * skel, pair), (half, skel, pair)
    side, column = iota(small, 1) & skel, iota(small, 1) & (skel - 1)
    wide_side, wide_column = iota(flat, 1) & skel, iota(size, 2) & (skel - 1)

    def pick(x, k):
        return jnp.take_along_axis(x, side + k, axis=1)

    def line(k):
        rows = [jnp.broadcast_to(inverse[pl.ds(h * skel + k, 1), :], (8, pair)) for h in range(half)]
        return jnp.concatenate(rows, axis=0)

    def eliminate(step, carry):
        k = 2 * step
        a = inverse[...]
        first, second = line(k), line(k + 1)
        p00, p01, p10, p11 = pick(first, k), pick(first, k + 1), pick(second, k), pick(second, k + 1)
        r0 = 1.0 / p00
        up, down = p01 * r0, p10 * r0
        r1 = 1.0 / (p11 - down * p01)
        at0, at1 = column == k, column == k + 1
        second = jnp.where(at0, -down, jnp.where(at1, 1.0, second - down * first)) * r1
        first = jnp.where(at0, r0, jnp.where(at1, 0.0, first * r0)) - up * second
        first = first.reshape(half, 8, pair)[:, :1]
        second = second.reshape(half, 8, pair)[:, :1]
        c0 = jnp.take_along_axis(a, wide_side + k, axis=1).reshape(size)
        c1 = jnp.take_along_axis(a, wide_side + (k + 1), axis=1).reshape(size)
        kept = jnp.where((wide_column >> 1) == step, 0.0, a.reshape(size))
        inverse[...] = (kept - c0 * first - c1 * second).reshape(flat)
        for h in range(half):
            inverse[pl.ds(h * skel + k, 1), :] = first[h]
            inverse[pl.ds(h * skel + k + 1, 1), :] = second[h]
        return carry

    lax.fori_loop(0, skel // 2, eliminate, 0)

    groups = counts_ref.shape[0]
    unit = (iota((groups, unknowns - pair), 0) == iota((groups, unknowns - pair), 1)).astype(F32).astype(BF16)
    owed = dot(counts_ref[...].astype(F32).astype(BF16), unit, TN)
    tails[...] = jnp.zeros_like(tails)
    left = iota((skel, pair), 1) < skel
    blank = jnp.zeros((skel, width), BF16)
    writes = []
    for h in range(half):
        right = None
        for side in range(2):
            s = h + side * half
            rows = skeleton[s * skel : (s + 1) * skel, :] * mask[base + s : base + s + 1, :]
            rows = jnp.concatenate([rows, blank] if side == 0 else [blank, rows], axis=0)
            term = dot(proxy_ref[base + s], rows, NT)
            right = term if right is None else right + term
        both = inverse[h * skel : (h + 1) * skel, :]
        both = jnp.concatenate([jnp.where(left, both, 0.0), jnp.where(left, 0.0, both)], axis=0)
        xs = dot(both, right, NT, lax.Precision.HIGHEST)
        tops = jnp.maximum(jnp.max(jnp.abs(xs), axis=1, keepdims=True), 1e-30)
        powers = jnp.clip(jnp.floor(jnp.log2(tops)), -100.0, 126.0)
        mains = jnp.floor(tops * jnp.exp2(-powers) * MAIN) + 1.0
        codes = xs * ((Q_MAX * MAIN) / (mains * jnp.exp2(powers)))
        codes = (codes + jnp.where(codes >= 0, 0.5, -0.5)).astype(I32).astype(jnp.int16)
        for side in range(2):
            s = h + side * half
            part = slice(side * skel, (side + 1) * skel)
            found[s] = xs[part]
            writes.append(pltpu.make_async_copy(found.at[s], interp_ref.at[base + s], sems.at[1 + s]))
            writes[-1].start()
            coded_ref[s * skel : (s + 1) * skel, :] = codes[part]
            tails[s : s + 1, :] = jnp.concatenate(
                [to_row(mains[part], diagonal), to_row(powers[part], diagonal), owed[base + s : base + s + 1, :]], axis=1
            )
    coded_ref[slots * skel :, :] = tails[...].astype(I32).astype(jnp.int16)
    for copy in writes:
        copy.wait()


def solve(chunk_index, most, where, pattern, counts, dense, proxy, pieces, interp):
    unknowns, width = proxy.shape[1:]
    slots, skel = where.shape
    parts, room = len(pieces), pieces[0].shape[0]
    extra = -(-slots // 16) * 16
    args = [most, where, pattern, counts, *in_hbm(dense), proxy, *pieces] + ([] if interp is None else [interp])
    return pl.pallas_call(
        functools.partial(solve_kernel, chunk_index, parts),
        name="solve",
        out_shape=[
            jax.ShapeDtypeStruct((proxy.shape[0], skel, unknowns), F32),
            jax.ShapeDtypeStruct((slots * skel + extra, unknowns), jnp.int16),
        ],
        in_specs=[SMEM, VMEM, VMEM, VMEM, HBM, VMEM] + [VMEM] * parts + [HBM] * (interp is not None),
        out_specs=[HBM, VMEM],
        input_output_aliases={} if interp is None else {len(args) - 1: 0},
        scratch_shapes=[
            pltpu.VMEM((parts * room, width), BF16),
            pltpu.VMEM((slots * skel, parts * room), BF16),
            pltpu.VMEM((slots * skel, width), BF16),
            pltpu.VMEM((slots // 2 * skel, 2 * skel), F32),
            pltpu.VMEM((extra, unknowns), F32),
            pltpu.VMEM((slots, skel, unknowns), F32),
            pltpu.SemaphoreType.DMA((1 + slots,)),
        ],
        compiler_params=pltpu.CompilerParams(vmem_limit_bytes=24 << 20),
        cost_estimate=pl.CostEstimate(flops=1 << 33, bytes_accessed=8 << 20, transcendentals=0),
    )(*args)


def couple_kernel(chunk_index, groups, near_ref, inverse_ref, own_ref, counts_ref, *refs):
    coded_refs = refs[: groups - 1]
    out_ref, near, inverse, own, out, sems = refs[-6:]
    slots, skel, unknowns = own.shape
    base = chunk_index * slots
    copies = []
    for b in range(slots):
        here = base + b
        for i, (source, target) in enumerate(((own_ref, own), (inverse_ref, inverse), (near_ref, near))):
            copies.append(pltpu.make_async_copy(source.at[here], target.at[b], sems.at[3 * b + i]))
    for copy in copies:
        copy.start()
    here = lax.axis_index("grp")
    diagonal = iota((skel, skel), 0) == iota((skel, skel), 1)

    def owed(counts):
        mine = jnp.where(iota(counts.shape, 1) == here, counts, 0.0)
        return iota((counts.shape[0], skel), 1) < jnp.sum(mine, axis=1, keepdims=True).astype(I32)

    unit = (iota((groups, 2 * skel), 0) == iota((groups, 2 * skel), 1)).astype(F32).astype(BF16)
    mine = dot(counts_ref[...].astype(F32).astype(BF16), unit, TN)
    scales = [owed(mine).astype(F32)[base : base + slots]]
    for ref in coded_refs:
        tail = ref[slots * skel :, :].astype(I32).astype(F32)
        main, power, counts = tail[:, :skel], tail[:, skel : 2 * skel], tail[:, 2 * skel :]
        scales.append(jnp.where(owed(counts), main * jnp.exp2(power) * (1.0 / (MAIN * Q_MAX)), 0.0))
    writes = []
    for b in range(slots):
        for copy in copies[3 * b : 3 * b + 3]:
            copy.wait()
        rows = [own[b]] + [ref[b * skel : (b + 1) * skel, :].astype(I32).astype(F32) for ref in coded_refs]
        scale = jnp.concatenate([to_column(scales[k][b : b + 1, :], diagonal) for k in range(groups)], axis=0)
        x = jnp.concatenate(rows, axis=0)
        high = x.astype(BF16)
        low = (x - high.astype(F32)).astype(BF16)
        turned = (dot(high, inverse[b], NT) + dot(low, inverse[b], NT)) * scale
        high = turned.astype(BF16)
        low = (turned - high.astype(F32)).astype(BF16)
        total = None
        for k in range(groups):
            part = slice(k * skel, (k + 1) * skel)
            term = dot(jnp.concatenate([high[part], low[part]], axis=0), near[b, here ^ k], NT)
            total = term if total is None else total + term
        out[b] = total[:skel] + total[skel:]
        writes.append(pltpu.make_async_copy(out.at[b], out_ref.at[base + b], sems.at[3 * slots + b]))
        writes[-1].start()
    for copy in writes:
        copy.wait()


def couple(chunk_index, near, inverse, own, counts, coded, coupling):
    groups, unknowns = near.shape[1:3]
    slots, skel = own.shape[0] // CHUNKS, own.shape[1]
    args = [*in_hbm(near, inverse, own), counts, *coded] + ([] if coupling is None else [coupling])
    return pl.pallas_call(
        functools.partial(couple_kernel, chunk_index, groups),
        name="couple",
        out_shape=jax.ShapeDtypeStruct(own.shape, F32),
        in_specs=[HBM, HBM, HBM, VMEM] + [VMEM] * len(coded) + [HBM] * (coupling is not None),
        out_specs=HBM,
        input_output_aliases={} if coupling is None else {len(args) - 1: 0},
        scratch_shapes=[
            pltpu.VMEM((slots, groups, unknowns, unknowns), BF16),
            pltpu.VMEM((slots, unknowns, unknowns), BF16),
            pltpu.VMEM((slots, skel, unknowns), F32),
            pltpu.VMEM((slots, skel, unknowns), F32),
            pltpu.SemaphoreType.DMA((4 * slots,)),
        ],
        compiler_params=pltpu.CompilerParams(vmem_limit_bytes=24 << 20),
    )(*args)


def swap(x, axis, size, k):
    return lax.ppermute(x, axis, [(i, i ^ k) for i in range(size)])


def send_all(merge, taken, pattern, proxy):
    cols = lax.axis_size("col")
    slots, skel = taken.shape
    width = proxy.shape[2]
    mask = jnp.repeat(pattern, width // pattern.shape[1], axis=1).astype(BF16)
    rows = jnp.take_along_axis(proxy, jnp.maximum(taken, 0)[:, :, None], axis=1) * mask[:, None, :]
    rows = jnp.where(taken[:, :, None] >= 0, rows, jnp.zeros_like(rows)).astype(F32)
    placed = jnp.zeros((cols // merge,) + rows.shape, F32)
    final = lax.axis_index("col") // merge
    placed = lax.dynamic_update_index_in_dim(placed, rows, final, 0)
    summed = lax.psum(placed, "col")
    rows = lax.dynamic_index_in_dim(summed, final, 0, keepdims=False).astype(BF16)
    return jnp.zeros((), bool), rows.reshape(slots * skel, width)


def local(proxy_rows, pattern, first_pivots, merge_pivots, send_counts, near_field, self_inverse):
    cols, groups = lax.axis_size("col"), lax.axis_size("grp")
    merge = 1 << min(5, cols.bit_length() - 1)
    slots, skel = first_pivots.shape[1:]
    proxy = proxy_rows[0]
    share = slots * skel // merge // CHUNKS
    room = -(-(share * 5) // (3 * 16)) * 16
    blocks, counts = pattern[0].T, send_counts[0].T
    routed = route(merge, room, jnp.swapaxes(merge_pivots[0], 1, 2), jnp.swapaxes(first_pivots, 0, 1), blocks, proxy)
    compacts, wheres, (taken, most, dense) = routed[:CHUNKS], routed[CHUNKS : 2 * CHUNKS], routed[2 * CHUNKS :]

    chunks = []
    for compact in compacts:
        pieces = {0: compact, 1: swap(compact, "col", cols, 1)}
        for k in range(2, merge, 2):
            pieces[k] = swap(compact, "col", cols, k)
        chunks.append(pieces)
    dense = lax.while_loop(
        lambda now: now[0], lambda now: send_all(merge, taken, pattern[0], proxy), (most[0] >= room, dense)
    )[1]
    interp = coupling = coded = None
    codes = []
    for c, pieces in enumerate(chunks):
        if c > 0:
            pieces, coded = lax.optimization_barrier((pieces, coded))
            codes.append([swap(coded, "grp", groups, k) for k in range(1, groups)])
        for k in range(2, merge, 2):
            pieces[k + 1] = swap(pieces[k], "col", cols, 1)
        interp, coded = solve(c, most, wheres[c], blocks, counts, dense, proxy, [pieces[k] for k in range(merge)], interp)
    codes.append([swap(coded, "grp", groups, k) for k in range(1, groups)])
    for c in range(CHUNKS):
        coupling = couple(c, near_field[0], self_inverse[0], interp, counts, codes[c], coupling)
    return (interp[None], coupling[None])


def solution(mesh):
    return jax.shard_map(
        local,
        mesh=mesh,
        in_specs=(
            P("grp", "col", None, None),
            P("grp", "col", None),
            P("grp", "col", None),
            P("grp", None, None, None, None),
            P("grp", "col", None),
            P("grp", "col", None, None, None),
            P("grp", "col", None, None),
        ),
        out_specs=(P("grp", "col", None, None), P("grp", "col", None, None)),
        check_vma=False,
    )
```

```python
import functools

import jax
import jax.numpy as jnp
from jax import lax
from jax.experimental import pallas as pl
from jax.experimental.pallas import tpu as pltpu
from jax.sharding import PartitionSpec as P


F32 = jnp.float32
BF16 = jnp.bfloat16
I32 = jnp.int32
NT = (((1,), (1,)), ((), ()))
NN = (((1,), (0,)), ((), ()))
TN = (((0,), (0,)), ((), ()))
VMEM = pl.BlockSpec(memory_space=pltpu.VMEM)
HBM = pl.BlockSpec(memory_space=pltpu.HBM)
SMEM = pl.BlockSpec(memory_space=pltpu.SMEM)
CHUNKS = 2
PIVOTS = 4
Q_MAX = 32000.0
MAIN = 8000.0


def dot(a, b, dims=NN, precision=None):
    return lax.dot_general(a, b, dims, preferred_element_type=F32, precision=precision)


def in_hbm(*arrays):
    return [pltpu.with_memory_space_constraint(x, pltpu.HBM) for x in arrays]


def iota(shape, dim):
    return lax.broadcasted_iota(I32, shape, dim)


def box_masks(pattern_ref, width):
    blocks = pattern_ref.shape[0]
    spread = (iota((blocks, width), 1) // (width // blocks) == iota((blocks, width), 0)).astype(F32).astype(BF16)
    return dot(pattern_ref[...].astype(F32).astype(BF16), spread, TN)


def to_column(row, diagonal):
    return jnp.sum(jnp.where(diagonal, row, 0.0), axis=1, keepdims=True)


def to_row(column, diagonal):
    return jnp.sum(jnp.where(diagonal, column, 0.0), axis=0, keepdims=True)


def thirds(x):
    high = x.astype(BF16)
    rest = x - high.astype(F32)
    middle = rest.astype(BF16)
    return high, middle, (rest - middle.astype(F32)).astype(BF16)


def exact_dot(a, b):
    a, b = thirds(a), thirds(b)
    order = ((0, 0), (0, 1), (1, 0), (0, 2), (2, 0), (1, 1))
    return dot(jnp.concatenate([a[i] for i, _ in order], axis=1), jnp.concatenate([b[j] for _, j in order], axis=1), NT)


def route_kernel(merge, only, merge_hbm, first_hbm, pattern_hbm, proxy_ref, *refs):
    compact_refs, where_refs = refs[:CHUNKS], refs[CHUNKS : 2 * CHUNKS]
    taken_ref, most_ref, _, merge_ref, first_ref, pattern_ref, boxes, move, sems = refs[2 * CHUNKS :]
    rounds = merge.bit_length() - 1
    slots, unknowns, width = boxes.shape
    chunk = slots // CHUNKS
    skel = first_ref.shape[2]
    room = compact_refs[0].shape[0]
    tables = ((merge_hbm, merge_ref), (first_hbm, first_ref), (pattern_hbm, pattern_ref))
    tables = [pltpu.make_async_copy(a, b, sems.at[slots + i]) for i, (a, b) in enumerate(tables)]
    copies = [pltpu.make_async_copy(proxy_ref.at[s], boxes.at[s], sems.at[s]) for s in range(slots)]
    for copy in tables + copies:
        copy.start()
    for copy in tables:
        copy.wait()
    me = lax.axis_index("col")
    final, local = (0 if only else me >> rounds), me & (merge - 1)
    picked = merge_ref[rounds - 1, :, final, :]
    upper = (picked >= skel).astype(I32)
    node, row = upper, picked - upper * skel
    for section in range(rounds - 2, -1, -1):
        count = merge >> (section + 1)
        picked = jnp.zeros_like(row)
        for n in range(count):
            found = jnp.take_along_axis(merge_ref[section, :, final * count + n, :], row, axis=1)
            picked = jnp.where(node == n, found, picked)
        upper = (picked >= skel).astype(I32)
        node, row = 2 * node + upper, picked - upper * skel
    unknown = jnp.take_along_axis(first_ref[:, 0, :], row, axis=1)
    before = (iota((skel, skel), 0) < iota((skel, skel), 1)).astype(BF16)
    ones = jnp.ones((skel, skel), BF16)
    later, sooner = iota((slots, slots), 0), iota((slots, slots), 1)
    above = ((sooner < later) & (sooner // chunk == later // chunk)).astype(BF16)
    place = jnp.zeros((slots, skel), F32)
    for d in range(merge):
        here = (node == d).astype(F32).astype(BF16)
        rank = dot(here, before) + dot(dot(above, here).astype(BF16), ones)
        place = jnp.where(node == d, rank, place)
    place = place.astype(I32)
    most_ref[0] = jnp.max(place)
    where = jnp.where(place < room, (node ^ local) * room + place, -1)
    mine = jnp.where(node == local, place, -1)
    taken_ref[...] = jnp.where(node == local, unknown, -1)
    mask = box_masks(pattern_ref, width).astype(BF16)
    kind = iota((8, skel), 0)
    for c in range(CHUNKS):
        where_refs[c][...] = where[c * chunk : (c + 1) * chunk]
        source = jnp.zeros((room, 8), F32)
        for s in range(c * chunk, (c + 1) * chunk):
            into = (iota((room, skel), 0) == mine[s : s + 1, :]).astype(F32).astype(BF16)
            facts = jnp.where(kind == 0, unknown[s : s + 1, :], jnp.where(kind == 1, s + 1, 0))
            source += dot(into, facts.astype(F32).astype(BF16), NT)
        slot = source[:, 1:2].astype(I32) - 1
        source = source[:, 0:1].astype(I32)
        for s in range(c * chunk, (c + 1) * chunk):
            match = iota((room, unknowns), 1) == jnp.where(slot == s, source, -1)
            move[:, s * unknowns : (s + 1) * unknowns] = match.astype(F32).astype(BF16)
        own = (iota((room, slots), 1) == slot).astype(F32).astype(BF16)
        for s in range(c * chunk, (c + 1) * chunk):
            copies[s].wait()
        part = slice(c * chunk * unknowns, (c + 1) * chunk * unknowns)
        held = boxes[c * chunk : (c + 1) * chunk].reshape(chunk * unknowns, width)
        compact_refs[c][...] = (dot(move[:, part], held) * dot(own, mask)).astype(BF16)


def route(merge, room, merge_pivots, first_pivots, pattern, proxy):
    slots, unknowns, width = proxy.shape
    skel = first_pivots.shape[2]
    return pl.pallas_call(
        functools.partial(route_kernel, merge, lax.axis_size("col") == merge),
        name="route",
        out_shape=[jax.ShapeDtypeStruct((room, width), BF16)] * CHUNKS
        + [jax.ShapeDtypeStruct((slots // CHUNKS, skel), I32)] * CHUNKS
        + [
            jax.ShapeDtypeStruct((slots, skel), I32),
            jax.ShapeDtypeStruct((1,), I32),
            jax.ShapeDtypeStruct((slots * skel, width), BF16),
        ],
        in_specs=[HBM] * 4,
        out_specs=[VMEM] * (2 * CHUNKS + 1) + [SMEM, HBM],
        scratch_shapes=[
            pltpu.VMEM(merge_pivots.shape, I32),
            pltpu.VMEM(first_pivots.shape, I32),
            pltpu.VMEM(pattern.shape, I32),
            pltpu.VMEM((slots, unknowns, width), BF16),
            pltpu.VMEM((room, slots * unknowns), BF16),
            pltpu.SemaphoreType.DMA((slots + 3,)),
        ],
        compiler_params=pltpu.CompilerParams(vmem_limit_bytes=16 << 20),
    )(*in_hbm(merge_pivots, first_pivots, pattern, proxy))


def solve_kernel(chunk_index, parts, most_ref, where_ref, pattern_ref, counts_ref, dense_ref, proxy_ref, *refs):
    piece_refs = refs[:parts]
    interp_ref, coded_ref, pieces, choose, skeleton, inverse, tails, found, boxes, sems = refs[-10:]
    slots, skel = where_ref.shape
    unknowns, width = proxy_ref.shape[1:]
    base = chunk_index * slots
    room = piece_refs[0].shape[0]
    total = parts * room
    half = slots // 2
    pair = 2 * skel
    diagonal = iota((skel, skel), 0) == iota((skel, skel), 1)
    loads = [pltpu.make_async_copy(proxy_ref.at[base + s], boxes.at[s], sems.at[1 + slots + s]) for s in range(slots)]
    for copy in loads:
        copy.start()

    @pl.when(most_ref[0] < room)
    def _():
        for k in range(parts):
            pieces[k * room : (k + 1) * room, :] = piece_refs[k][...]
        lanes = iota((skel, total), 1)
        for s in range(slots):
            spot = to_column(where_ref[s : s + 1, :].astype(F32), diagonal).astype(I32)
            choose[s * skel : (s + 1) * skel, :] = (lanes == spot).astype(F32).astype(BF16)
        skeleton[...] = dot(choose[...], pieces[...]).astype(BF16)

    @pl.when(most_ref[0] >= room)
    def _():
        copy = pltpu.make_async_copy(dense_ref.at[pl.ds(base * skel, slots * skel), :], skeleton, sems.at[0])
        copy.start()
        copy.wait()

    mask = box_masks(pattern_ref, width).astype(BF16)
    for h in range(half):
        for side in range(2):
            rows = skeleton[(h + side * half) * skel : (h + side * half + 1) * skel, :]
            inverse[h * skel : (h + 1) * skel, side * skel : (side + 1) * skel] = dot(rows, rows, NT)

    side, column, sublane = iota((8, pair), 1) & skel, iota((8, pair), 1) & (skel - 1), iota((8, pair), 0)
    wide_side, wide_column = iota((skel, pair), 1) & skel, iota((skel, pair), 1) & (skel - 1)

    def line(k):
        row = jnp.broadcast_to(inverse[pl.ds(k, 1), :], (8, pair))
        for h in range(1, half):
            row = jnp.where(sublane == h, jnp.broadcast_to(inverse[pl.ds(h * skel + k, 1), :], (8, pair)), row)
        return row

    def eliminate(step, carry):
        k = PIVOTS * step
        span = range(PIVOTS)
        rows = [line(k + i) for i in span]
        small = [[jnp.take_along_axis(rows[i], side + (k + j), axis=1) for j in span] for i in span]
        for p in span:
            r = 1.0 / small[p][p]
            pivot = [r if j == p else small[p][j] * r for j in span]
            for i in span:
                if i != p:
                    f = small[i][p]
                    small[i] = [-f * r if j == p else small[i][j] - f * pivot[j] for j in span]
            small[p] = pivot
        fresh = []
        for i in span:
            row = small[i][0] * rows[0]
            for j in span[1:]:
                row = row + small[i][j] * rows[j]
            for j in span:
                row = jnp.where(column == k + j, small[i][j], row)
            fresh.append(row)
        blocks = [inverse[h * skel : (h + 1) * skel, :] for h in range(half)]
        for h, block in enumerate(blocks):
            kept = jnp.where((wide_column // PIVOTS) == step, 0.0, block)
            for j in span:
                kept = kept - jnp.take_along_axis(block, wide_side + (k + j), axis=1) * fresh[j][h : h + 1, :]
            inverse[h * skel : (h + 1) * skel, :] = kept
        for h in range(half):
            for j in span:
                inverse[pl.ds(h * skel + k + j, 1), :] = fresh[j][h : h + 1, :]
        return carry

    lax.fori_loop(0, skel // PIVOTS, eliminate, 0)
    for copy in loads:
        copy.wait()

    groups = counts_ref.shape[0]
    unit = (iota((groups, unknowns - pair), 0) == iota((groups, unknowns - pair), 1)).astype(F32).astype(BF16)
    owed = dot(counts_ref[...].astype(F32).astype(BF16), unit, TN)
    tails[...] = jnp.zeros_like(tails)
    left = iota((skel, pair), 1) < skel
    blank = jnp.zeros((skel, width), BF16)
    writes = []
    for h in range(half):
        right = None
        for side in range(2):
            s = h + side * half
            rows = skeleton[s * skel : (s + 1) * skel, :] * mask[base + s : base + s + 1, :]
            rows = jnp.concatenate([rows, blank] if side == 0 else [blank, rows], axis=0)
            term = dot(boxes[s], rows, NT)
            right = term if right is None else right + term
        both = inverse[h * skel : (h + 1) * skel, :]
        both = jnp.concatenate([jnp.where(left, both, 0.0), jnp.where(left, 0.0, both)], axis=0)
        xs = exact_dot(both, right)
        tops = jnp.maximum(jnp.max(jnp.abs(xs), axis=1, keepdims=True), 1e-30)
        powers = jnp.clip(jnp.floor(jnp.log2(tops)), -100.0, 126.0)
        mains = jnp.floor(tops * jnp.exp2(-powers) * MAIN) + 1.0
        codes = xs * ((Q_MAX * MAIN) / (mains * jnp.exp2(powers)))
        codes = (codes + jnp.where(codes >= 0, 0.5, -0.5)).astype(I32).astype(jnp.int16)
        for side in range(2):
            s = h + side * half
            part = slice(side * skel, (side + 1) * skel)
            found[s] = xs[part]
            writes.append(pltpu.make_async_copy(found.at[s], interp_ref.at[base + s], sems.at[1 + s]))
            writes[-1].start()
            coded_ref[s * skel : (s + 1) * skel, :] = codes[part]
            tails[s : s + 1, :] = jnp.concatenate(
                [to_row(mains[part], diagonal), to_row(powers[part], diagonal), owed[base + s : base + s + 1, :]], axis=1
            )
    coded_ref[slots * skel :, :] = tails[...].astype(I32).astype(jnp.int16)
    for copy in writes:
        copy.wait()


def solve(chunk_index, most, where, pattern, counts, dense, proxy, pieces, interp):
    unknowns, width = proxy.shape[1:]
    slots, skel = where.shape
    parts, room = len(pieces), pieces[0].shape[0]
    extra = -(-slots // 16) * 16
    args = [most, where, pattern, counts, *in_hbm(dense, proxy), *pieces] + ([] if interp is None else [interp])
    return pl.pallas_call(
        functools.partial(solve_kernel, chunk_index, parts),
        name="solve",
        out_shape=[
            jax.ShapeDtypeStruct((proxy.shape[0], skel, unknowns), F32),
            jax.ShapeDtypeStruct((slots * skel + extra, unknowns), jnp.int16),
        ],
        in_specs=[SMEM, VMEM, VMEM, VMEM, HBM, HBM] + [VMEM] * parts + [HBM] * (interp is not None),
        out_specs=[HBM, VMEM],
        input_output_aliases={} if interp is None else {len(args) - 1: 0},
        scratch_shapes=[
            pltpu.VMEM((parts * room, width), BF16),
            pltpu.VMEM((slots * skel, parts * room), BF16),
            pltpu.VMEM((slots * skel, width), BF16),
            pltpu.VMEM((slots // 2 * skel, 2 * skel), F32),
            pltpu.VMEM((extra, unknowns), F32),
            pltpu.VMEM((slots, skel, unknowns), F32),
            pltpu.VMEM((slots, unknowns, width), BF16),
            pltpu.SemaphoreType.DMA((1 + 2 * slots,)),
        ],
        compiler_params=pltpu.CompilerParams(vmem_limit_bytes=24 << 20),
        cost_estimate=pl.CostEstimate(flops=1 << 33, bytes_accessed=8 << 20, transcendentals=0),
    )(*args)


def couple_kernel(chunk_index, groups, near_ref, inverse_ref, own_ref, counts_ref, *refs):
    coded_refs = refs[: groups - 1]
    out_ref, near, inverse, own, out, turns, sems = refs[-7:]
    slots, skel, unknowns = own.shape
    base = chunk_index * slots
    part = pl.ds(base, slots)
    tables = [pltpu.make_async_copy(own_ref.at[part], own, sems.at[0]), pltpu.make_async_copy(inverse_ref.at[part], inverse, sems.at[1])]
    copies = [pltpu.make_async_copy(near_ref.at[base + b], near.at[b], sems.at[2 + b]) for b in range(slots)]
    for copy in tables + copies:
        copy.start()
    here = lax.axis_index("grp")
    diagonal = iota((skel, skel), 0) == iota((skel, skel), 1)

    def owed(counts):
        mine = jnp.where(iota(counts.shape, 1) == here, counts, 0.0)
        return iota((counts.shape[0], skel), 1) < jnp.sum(mine, axis=1, keepdims=True).astype(I32)

    unit = (iota((groups, 2 * skel), 0) == iota((groups, 2 * skel), 1)).astype(F32).astype(BF16)
    mine = dot(counts_ref[...].astype(F32).astype(BF16), unit, TN)
    scales = [owed(mine).astype(F32)[base : base + slots]]
    for ref in coded_refs:
        tail = ref[slots * skel :, :].astype(I32).astype(F32)
        main, power, counts = tail[:, :skel], tail[:, skel : 2 * skel], tail[:, 2 * skel :]
        scales.append(jnp.where(owed(counts), main * jnp.exp2(power) * (1.0 / (MAIN * Q_MAX)), 0.0))
    for copy in tables:
        copy.wait()
    for b in range(slots):
        rows = [own[b]] + [ref[b * skel : (b + 1) * skel, :].astype(I32).astype(F32) for ref in coded_refs]
        for k in range(groups):
            high = rows[k].astype(BF16)
            low = (rows[k] - high.astype(F32)).astype(BF16)
            turned = dot(jnp.concatenate([high, low], axis=0), inverse[b], NT)
            turned = (turned[:skel] + turned[skel:]) * to_column(scales[k][b : b + 1, :], diagonal)
            high = turned.astype(BF16)
            turns[b, k, :skel, :] = high
            turns[b, k, skel:, :] = (turned - high.astype(F32)).astype(BF16)
    for copy in copies:
        copy.wait()
    writes = []
    for b in range(slots):
        total = None
        for k in range(groups):
            term = dot(turns[b, k], near[b, here ^ k], NT)
            total = term if total is None else total + term
        out[b] = total[:skel] + total[skel:]
        writes.append(pltpu.make_async_copy(out.at[b], out_ref.at[base + b], sems.at[2 + slots + b]))
        writes[-1].start()
    for copy in writes:
        copy.wait()


def couple(chunk_index, near, inverse, own, counts, coded, coupling):
    groups, unknowns = near.shape[1:3]
    slots, skel = own.shape[0] // CHUNKS, own.shape[1]
    args = [*in_hbm(near, inverse, own), counts, *coded] + ([] if coupling is None else [coupling])
    return pl.pallas_call(
        functools.partial(couple_kernel, chunk_index, groups),
        name="couple",
        out_shape=jax.ShapeDtypeStruct(own.shape, F32),
        in_specs=[HBM, HBM, HBM, VMEM] + [VMEM] * len(coded) + [HBM] * (coupling is not None),
        out_specs=HBM,
        input_output_aliases={} if coupling is None else {len(args) - 1: 0},
        scratch_shapes=[
            pltpu.VMEM((slots, groups, unknowns, unknowns), BF16),
            pltpu.VMEM((slots, unknowns, unknowns), BF16),
            pltpu.VMEM((slots, skel, unknowns), F32),
            pltpu.VMEM((slots, skel, unknowns), F32),
            pltpu.VMEM((slots, groups, 2 * skel, unknowns), BF16),
            pltpu.SemaphoreType.DMA((2 + 2 * slots,)),
        ],
        compiler_params=pltpu.CompilerParams(vmem_limit_bytes=24 << 20),
    )(*args)


def swap(x, axis, size, k):
    return lax.ppermute(x, axis, [(i, i ^ k) for i in range(size)])


def send_all(merge, taken, pattern, proxy):
    cols = lax.axis_size("col")
    slots, skel = taken.shape
    width = proxy.shape[2]
    mask = jnp.repeat(pattern, width // pattern.shape[1], axis=1).astype(BF16)
    rows = jnp.take_along_axis(proxy, jnp.maximum(taken, 0)[:, :, None], axis=1) * mask[:, None, :]
    rows = jnp.where(taken[:, :, None] >= 0, rows, jnp.zeros_like(rows)).astype(F32)
    placed = jnp.zeros((cols // merge,) + rows.shape, F32)
    final = lax.axis_index("col") // merge
    placed = lax.dynamic_update_index_in_dim(placed, rows, final, 0)
    summed = lax.psum(placed, "col")
    rows = lax.dynamic_index_in_dim(summed, final, 0, keepdims=False).astype(BF16)
    return jnp.zeros((), bool), rows.reshape(slots * skel, width)


def local(proxy_rows, pattern, first_pivots, merge_pivots, send_counts, near_field, self_inverse):
    cols, groups = lax.axis_size("col"), lax.axis_size("grp")
    merge = 1 << min(5, cols.bit_length() - 1)
    slots, skel = first_pivots.shape[1:]
    proxy = proxy_rows[0]
    share = slots * skel // merge // CHUNKS
    room = -(-(share * 5) // (3 * 16)) * 16
    blocks, counts = pattern[0].T, send_counts[0].T
    routed = route(merge, room, jnp.swapaxes(merge_pivots[0], 1, 2), jnp.swapaxes(first_pivots, 0, 1), blocks, proxy)
    compacts, wheres, (taken, most, dense) = routed[:CHUNKS], routed[CHUNKS : 2 * CHUNKS], routed[2 * CHUNKS :]

    chunks = []
    for compact in compacts:
        pieces = {0: compact, 1: swap(compact, "col", cols, 1)}
        for k in range(2, merge, 2):
            pieces[k] = swap(compact, "col", cols, k)
        chunks.append(pieces)
    dense = lax.while_loop(
        lambda now: now[0], lambda now: send_all(merge, taken, pattern[0], proxy), (most[0] >= room, dense)
    )[1]
    interp = coupling = coded = None
    codes = []
    for c, pieces in enumerate(chunks):
        if c > 0:
            pieces, coded = lax.optimization_barrier((pieces, coded))
            codes.append([swap(coded, "grp", groups, k) for k in range(1, groups)])
        for k in range(2, merge, 2):
            pieces[k + 1] = swap(pieces[k], "col", cols, 1)
        interp, coded = solve(c, most, wheres[c], blocks, counts, dense, proxy, [pieces[k] for k in range(merge)], interp)
    codes.append([swap(coded, "grp", groups, k) for k in range(1, groups)])
    for c in range(CHUNKS):
        coupling = couple(c, near_field[0], self_inverse[0], interp, counts, codes[c], coupling)
    return (interp[None], coupling[None])


def solution(mesh):
    return jax.shard_map(
        local,
        mesh=mesh,
        in_specs=(
            P("grp", "col", None, None),
            P("grp", "col", None),
            P("grp", "col", None),
            P("grp", None, None, None, None),
            P("grp", "col", None),
            P("grp", "col", None, None, None),
            P("grp", "col", None, None),
        ),
        out_specs=(P("grp", "col", None, None), P("grp", "col", None, None)),
        check_vma=False,
    )
```

```python
import functools

import jax
import jax.numpy as jnp
from jax import lax
from jax.experimental import pallas as pl
from jax.experimental.pallas import tpu as pltpu
from jax.sharding import PartitionSpec as P


F32 = jnp.float32
BF16 = jnp.bfloat16
I32 = jnp.int32
NT = (((1,), (1,)), ((), ()))
NN = (((1,), (0,)), ((), ()))
TN = (((0,), (0,)), ((), ()))
VMEM = pl.BlockSpec(memory_space=pltpu.VMEM)
HBM = pl.BlockSpec(memory_space=pltpu.HBM)
SMEM = pl.BlockSpec(memory_space=pltpu.SMEM)
PIVOTS = 4
Q_MAX = 32000.0
MAIN = 8000.0


def dot(a, b, dims=NN, precision=None):
    return lax.dot_general(a, b, dims, preferred_element_type=F32, precision=precision)


def in_hbm(*arrays):
    return [pltpu.with_memory_space_constraint(x, pltpu.HBM) for x in arrays]


def iota(shape, dim):
    return lax.broadcasted_iota(I32, shape, dim)


def box_masks(pattern_ref, width):
    blocks = pattern_ref.shape[0]
    spread = (iota((blocks, width), 1) // (width // blocks) == iota((blocks, width), 0)).astype(F32).astype(BF16)
    return dot(pattern_ref[...].astype(F32).astype(BF16), spread, TN)


def to_column(row, diagonal):
    return jnp.sum(jnp.where(diagonal, row, 0.0), axis=1, keepdims=True)


def to_row(column, diagonal):
    return jnp.sum(jnp.where(diagonal, column, 0.0), axis=0, keepdims=True)


def thirds(x):
    high = x.astype(BF16)
    rest = x - high.astype(F32)
    middle = rest.astype(BF16)
    return high, middle, (rest - middle.astype(F32)).astype(BF16)


def exact_dot(a, b):
    a, b = thirds(a), thirds(b)
    order = ((0, 0), (0, 1), (1, 0), (0, 2), (2, 0), (1, 1))
    return dot(jnp.concatenate([a[i] for i, _ in order], axis=1), jnp.concatenate([b[j] for _, j in order], axis=1), NT)


def route_kernel(merge, only, merge_hbm, first_hbm, pattern_hbm, proxy_ref, *refs):
    compact_ref, where_ref, taken_ref, most_ref, _, merge_ref, first_ref, pattern_ref, boxes, move, sems = refs
    rounds = merge.bit_length() - 1
    slots, unknowns, width = boxes.shape
    skel = first_ref.shape[2]
    room = compact_ref.shape[0]
    tables = ((merge_hbm, merge_ref), (first_hbm, first_ref), (pattern_hbm, pattern_ref))
    tables = [pltpu.make_async_copy(a, b, sems.at[slots + i]) for i, (a, b) in enumerate(tables)]
    copies = [pltpu.make_async_copy(proxy_ref.at[s], boxes.at[s], sems.at[s]) for s in range(slots)]
    for copy in tables + copies:
        copy.start()
    for copy in tables:
        copy.wait()
    me = lax.axis_index("col")
    final, local = (0 if only else me >> rounds), me & (merge - 1)
    picked = merge_ref[rounds - 1, :, final, :]
    upper = (picked >= skel).astype(I32)
    node, row = upper, picked - upper * skel
    for section in range(rounds - 2, -1, -1):
        count = merge >> (section + 1)
        picked = jnp.zeros_like(row)
        for n in range(count):
            found = jnp.take_along_axis(merge_ref[section, :, final * count + n, :], row, axis=1)
            picked = jnp.where(node == n, found, picked)
        upper = (picked >= skel).astype(I32)
        node, row = 2 * node + upper, picked - upper * skel
    unknown = jnp.take_along_axis(first_ref[:, 0, :], row, axis=1)
    before = (iota((skel, skel), 0) < iota((skel, skel), 1)).astype(BF16)
    ones = jnp.ones((skel, skel), BF16)
    above = (iota((slots, slots), 1) < iota((slots, slots), 0)).astype(BF16)
    place = jnp.zeros((slots, skel), F32)
    for d in range(merge):
        here = (node == d).astype(F32).astype(BF16)
        rank = dot(here, before) + dot(dot(above, here).astype(BF16), ones)
        place = jnp.where(node == d, rank, place)
    place = place.astype(I32)
    most_ref[0] = jnp.max(place)
    where_ref[...] = jnp.where(place < room, (node ^ local) * room + place, -1)
    mine = jnp.where(node == local, place, -1)
    taken_ref[...] = jnp.where(node == local, unknown, -1)
    mask = box_masks(pattern_ref, width).astype(BF16)
    kind = iota((8, skel), 0)
    source = jnp.zeros((room, 8), F32)
    for s in range(slots):
        into = (iota((room, skel), 0) == mine[s : s + 1, :]).astype(F32).astype(BF16)
        facts = jnp.where(kind == 0, unknown[s : s + 1, :], jnp.where(kind == 1, s + 1, 0))
        source += dot(into, facts.astype(F32).astype(BF16), NT)
    slot = source[:, 1:2].astype(I32) - 1
    source = source[:, 0:1].astype(I32)
    for s in range(slots):
        match = iota((room, unknowns), 1) == jnp.where(slot == s, source, -1)
        move[:, s * unknowns : (s + 1) * unknowns] = match.astype(F32).astype(BF16)
    own = (iota((room, slots), 1) == slot).astype(F32).astype(BF16)
    for copy in copies:
        copy.wait()
    rows = dot(move[...], boxes[...].reshape(slots * unknowns, width)) * dot(own, mask)
    compact_ref[...] = rows.astype(BF16)


def route(merge, room, merge_pivots, first_pivots, pattern, proxy):
    slots, unknowns, width = proxy.shape
    skel = first_pivots.shape[2]
    return pl.pallas_call(
        functools.partial(route_kernel, merge, lax.axis_size("col") == merge),
        name="route",
        out_shape=[
            jax.ShapeDtypeStruct((room, width), BF16),
            jax.ShapeDtypeStruct((slots, skel), I32),
            jax.ShapeDtypeStruct((slots, skel), I32),
            jax.ShapeDtypeStruct((1,), I32),
            jax.ShapeDtypeStruct((slots * skel, width), BF16),
        ],
        in_specs=[HBM] * 4,
        out_specs=[VMEM, VMEM, VMEM, SMEM, HBM],
        scratch_shapes=[
            pltpu.VMEM(merge_pivots.shape, I32),
            pltpu.VMEM(first_pivots.shape, I32),
            pltpu.VMEM(pattern.shape, I32),
            pltpu.VMEM((slots, unknowns, width), BF16),
            pltpu.VMEM((room, slots * unknowns), BF16),
            pltpu.SemaphoreType.DMA((slots + 3,)),
        ],
        compiler_params=pltpu.CompilerParams(vmem_limit_bytes=16 << 20),
    )(*in_hbm(merge_pivots, first_pivots, pattern, proxy))


def solve_kernel(base, slots, parts, most_ref, where_ref, pattern_ref, counts_ref, dense_ref, proxy_ref, *refs):
    piece_refs = refs[:parts]
    interp_ref, coded_ref, pieces, choose, skeleton, inverse, tails, found, boxes, weights, right, sems = refs[-12:]
    skel = where_ref.shape[1]
    unknowns, width = proxy_ref.shape[1:]
    room = piece_refs[0].shape[0]
    total = parts * room
    half = slots // 2
    pair = 2 * skel
    diagonal = iota((skel, skel), 0) == iota((skel, skel), 1)
    loads = [pltpu.make_async_copy(proxy_ref.at[base + s], boxes.at[s], sems.at[1 + slots + s]) for s in range(slots)]
    for copy in loads:
        copy.start()

    @pl.when(most_ref[0] < room)
    def _():
        for k in range(parts):
            pieces[k * room : (k + 1) * room, :] = piece_refs[k][...]
        lanes = iota((skel, total), 1)
        for s in range(slots):
            spot = to_column(where_ref[base + s : base + s + 1, :].astype(F32), diagonal).astype(I32)
            choose[s * skel : (s + 1) * skel, :] = (lanes == spot).astype(F32).astype(BF16)
        skeleton[...] = dot(choose[...], pieces[...]).astype(BF16)

    @pl.when(most_ref[0] >= room)
    def _():
        copy = pltpu.make_async_copy(dense_ref.at[pl.ds(base * skel, slots * skel), :], skeleton, sems.at[0])
        copy.start()
        copy.wait()

    mask = box_masks(pattern_ref, width).astype(BF16)
    for h in range(half):
        for side in range(2):
            rows = skeleton[(h + side * half) * skel : (h + side * half + 1) * skel, :]
            inverse[h * skel : (h + 1) * skel, side * skel : (side + 1) * skel] = dot(rows, rows, NT)

    side, column, sublane = iota((8, pair), 1) & skel, iota((8, pair), 1) & (skel - 1), iota((8, pair), 0)
    wide_side, wide_column = iota((skel, pair), 1) & skel, iota((skel, pair), 1) & (skel - 1)

    blank = jnp.zeros((skel, width), BF16)
    for s in range(slots):
        rows = skeleton[s * skel : (s + 1) * skel, :] * mask[base + s : base + s + 1, :]
        weights[s] = jnp.concatenate([rows, blank] if s < half else [blank, rows], axis=0)
    for copy in loads:
        copy.wait()
    steps = skel // PIVOTS
    stretch = unknowns
    while slots * unknowns <= steps * stretch // 2:
        stretch //= 2
    turns = unknowns // stretch

    def line(k):
        row = jnp.broadcast_to(inverse[pl.ds(k, 1), :], (8, pair))
        for h in range(1, half):
            row = jnp.where(sublane == h, jnp.broadcast_to(inverse[pl.ds(h * skel + k, 1), :], (8, pair)), row)
        return row

    def eliminate(step, carry):
        k = PIVOTS * step
        span = range(PIVOTS)
        rows = [line(k + i) for i in span]
        small = [[jnp.take_along_axis(rows[i], side + (k + j), axis=1) for j in span] for i in span]
        for p in span:
            r = 1.0 / small[p][p]
            pivot = [r if j == p else small[p][j] * r for j in span]
            for i in span:
                if i != p:
                    f = small[i][p]
                    small[i] = [-f * r if j == p else small[i][j] - f * pivot[j] for j in span]
            small[p] = pivot
        fresh = []
        for i in span:
            row = small[i][0] * rows[0]
            for j in span[1:]:
                row = row + small[i][j] * rows[j]
            for j in span:
                row = jnp.where(column == k + j, small[i][j], row)
            fresh.append(row)
        blocks = [inverse[h * skel : (h + 1) * skel, :] for h in range(half)]
        for h, block in enumerate(blocks):
            kept = jnp.where((wide_column // PIVOTS) == step, 0.0, block)
            for j in span:
                kept = kept - jnp.take_along_axis(block, wide_side + (k + j), axis=1) * fresh[j][h : h + 1, :]
            inverse[h * skel : (h + 1) * skel, :] = kept
        for h in range(half):
            for j in span:
                inverse[pl.ds(h * skel + k + j, 1), :] = fresh[j][h : h + 1, :]
        turn = jnp.minimum(step, slots * turns - 1)
        box, part = turn // turns, pl.ds(pl.multiple_of((turn % turns) * stretch, stretch), stretch)
        right[box, part, :] = dot(boxes[box, part, :], weights[box], NT)
        return carry

    lax.fori_loop(0, steps, eliminate, 0)

    groups = counts_ref.shape[0]
    unit = (iota((groups, unknowns - pair), 0) == iota((groups, unknowns - pair), 1)).astype(F32).astype(BF16)
    owed = dot(counts_ref[...].astype(F32).astype(BF16), unit, TN)
    tails[...] = jnp.zeros_like(tails)
    left = iota((skel, pair), 1) < skel
    writes = []
    for h in range(half):
        both = inverse[h * skel : (h + 1) * skel, :]
        both = jnp.concatenate([jnp.where(left, both, 0.0), jnp.where(left, 0.0, both)], axis=0)
        xs = exact_dot(both, right[h] + right[h + half])
        tops = jnp.maximum(jnp.max(jnp.abs(xs), axis=1, keepdims=True), 1e-30)
        powers = jnp.clip(jnp.floor(jnp.log2(tops)), -100.0, 126.0)
        mains = jnp.floor(tops * jnp.exp2(-powers) * MAIN) + 1.0
        codes = xs * ((Q_MAX * MAIN) / (mains * jnp.exp2(powers)))
        codes = (codes + jnp.where(codes >= 0, 0.5, -0.5)).astype(I32).astype(jnp.int16)
        for side in range(2):
            s = h + side * half
            part = slice(side * skel, (side + 1) * skel)
            found[s] = xs[part]
            writes.append(pltpu.make_async_copy(found.at[s], interp_ref.at[base + s], sems.at[1 + s]))
            writes[-1].start()
            coded_ref[s * skel : (s + 1) * skel, :] = codes[part]
            tails[s : s + 1, :] = jnp.concatenate(
                [to_row(mains[part], diagonal), to_row(powers[part], diagonal), owed[base + s : base + s + 1, :]], axis=1
            )
    coded_ref[slots * skel :, :] = tails[...].astype(I32).astype(jnp.int16)
    for copy in writes:
        copy.wait()


def solve(base, slots, most, where, pattern, counts, dense, proxy, pieces, interp):
    unknowns, width = proxy.shape[1:]
    skel = where.shape[1]
    parts, room = len(pieces), pieces[0].shape[0]
    extra = -(-slots // 16) * 16
    args = [most, where, pattern, counts, *in_hbm(dense, proxy), *pieces] + ([] if interp is None else [interp])
    return pl.pallas_call(
        functools.partial(solve_kernel, base, slots, parts),
        name="solve",
        out_shape=[
            jax.ShapeDtypeStruct((proxy.shape[0], skel, unknowns), F32),
            jax.ShapeDtypeStruct((slots * skel + extra, unknowns), jnp.int16),
        ],
        in_specs=[SMEM, VMEM, VMEM, VMEM, HBM, HBM] + [VMEM] * parts + [HBM] * (interp is not None),
        out_specs=[HBM, VMEM],
        input_output_aliases={} if interp is None else {len(args) - 1: 0},
        scratch_shapes=[
            pltpu.VMEM((parts * room, width), BF16),
            pltpu.VMEM((slots * skel, parts * room), BF16),
            pltpu.VMEM((slots * skel, width), BF16),
            pltpu.VMEM((slots // 2 * skel, 2 * skel), F32),
            pltpu.VMEM((extra, unknowns), F32),
            pltpu.VMEM((slots, skel, unknowns), F32),
            pltpu.VMEM((slots, unknowns, width), BF16),
            pltpu.VMEM((slots, 2 * skel, width), BF16),
            pltpu.VMEM((slots, unknowns, 2 * skel), F32),
            pltpu.SemaphoreType.DMA((1 + 2 * slots,)),
        ],
        compiler_params=pltpu.CompilerParams(vmem_limit_bytes=24 << 20),
        cost_estimate=pl.CostEstimate(flops=1 << 33, bytes_accessed=8 << 20, transcendentals=0),
    )(*args)


def couple_kernel(base, groups, near_ref, inverse_ref, own_ref, counts_ref, *refs):
    coded_refs = refs[: groups - 1]
    out_ref, near, inverse, own, out, turns, sems = refs[-7:]
    slots, skel, unknowns = own.shape
    part = pl.ds(base, slots)
    tables = [pltpu.make_async_copy(own_ref.at[part], own, sems.at[0]), pltpu.make_async_copy(inverse_ref.at[part], inverse, sems.at[1])]
    copies = [pltpu.make_async_copy(near_ref.at[base + b], near.at[b], sems.at[2 + b]) for b in range(slots)]
    for copy in tables + copies:
        copy.start()
    here = lax.axis_index("grp")
    diagonal = iota((skel, skel), 0) == iota((skel, skel), 1)

    def owed(counts):
        mine = jnp.where(iota(counts.shape, 1) == here, counts, 0.0)
        return iota((counts.shape[0], skel), 1) < jnp.sum(mine, axis=1, keepdims=True).astype(I32)

    unit = (iota((groups, 2 * skel), 0) == iota((groups, 2 * skel), 1)).astype(F32).astype(BF16)
    mine = dot(counts_ref[...].astype(F32).astype(BF16), unit, TN)
    scales = [owed(mine).astype(F32)[base : base + slots]]
    for ref in coded_refs:
        tail = ref[slots * skel :, :].astype(I32).astype(F32)
        main, power, counts = tail[:, :skel], tail[:, skel : 2 * skel], tail[:, 2 * skel :]
        scales.append(jnp.where(owed(counts), main * jnp.exp2(power) * (1.0 / (MAIN * Q_MAX)), 0.0))
    for copy in tables:
        copy.wait()
    for b in range(slots):
        rows = [own[b]] + [ref[b * skel : (b + 1) * skel, :].astype(I32).astype(F32) for ref in coded_refs]
        for k in range(groups):
            high = rows[k].astype(BF16)
            low = (rows[k] - high.astype(F32)).astype(BF16)
            turned = dot(jnp.concatenate([high, low], axis=0), inverse[b], NT)
            turned = (turned[:skel] + turned[skel:]) * to_column(scales[k][b : b + 1, :], diagonal)
            high = turned.astype(BF16)
            turns[b, k, :skel, :] = high
            turns[b, k, skel:, :] = (turned - high.astype(F32)).astype(BF16)
    for copy in copies:
        copy.wait()
    writes = []
    for b in range(slots):
        total = None
        for k in range(groups):
            term = dot(turns[b, k], near[b, here ^ k], NT)
            total = term if total is None else total + term
        out[b] = total[:skel] + total[skel:]
        writes.append(pltpu.make_async_copy(out.at[b], out_ref.at[base + b], sems.at[2 + slots + b]))
        writes[-1].start()
    for copy in writes:
        copy.wait()


def couple(base, slots, near, inverse, own, counts, coded, coupling):
    groups, unknowns = near.shape[1:3]
    skel = own.shape[1]
    args = [*in_hbm(near, inverse, own), counts, *coded] + ([] if coupling is None else [coupling])
    return pl.pallas_call(
        functools.partial(couple_kernel, base, groups),
        name="couple",
        out_shape=jax.ShapeDtypeStruct(own.shape, F32),
        in_specs=[HBM, HBM, HBM, VMEM] + [VMEM] * len(coded) + [HBM] * (coupling is not None),
        out_specs=HBM,
        input_output_aliases={} if coupling is None else {len(args) - 1: 0},
        scratch_shapes=[
            pltpu.VMEM((slots, groups, unknowns, unknowns), BF16),
            pltpu.VMEM((slots, unknowns, unknowns), BF16),
            pltpu.VMEM((slots, skel, unknowns), F32),
            pltpu.VMEM((slots, skel, unknowns), F32),
            pltpu.VMEM((slots, groups, 2 * skel, unknowns), BF16),
            pltpu.SemaphoreType.DMA((2 + 2 * slots,)),
        ],
        compiler_params=pltpu.CompilerParams(vmem_limit_bytes=24 << 20),
    )(*args)


def swap(x, axis, size, k):
    return lax.ppermute(x, axis, [(i, i ^ k) for i in range(size)])


def send_all(merge, taken, pattern, proxy):
    cols = lax.axis_size("col")
    slots, skel = taken.shape
    width = proxy.shape[2]
    mask = jnp.repeat(pattern, width // pattern.shape[1], axis=1).astype(BF16)
    rows = jnp.take_along_axis(proxy, jnp.maximum(taken, 0)[:, :, None], axis=1) * mask[:, None, :]
    rows = jnp.where(taken[:, :, None] >= 0, rows, jnp.zeros_like(rows)).astype(F32)
    placed = jnp.zeros((cols // merge,) + rows.shape, F32)
    final = lax.axis_index("col") // merge
    placed = lax.dynamic_update_index_in_dim(placed, rows, final, 0)
    summed = lax.psum(placed, "col")
    rows = lax.dynamic_index_in_dim(summed, final, 0, keepdims=False).astype(BF16)
    return jnp.zeros((), bool), rows.reshape(slots * skel, width)


def local(proxy_rows, pattern, first_pivots, merge_pivots, send_counts, near_field, self_inverse):
    cols, groups = lax.axis_size("col"), lax.axis_size("grp")
    merge = 1 << min(5, cols.bit_length() - 1)
    slots, skel = first_pivots.shape[1:]
    proxy = proxy_rows[0]
    share = slots * skel // merge
    room = -(-(share * 4) // (3 * 32)) * 32
    blocks, counts = pattern[0].T, send_counts[0].T
    compact, where, taken, most, dense = route(
        merge, room, jnp.swapaxes(merge_pivots[0], 1, 2), jnp.swapaxes(first_pivots, 0, 1), blocks, proxy
    )

    pieces = {0: compact, 1: swap(compact, "col", cols, 1)}
    for k in range(2, merge, 2):
        pieces[k] = swap(compact, "col", cols, k)
    for k in range(2, merge, 2):
        pieces[k + 1] = swap(pieces[k], "col", cols, 1)
    pieces = [pieces[k] for k in range(merge)]
    dense = lax.while_loop(
        lambda now: now[0], lambda now: send_all(merge, taken, pattern[0], proxy), (most[0] >= room, dense)
    )[1]
    early = slots * 2 // 3 // 2 * 2
    chunks = ((0, early), (early, slots - early))
    interp = coupling = None
    codes = []
    for base, count in chunks:
        interp, coded = solve(base, count, most, where, blocks, counts, dense, proxy, pieces, interp)
        codes.append([swap(coded, "grp", groups, k) for k in range(1, groups)])
    for (base, count), coded in zip(chunks, codes):
        coupling = couple(base, count, near_field[0], self_inverse[0], interp, counts, coded, coupling)
    return (interp[None], coupling[None])


def solution(mesh):
    return jax.shard_map(
        local,
        mesh=mesh,
        in_specs=(
            P("grp", "col", None, None),
            P("grp", "col", None),
            P("grp", "col", None),
            P("grp", None, None, None, None),
            P("grp", "col", None),
            P("grp", "col", None, None, None),
            P("grp", "col", None, None),
        ),
        out_specs=(P("grp", "col", None, None), P("grp", "col", None, None)),
        check_vma=False,
    )
```

```python
import functools

import jax
import jax.numpy as jnp
from jax import lax
from jax.experimental import pallas as pl
from jax.experimental.pallas import tpu as pltpu
from jax.sharding import PartitionSpec as P


F32 = jnp.float32
BF16 = jnp.bfloat16
I32 = jnp.int32
NT = (((1,), (1,)), ((), ()))
NN = (((1,), (0,)), ((), ()))
TN = (((0,), (0,)), ((), ()))
VMEM = pl.BlockSpec(memory_space=pltpu.VMEM)
HBM = pl.BlockSpec(memory_space=pltpu.HBM)
SMEM = pl.BlockSpec(memory_space=pltpu.SMEM)
PIVOTS = 4
Q_MAX = 32000.0
MAIN = 8000.0


def dot(a, b, dims=NN, precision=None):
    return lax.dot_general(a, b, dims, preferred_element_type=F32, precision=precision)


def in_hbm(*arrays):
    return [pltpu.with_memory_space_constraint(x, pltpu.HBM) for x in arrays]


def iota(shape, dim):
    return lax.broadcasted_iota(I32, shape, dim)


def box_masks(pattern_ref, width):
    blocks = pattern_ref.shape[0]
    spread = (iota((blocks, width), 1) // (width // blocks) == iota((blocks, width), 0)).astype(F32).astype(BF16)
    return dot(pattern_ref[...].astype(F32).astype(BF16), spread, TN)


def to_column(row, diagonal):
    return jnp.sum(jnp.where(diagonal, row, 0.0), axis=1, keepdims=True)


def to_row(column, diagonal):
    return jnp.sum(jnp.where(diagonal, column, 0.0), axis=0, keepdims=True)


def thirds(x):
    high = x.astype(BF16)
    rest = x - high.astype(F32)
    middle = rest.astype(BF16)
    return high, middle, (rest - middle.astype(F32)).astype(BF16)


def exact_dot(a, b):
    a, b = thirds(a), thirds(b)
    order = ((0, 0), (0, 1), (1, 0), (0, 2), (2, 0), (1, 1))
    return dot(jnp.concatenate([a[i] for i, _ in order], axis=1), jnp.concatenate([b[j] for _, j in order], axis=1), NT)


def route_kernel(merge, only, merge_hbm, first_hbm, pattern_hbm, proxy_ref, *refs):
    compact_ref, where_ref, taken_ref, most_ref, _, merge_ref, first_ref, pattern_ref, boxes, move, sems = refs
    rounds = merge.bit_length() - 1
    slots, unknowns, width = boxes.shape
    skel = first_ref.shape[2]
    room = compact_ref.shape[0]
    tables = ((merge_hbm, merge_ref), (first_hbm, first_ref), (pattern_hbm, pattern_ref))
    tables = [pltpu.make_async_copy(a, b, sems.at[slots + i]) for i, (a, b) in enumerate(tables)]
    copies = [pltpu.make_async_copy(proxy_ref.at[s], boxes.at[s], sems.at[s]) for s in range(slots)]
    for copy in tables + copies:
        copy.start()
    for copy in tables:
        copy.wait()
    me = lax.axis_index("col")
    final, local = (0 if only else me >> rounds), me & (merge - 1)
    picked = merge_ref[rounds - 1, :, final, :]
    upper = (picked >= skel).astype(I32)
    node, row = upper, picked - upper * skel
    for section in range(rounds - 2, -1, -1):
        count = merge >> (section + 1)
        picked = jnp.zeros_like(row)
        for n in range(count):
            found = jnp.take_along_axis(merge_ref[section, :, final * count + n, :], row, axis=1)
            picked = jnp.where(node == n, found, picked)
        upper = (picked >= skel).astype(I32)
        node, row = 2 * node + upper, picked - upper * skel
    unknown = jnp.take_along_axis(first_ref[:, 0, :], row, axis=1)
    before = (iota((skel, skel), 0) < iota((skel, skel), 1)).astype(BF16)
    ones = jnp.ones((skel, skel), BF16)
    above = (iota((slots, slots), 1) < iota((slots, slots), 0)).astype(BF16)
    place = jnp.zeros((slots, skel), F32)
    for d in range(merge):
        here = (node == d).astype(F32).astype(BF16)
        rank = dot(here, before) + dot(dot(above, here).astype(BF16), ones)
        place = jnp.where(node == d, rank, place)
    place = place.astype(I32)
    most_ref[0] = jnp.max(place)
    where_ref[...] = jnp.where(place < room, (node ^ local) * room + place, -1)
    mine = jnp.where(node == local, place, -1)
    taken_ref[...] = jnp.where(node == local, unknown, -1)
    mask = box_masks(pattern_ref, width).astype(BF16)
    kind = iota((8, skel), 0)
    source = jnp.zeros((room, 8), F32)
    for s in range(slots):
        into = (iota((room, skel), 0) == mine[s : s + 1, :]).astype(F32).astype(BF16)
        facts = jnp.where(kind == 0, unknown[s : s + 1, :], jnp.where(kind == 1, s + 1, 0))
        source += dot(into, facts.astype(F32).astype(BF16), NT)
    slot = source[:, 1:2].astype(I32) - 1
    source = source[:, 0:1].astype(I32)
    for s in range(slots):
        match = iota((room, unknowns), 1) == jnp.where(slot == s, source, -1)
        move[:, s * unknowns : (s + 1) * unknowns] = match.astype(F32).astype(BF16)
    own = (iota((room, slots), 1) == slot).astype(F32).astype(BF16)
    for copy in copies:
        copy.wait()
    rows = dot(move[...], boxes[...].reshape(slots * unknowns, width)) * dot(own, mask)
    compact_ref[...] = rows.astype(BF16)


def route(merge, room, merge_pivots, first_pivots, pattern, proxy):
    slots, unknowns, width = proxy.shape
    skel = first_pivots.shape[2]
    return pl.pallas_call(
        functools.partial(route_kernel, merge, lax.axis_size("col") == merge),
        name="route",
        out_shape=[
            jax.ShapeDtypeStruct((room, width), BF16),
            jax.ShapeDtypeStruct((slots, skel), I32),
            jax.ShapeDtypeStruct((slots, skel), I32),
            jax.ShapeDtypeStruct((1,), I32),
            jax.ShapeDtypeStruct((slots * skel, width), BF16),
        ],
        in_specs=[HBM] * 4,
        out_specs=[VMEM, VMEM, VMEM, SMEM, HBM],
        scratch_shapes=[
            pltpu.VMEM(merge_pivots.shape, I32),
            pltpu.VMEM(first_pivots.shape, I32),
            pltpu.VMEM(pattern.shape, I32),
            pltpu.VMEM((slots, unknowns, width), BF16),
            pltpu.VMEM((room, slots * unknowns), BF16),
            pltpu.SemaphoreType.DMA((slots + 3,)),
        ],
        compiler_params=pltpu.CompilerParams(vmem_limit_bytes=16 << 20),
    )(*in_hbm(merge_pivots, first_pivots, pattern, proxy))


def solve_kernel(base, slots, parts, most_ref, where_ref, pattern_ref, counts_ref, dense_ref, proxy_ref, *refs):
    piece_refs = refs[:parts]
    interp_ref, coded_ref, found, pieces, choose, skeleton, inverse, tails, boxes, weights, right, sems = refs[-12:]
    skel = where_ref.shape[1]
    unknowns, width = proxy_ref.shape[1:]
    room = piece_refs[0].shape[0]
    total = parts * room
    half = slots // 2
    pair = 2 * skel
    diagonal = iota((skel, skel), 0) == iota((skel, skel), 1)
    loads = [pltpu.make_async_copy(proxy_ref.at[base + s], boxes.at[s], sems.at[1 + slots + s]) for s in range(slots)]
    for copy in loads:
        copy.start()

    @pl.when(most_ref[0] < room)
    def _():
        for k in range(parts):
            pieces[k * room : (k + 1) * room, :] = piece_refs[k][...]
        lanes = iota((skel, total), 1)
        for s in range(slots):
            spot = to_column(where_ref[base + s : base + s + 1, :].astype(F32), diagonal).astype(I32)
            choose[s * skel : (s + 1) * skel, :] = (lanes == spot).astype(F32).astype(BF16)
        skeleton[...] = dot(choose[...], pieces[...]).astype(BF16)

    @pl.when(most_ref[0] >= room)
    def _():
        copy = pltpu.make_async_copy(dense_ref.at[pl.ds(base * skel, slots * skel), :], skeleton, sems.at[0])
        copy.start()
        copy.wait()

    mask = box_masks(pattern_ref, width).astype(BF16)
    for h in range(half):
        for side in range(2):
            rows = skeleton[(h + side * half) * skel : (h + side * half + 1) * skel, :]
            inverse[h * skel : (h + 1) * skel, side * skel : (side + 1) * skel] = dot(rows, rows, NT)

    side, column, sublane = iota((8, pair), 1) & skel, iota((8, pair), 1) & (skel - 1), iota((8, pair), 0)
    wide_side, wide_column = iota((skel, pair), 1) & skel, iota((skel, pair), 1) & (skel - 1)

    blank = jnp.zeros((skel, width), BF16)
    for s in range(slots):
        rows = skeleton[s * skel : (s + 1) * skel, :] * mask[base + s : base + s + 1, :]
        weights[s] = jnp.concatenate([rows, blank] if s < half else [blank, rows], axis=0)
    for copy in loads:
        copy.wait()
    steps = skel // PIVOTS
    stretch = unknowns
    while slots * unknowns <= steps * stretch // 2:
        stretch //= 2
    turns = unknowns // stretch

    def line(k):
        row = jnp.broadcast_to(inverse[pl.ds(k, 1), :], (8, pair))
        for h in range(1, half):
            row = jnp.where(sublane == h, jnp.broadcast_to(inverse[pl.ds(h * skel + k, 1), :], (8, pair)), row)
        return row

    def eliminate(step, carry):
        k = PIVOTS * step
        span = range(PIVOTS)
        rows = [line(k + i) for i in span]
        small = [[jnp.take_along_axis(rows[i], side + (k + j), axis=1) for j in span] for i in span]
        for p in span:
            r = 1.0 / small[p][p]
            pivot = [r if j == p else small[p][j] * r for j in span]
            for i in span:
                if i != p:
                    f = small[i][p]
                    small[i] = [-f * r if j == p else small[i][j] - f * pivot[j] for j in span]
            small[p] = pivot
        fresh = []
        for i in span:
            row = small[i][0] * rows[0]
            for j in span[1:]:
                row = row + small[i][j] * rows[j]
            for j in span:
                row = jnp.where(column == k + j, small[i][j], row)
            fresh.append(row)
        blocks = [inverse[h * skel : (h + 1) * skel, :] for h in range(half)]
        for h, block in enumerate(blocks):
            kept = jnp.where((wide_column // PIVOTS) == step, 0.0, block)
            for j in span:
                kept = kept - jnp.take_along_axis(block, wide_side + (k + j), axis=1) * fresh[j][h : h + 1, :]
            inverse[h * skel : (h + 1) * skel, :] = kept
        for h in range(half):
            for j in span:
                inverse[pl.ds(h * skel + k + j, 1), :] = fresh[j][h : h + 1, :]
        turn = jnp.minimum(step, slots * turns - 1)
        box, part = turn // turns, pl.ds(pl.multiple_of((turn % turns) * stretch, stretch), stretch)
        right[box, part, :] = dot(boxes[box, part, :], weights[box], NT)
        return carry

    lax.fori_loop(0, steps, eliminate, 0)

    groups = counts_ref.shape[0]
    unit = (iota((groups, unknowns - pair), 0) == iota((groups, unknowns - pair), 1)).astype(F32).astype(BF16)
    owed = dot(counts_ref[...].astype(F32).astype(BF16), unit, TN)
    tails[...] = jnp.zeros_like(tails)
    left = iota((skel, pair), 1) < skel
    writes = []
    for h in range(half):
        both = inverse[h * skel : (h + 1) * skel, :]
        both = jnp.concatenate([jnp.where(left, both, 0.0), jnp.where(left, 0.0, both)], axis=0)
        xs = exact_dot(both, right[h] + right[h + half])
        tops = jnp.maximum(jnp.max(jnp.abs(xs), axis=1, keepdims=True), 1e-30)
        powers = jnp.clip(jnp.floor(jnp.log2(tops)), -100.0, 126.0)
        mains = jnp.floor(tops * jnp.exp2(-powers) * MAIN) + 1.0
        codes = xs * ((Q_MAX * MAIN) / (mains * jnp.exp2(powers)))
        codes = (codes + jnp.where(codes >= 0, 0.5, -0.5)).astype(I32).astype(jnp.int16)
        for side in range(2):
            s = h + side * half
            part = slice(side * skel, (side + 1) * skel)
            found[s] = xs[part]
            writes.append(pltpu.make_async_copy(found.at[s], interp_ref.at[base + s], sems.at[1 + s]))
            writes[-1].start()
            coded_ref[s * skel : (s + 1) * skel, :] = codes[part]
            tails[s : s + 1, :] = jnp.concatenate(
                [to_row(mains[part], diagonal), to_row(powers[part], diagonal), owed[base + s : base + s + 1, :]], axis=1
            )
    coded_ref[slots * skel :, :] = tails[...].astype(I32).astype(jnp.int16)
    for copy in writes:
        copy.wait()


def solve(base, slots, most, where, pattern, counts, dense, proxy, pieces, interp):
    unknowns, width = proxy.shape[1:]
    skel = where.shape[1]
    parts, room = len(pieces), pieces[0].shape[0]
    extra = -(-slots // 16) * 16
    args = [most, where, pattern, counts, *in_hbm(dense, proxy), *pieces] + ([] if interp is None else [interp])
    return pl.pallas_call(
        functools.partial(solve_kernel, base, slots, parts),
        name="solve",
        out_shape=[
            jax.ShapeDtypeStruct((proxy.shape[0], skel, unknowns), F32),
            jax.ShapeDtypeStruct((slots * skel + extra, unknowns), jnp.int16),
            jax.ShapeDtypeStruct((slots, skel, unknowns), F32),
        ],
        in_specs=[SMEM, VMEM, VMEM, VMEM, HBM, HBM] + [VMEM] * parts + [HBM] * (interp is not None),
        out_specs=[HBM, VMEM, VMEM],
        input_output_aliases={} if interp is None else {len(args) - 1: 0},
        scratch_shapes=[
            pltpu.VMEM((parts * room, width), BF16),
            pltpu.VMEM((slots * skel, parts * room), BF16),
            pltpu.VMEM((slots * skel, width), BF16),
            pltpu.VMEM((slots // 2 * skel, 2 * skel), F32),
            pltpu.VMEM((extra, unknowns), F32),
            pltpu.VMEM((slots, unknowns, width), BF16),
            pltpu.VMEM((slots, 2 * skel, width), BF16),
            pltpu.VMEM((slots, unknowns, 2 * skel), F32),
            pltpu.SemaphoreType.DMA((1 + 2 * slots,)),
        ],
        compiler_params=pltpu.CompilerParams(vmem_limit_bytes=24 << 20),
        cost_estimate=pl.CostEstimate(flops=1 << 33, bytes_accessed=8 << 20, transcendentals=0),
    )(*args)


def owed_rows(counts, skel):
    mine = jnp.where(iota(counts.shape, 1) == lax.axis_index("grp"), counts, 0.0)
    return iota((counts.shape[0], skel), 1) < jnp.sum(mine, axis=1, keepdims=True).astype(I32)


def turn(rows, inverse, scale):
    skel = rows.shape[0]
    high = rows.astype(BF16)
    low = (rows - high.astype(F32)).astype(BF16)
    turned = dot(jnp.concatenate([high, low], axis=0), inverse, NT)
    turned = (turned[:skel] + turned[skel:]) * scale
    high = turned.astype(BF16)
    return jnp.concatenate([high, (turned - high.astype(F32)).astype(BF16)], axis=0)


def own_kernel(groups, near_ref, inverse_ref, counts_ref, *refs):
    own_refs = refs[:-4]
    near, part_ref, turns, sems = refs[-4:]
    slots, skel, unknowns = part_ref.shape
    copies = [pltpu.make_async_copy(near_ref.at[b], near.at[b], sems.at[b]) for b in range(slots)]
    for copy in copies:
        copy.start()
    here = lax.axis_index("grp")
    diagonal = iota((skel, skel), 0) == iota((skel, skel), 1)
    unit = (iota((groups, 2 * skel), 0) == iota((groups, 2 * skel), 1)).astype(F32).astype(BF16)
    counts = dot(counts_ref[...].astype(F32).astype(BF16), unit, TN)
    scales = owed_rows(counts, skel).astype(F32)
    b = 0
    for ref in own_refs:
        for i in range(ref.shape[0]):
            turns[b] = turn(ref[i], inverse_ref[b], to_column(scales[b : b + 1, :], diagonal))
            b += 1
    for copy in copies:
        copy.wait()
    for b in range(slots):
        both = dot(turns[b], near[b, here], NT)
        part_ref[b] = both[:skel] + both[skel:]


def own_part(near, inverse, counts, owns):
    slots, groups, unknowns = near.shape[:3]
    skel = owns[0].shape[1]
    return pl.pallas_call(
        functools.partial(own_kernel, groups),
        name="own_part",
        out_shape=[jax.ShapeDtypeStruct(near.shape, BF16), jax.ShapeDtypeStruct((slots, skel, unknowns), F32)],
        in_specs=[HBM] + [VMEM] * (2 + len(owns)),
        out_specs=[VMEM, VMEM],
        scratch_shapes=[pltpu.VMEM((slots, 2 * skel, unknowns), BF16), pltpu.SemaphoreType.DMA((slots,))],
        compiler_params=pltpu.CompilerParams(vmem_limit_bytes=24 << 20),
        cost_estimate=pl.CostEstimate(flops=1 << 31, bytes_accessed=8 << 20, transcendentals=0),
    )(*in_hbm(near), inverse, counts, *owns)


def couple_kernel(base, groups, near, inverse, part_ref, *refs):
    coded_refs = refs[: groups - 1]
    out_ref, out, turns, sems = refs[-4:]
    slots, skel, unknowns = out.shape
    here = lax.axis_index("grp")
    diagonal = iota((skel, skel), 0) == iota((skel, skel), 1)
    scales = []
    for ref in coded_refs:
        tail = ref[slots * skel :, :].astype(I32).astype(F32)
        main, power, counts = tail[:, :skel], tail[:, skel : 2 * skel], tail[:, 2 * skel :]
        scale = main * jnp.exp2(power) * (1.0 / (MAIN * Q_MAX))
        scales.append(jnp.where(owed_rows(counts, skel), scale, 0.0))
    for b in range(slots):
        for k, ref in enumerate(coded_refs):
            rows = ref[b * skel : (b + 1) * skel, :].astype(I32).astype(F32)
            turns[b, k] = turn(rows, inverse[base + b], to_column(scales[k][b : b + 1, :], diagonal))
    writes = []
    for b in range(slots):
        total = None
        for k in range(groups - 1):
            term = dot(turns[b, k], near[base + b, here ^ (k + 1)], NT)
            total = term if total is None else total + term
        out[b] = part_ref[base + b] + (total[:skel] + total[skel:])
        writes.append(pltpu.make_async_copy(out.at[b], out_ref.at[base + b], sems.at[b]))
        writes[-1].start()
    for copy in writes:
        copy.wait()


def couple(base, slots, near, inverse, part, coded, coupling):
    groups, unknowns = near.shape[1:3]
    skel = part.shape[1]
    args = [near, inverse, part, *coded] + ([] if coupling is None else [coupling])
    return pl.pallas_call(
        functools.partial(couple_kernel, base, groups),
        name="couple",
        out_shape=jax.ShapeDtypeStruct(part.shape, F32),
        in_specs=[VMEM] * (3 + len(coded)) + [HBM] * (coupling is not None),
        out_specs=HBM,
        input_output_aliases={} if coupling is None else {len(args) - 1: 0},
        scratch_shapes=[
            pltpu.VMEM((slots, skel, unknowns), F32),
            pltpu.VMEM((slots, groups - 1, 2 * skel, unknowns), BF16),
            pltpu.SemaphoreType.DMA((slots,)),
        ],
        compiler_params=pltpu.CompilerParams(vmem_limit_bytes=24 << 20),
    )(*args)


def swap(x, axis, size, k):
    return lax.ppermute(x, axis, [(i, i ^ k) for i in range(size)])


def send_all(merge, taken, pattern, proxy):
    cols = lax.axis_size("col")
    slots, skel = taken.shape
    width = proxy.shape[2]
    mask = jnp.repeat(pattern, width // pattern.shape[1], axis=1).astype(BF16)
    rows = jnp.take_along_axis(proxy, jnp.maximum(taken, 0)[:, :, None], axis=1) * mask[:, None, :]
    rows = jnp.where(taken[:, :, None] >= 0, rows, jnp.zeros_like(rows)).astype(F32)
    placed = jnp.zeros((cols // merge,) + rows.shape, F32)
    final = lax.axis_index("col") // merge
    placed = lax.dynamic_update_index_in_dim(placed, rows, final, 0)
    summed = lax.psum(placed, "col")
    rows = lax.dynamic_index_in_dim(summed, final, 0, keepdims=False).astype(BF16)
    return jnp.zeros((), bool), rows.reshape(slots * skel, width)


def local(proxy_rows, pattern, first_pivots, merge_pivots, send_counts, near_field, self_inverse):
    cols, groups = lax.axis_size("col"), lax.axis_size("grp")
    merge = 1 << min(5, cols.bit_length() - 1)
    slots, skel = first_pivots.shape[1:]
    proxy = proxy_rows[0]
    share = slots * skel // merge
    room = -(-(share * 4) // (3 * 32)) * 32
    blocks, counts = pattern[0].T, send_counts[0].T
    compact, where, taken, most, dense = route(
        merge, room, jnp.swapaxes(merge_pivots[0], 1, 2), jnp.swapaxes(first_pivots, 0, 1), blocks, proxy
    )

    pieces = {0: compact, 1: swap(compact, "col", cols, 1)}
    for k in range(2, merge, 2):
        pieces[k] = swap(compact, "col", cols, k)
    for k in range(2, merge, 2):
        pieces[k + 1] = swap(pieces[k], "col", cols, 1)
    pieces = [pieces[k] for k in range(merge)]
    dense = lax.while_loop(
        lambda now: now[0], lambda now: send_all(merge, taken, pattern[0], proxy), (most[0] >= room, dense)
    )[1]
    early = slots * 2 // 3 // 2 * 2
    chunks = ((0, early), (early, slots - early))
    interp = coupling = None
    codes, owns = [], []
    for base, count in chunks:
        interp, coded, own = solve(base, count, most, where, blocks, counts, dense, proxy, pieces, interp)
        codes.append([swap(coded, "grp", groups, k) for k in range(1, groups)])
        owns.append(own)
    near, part = own_part(near_field[0], self_inverse[0], counts, owns)
    for (base, count), coded in zip(chunks, codes):
        coupling = couple(base, count, near, self_inverse[0], part, coded, coupling)
    return (interp[None], coupling[None])


def solution(mesh):
    return jax.shard_map(
        local,
        mesh=mesh,
        in_specs=(
            P("grp", "col", None, None),
            P("grp", "col", None),
            P("grp", "col", None),
            P("grp", None, None, None, None),
            P("grp", "col", None),
            P("grp", "col", None, None, None),
            P("grp", "col", None, None),
        ),
        out_specs=(P("grp", "col", None, None), P("grp", "col", None, None)),
        check_vma=False,
    )
```

```python
import functools

import jax
import jax.numpy as jnp
from jax import lax
from jax.experimental import pallas as pl
from jax.experimental.pallas import tpu as pltpu
from jax.sharding import PartitionSpec as P


F32 = jnp.float32
BF16 = jnp.bfloat16
I32 = jnp.int32
NT = (((1,), (1,)), ((), ()))
NN = (((1,), (0,)), ((), ()))
TN = (((0,), (0,)), ((), ()))
VMEM = pl.BlockSpec(memory_space=pltpu.VMEM)
HBM = pl.BlockSpec(memory_space=pltpu.HBM)
SMEM = pl.BlockSpec(memory_space=pltpu.SMEM)
PIVOTS = 4
PARTS = 4
Q_MAX = 32000.0
MAIN = 8000.0


def dot(a, b, dims=NN, precision=None):
    return lax.dot_general(a, b, dims, preferred_element_type=F32, precision=precision)


def in_hbm(*arrays):
    return [pltpu.with_memory_space_constraint(x, pltpu.HBM) for x in arrays]


def iota(shape, dim):
    return lax.broadcasted_iota(I32, shape, dim)


def box_masks(pattern_ref, width):
    blocks = pattern_ref.shape[0]
    spread = (iota((blocks, width), 1) // (width // blocks) == iota((blocks, width), 0)).astype(F32).astype(BF16)
    return dot(pattern_ref[...].astype(F32).astype(BF16), spread, TN)


def to_column(row, diagonal):
    return jnp.sum(jnp.where(diagonal, row, 0.0), axis=1, keepdims=True)


def to_row(column, diagonal):
    return jnp.sum(jnp.where(diagonal, column, 0.0), axis=0, keepdims=True)


def thirds(x):
    high = x.astype(BF16)
    rest = x - high.astype(F32)
    middle = rest.astype(BF16)
    return high, middle, (rest - middle.astype(F32)).astype(BF16)


ORDER = ((0, 0), (0, 1), (1, 0), (0, 2), (2, 0), (1, 1))


def exact_dot(a, b):
    a, b = thirds(a), thirds(b)
    return dot(jnp.concatenate([a[i] for i, _ in ORDER], axis=1), jnp.concatenate([b[j] for _, j in ORDER], axis=1), NT)


def exact_gram(a, b):
    width = a.shape[1]
    identity = (iota((width, width), 0) == iota((width, width), 1)).astype(F32).astype(BF16)
    a, b = [dot(identity, part, NT).astype(BF16) for part in thirds(a)], thirds(b)
    return dot(jnp.concatenate([a[i] for i, _ in ORDER], axis=1), jnp.concatenate([b[j] for _, j in ORDER], axis=0))


def route_kernel(merge, only, merge_hbm, first_hbm, pattern_hbm, proxy_ref, *refs):
    compact_ref, where_ref, taken_ref, most_ref, _, merge_ref, first_ref, pattern_ref, boxes, move, sems = refs
    rounds = merge.bit_length() - 1
    slots, unknowns, width = boxes.shape
    skel = first_ref.shape[2]
    room = compact_ref.shape[0]
    tables = ((merge_hbm, merge_ref), (first_hbm, first_ref), (pattern_hbm, pattern_ref))
    tables = [pltpu.make_async_copy(a, b, sems.at[slots + i]) for i, (a, b) in enumerate(tables)]
    copies = [pltpu.make_async_copy(proxy_ref.at[s], boxes.at[s], sems.at[s]) for s in range(slots)]
    for copy in tables + copies:
        copy.start()
    for copy in tables:
        copy.wait()
    me = lax.axis_index("col")
    final, local = (0 if only else me >> rounds), me & (merge - 1)
    picked = merge_ref[rounds - 1, :, final, :]
    upper = (picked >= skel).astype(I32)
    node, row = upper, picked - upper * skel
    for section in range(rounds - 2, -1, -1):
        count = merge >> (section + 1)
        picked = jnp.zeros_like(row)
        for n in range(count):
            found = jnp.take_along_axis(merge_ref[section, :, final * count + n, :], row, axis=1)
            picked = jnp.where(node == n, found, picked)
        upper = (picked >= skel).astype(I32)
        node, row = 2 * node + upper, picked - upper * skel
    unknown = jnp.take_along_axis(first_ref[:, 0, :], row, axis=1)
    before = (iota((skel, skel), 0) < iota((skel, skel), 1)).astype(BF16)
    ones = jnp.ones((skel, skel), BF16)
    above = (iota((slots, slots), 1) < iota((slots, slots), 0)).astype(BF16)
    place = jnp.zeros((slots, skel), F32)
    for d in range(merge):
        here = (node == d).astype(F32).astype(BF16)
        rank = dot(here, before) + dot(dot(above, here).astype(BF16), ones)
        place = jnp.where(node == d, rank, place)
    place = place.astype(I32)
    most_ref[0] = jnp.max(place)
    where_ref[...] = jnp.where(place < room, (node ^ local) * room + place, -1)
    mine = jnp.where(node == local, place, -1)
    taken_ref[...] = jnp.where(node == local, unknown, -1)
    mask = box_masks(pattern_ref, width).astype(BF16)
    kind = iota((8, skel), 0)
    source = jnp.zeros((room, 8), F32)
    for s in range(slots):
        into = (iota((room, skel), 0) == mine[s : s + 1, :]).astype(F32).astype(BF16)
        facts = jnp.where(kind == 0, unknown[s : s + 1, :], jnp.where(kind == 1, s + 1, 0))
        source += dot(into, facts.astype(F32).astype(BF16), NT)
    slot = source[:, 1:2].astype(I32) - 1
    source = source[:, 0:1].astype(I32)
    for s in range(slots):
        match = iota((room, unknowns), 1) == jnp.where(slot == s, source, -1)
        move[:, s * unknowns : (s + 1) * unknowns] = match.astype(F32).astype(BF16)
    own = (iota((room, slots), 1) == slot).astype(F32).astype(BF16)
    for copy in copies:
        copy.wait()
    rows = dot(move[...], boxes[...].reshape(slots * unknowns, width)) * dot(own, mask)
    compact_ref[...] = rows.astype(BF16)


def route(merge, room, merge_pivots, first_pivots, pattern, proxy):
    slots, unknowns, width = proxy.shape
    skel = first_pivots.shape[2]
    return pl.pallas_call(
        functools.partial(route_kernel, merge, lax.axis_size("col") == merge),
        name="route",
        out_shape=[
            jax.ShapeDtypeStruct((room, width), BF16),
            jax.ShapeDtypeStruct((slots, skel), I32),
            jax.ShapeDtypeStruct((slots, skel), I32),
            jax.ShapeDtypeStruct((1,), I32),
            jax.ShapeDtypeStruct((slots * skel, width), BF16),
        ],
        in_specs=[HBM] * 4,
        out_specs=[VMEM, VMEM, VMEM, SMEM, HBM],
        scratch_shapes=[
            pltpu.VMEM(merge_pivots.shape, I32),
            pltpu.VMEM(first_pivots.shape, I32),
            pltpu.VMEM(pattern.shape, I32),
            pltpu.VMEM((slots, unknowns, width), BF16),
            pltpu.VMEM((room, slots * unknowns), BF16),
            pltpu.SemaphoreType.DMA((slots + 3,)),
        ],
        compiler_params=pltpu.CompilerParams(vmem_limit_bytes=16 << 20),
    )(*in_hbm(merge_pivots, first_pivots, pattern, proxy))


def aim_kernel(where_ref, choose_ref):
    slots, skel = where_ref.shape
    diagonal = iota((skel, skel), 0) == iota((skel, skel), 1)
    lanes = iota((skel, choose_ref.shape[1]), 1)
    for s in range(slots):
        spot = to_column(where_ref[s : s + 1, :].astype(F32), diagonal).astype(I32)
        choose_ref[s * skel : (s + 1) * skel, :] = (lanes == spot).astype(F32).astype(BF16)


def aim(where, total):
    return pl.pallas_call(
        aim_kernel,
        name="aim",
        out_shape=jax.ShapeDtypeStruct((where.shape[0] * where.shape[1], total), BF16),
        in_specs=[VMEM],
        out_specs=VMEM,
        compiler_params=pltpu.CompilerParams(vmem_limit_bytes=8 << 20),
        cost_estimate=pl.CostEstimate(flops=1 << 30, bytes_accessed=2 << 20, transcendentals=0),
    )(where)


def solve_kernel(base, slots, parts, most_ref, choose_ref, pattern_ref, counts_ref, dense_ref, proxy_ref, *refs):
    piece_refs = refs[:parts]
    interp_ref, coded_ref, found, pieces, skeleton, lower, scaled, tails, boxes, weights, right, sems = refs[-12:]
    skel = interp_ref.shape[1]
    unknowns, width = proxy_ref.shape[1:]
    room = piece_refs[0].shape[0]
    half = slots // 2
    pair = 2 * skel
    diagonal = iota((skel, skel), 0) == iota((skel, skel), 1)
    loads = [pltpu.make_async_copy(proxy_ref.at[base + s], boxes.at[s], sems.at[1 + slots + s]) for s in range(slots)]
    for copy in loads:
        copy.start()

    @pl.when(most_ref[0] < room)
    def _():
        for k in range(parts):
            pieces[k * room : (k + 1) * room, :] = piece_refs[k][...]
        skeleton[...] = dot(choose_ref[base * skel : (base + slots) * skel, :], pieces[...]).astype(BF16)

    @pl.when(most_ref[0] >= room)
    def _():
        copy = pltpu.make_async_copy(dense_ref.at[pl.ds(base * skel, slots * skel), :], skeleton, sems.at[0])
        copy.start()
        copy.wait()

    mask = box_masks(pattern_ref, width).astype(BF16)
    for h in range(half):
        for side in range(2):
            rows = skeleton[(h + side * half) * skel : (h + side * half + 1) * skel, :]
            lower[h * skel : (h + 1) * skel, side * skel : (side + 1) * skel] = dot(rows, rows, NT)

    side, column, sublane = iota((8, pair), 1) & skel, iota((8, pair), 1) & (skel - 1), iota((8, pair), 0)
    wide_side, wide_column = iota((skel, pair), 1) & skel, iota((skel, pair), 1) & (skel - 1)
    wide_line = iota((skel, pair), 0)

    blank = jnp.zeros((skel, width), BF16)
    for s in range(slots):
        rows = skeleton[s * skel : (s + 1) * skel, :] * mask[base + s : base + s + 1, :]
        weights[s] = jnp.concatenate([rows, blank] if s < half else [blank, rows], axis=0)
    for copy in loads:
        copy.wait()
    steps = skel // PIVOTS
    stretch = unknowns
    while slots * unknowns <= steps * stretch // 2:
        stretch //= 2
    turns = unknowns // stretch

    def line(k):
        row = jnp.broadcast_to(lower[pl.ds(k, 1), :], (8, pair))
        for h in range(1, half):
            row = jnp.where(sublane == h, jnp.broadcast_to(lower[pl.ds(h * skel + k, 1), :], (8, pair)), row)
        return row

    def eliminate(start, step, carry):
        k = PIVOTS * step
        span = range(PIVOTS)
        rows = [line(k + i) for i in span]
        small = [[jnp.take_along_axis(rows[i], side + (k + j), axis=1) for j in span] for i in span]
        for p in span:
            r = 1.0 / small[p][p]
            pivot = [r if j == p else small[p][j] * r for j in span]
            for i in span:
                if i != p:
                    f = small[i][p]
                    small[i] = [-f * r if j == p else small[i][j] - f * pivot[j] for j in span]
            small[p] = pivot
        fresh = []
        for i in span:
            row = small[i][0] * rows[0]
            for j in span[1:]:
                row = row + small[i][j] * rows[j]
            for j in span:
                row = jnp.where(column == k + j, small[i][j], row)
            fresh.append(row)
        blocks = [lower[h * skel + start : (h + 1) * skel, :] for h in range(half)]
        for h, block in enumerate(blocks):
            kept = jnp.where((wide_column[start:] // PIVOTS) == step, 0.0, block)
            for j in span:
                kept = kept - jnp.take_along_axis(block, wide_side[start:] + (k + j), axis=1) * fresh[j][h : h + 1, :]
            lower[h * skel + start : (h + 1) * skel, :] = jnp.where(wide_line[start:] >= k + PIVOTS, kept, block)
        for h in range(half):
            for j in span:
                scaled[pl.ds(h * skel + k + j, 1), :] = fresh[j][h : h + 1, :]
        turn = jnp.minimum(step, slots * turns - 1)
        box, part = turn // turns, pl.ds(pl.multiple_of((turn % turns) * stretch, stretch), stretch)
        right[box, part, :] = dot(boxes[box, part, :], weights[box], NT)
        return carry

    for part in range(PARTS):
        bounds = part * steps // PARTS, (part + 1) * steps // PARTS
        lax.fori_loop(*bounds, functools.partial(eliminate, bounds[0] * PIVOTS), 0)
    behind = wide_column // PIVOTS < wide_line // PIVOTS
    upto = wide_column // PIVOTS <= wide_line // PIVOTS
    unit_diagonal = (wide_column == wide_line).astype(F32)
    same = (iota((pair, pair), 0) & skel) == (iota((pair, pair), 1) & skel)

    groups = counts_ref.shape[0]
    unit = (iota((groups, unknowns - pair), 0) == iota((groups, unknowns - pair), 1)).astype(F32).astype(BF16)
    owed = dot(counts_ref[...].astype(F32).astype(BF16), unit, TN)
    tails[...] = jnp.zeros_like(tails)
    writes = []
    for h in range(half):
        part = slice(h * skel, (h + 1) * skel)
        both = exact_gram(jnp.where(behind, lower[part, :], unit_diagonal), jnp.where(upto, scaled[part, :], 0.0))
        both = jnp.where(same, both, 0.0)
        xs = exact_dot(both, right[h] + right[h + half])
        tops = jnp.max(jnp.abs(xs), axis=1, keepdims=True)
        for side in range(2):
            s = h + side * half
            part = slice(side * skel, (side + 1) * skel)
            found[s] = xs[part]
            writes.append(pltpu.make_async_copy(found.at[s], interp_ref.at[base + s], sems.at[1 + s]))
            writes[-1].start()
            tails[s : s + 1, :skel] = to_row(tops[part], diagonal)
    rows = jnp.maximum(tails[:, :skel], 1e-30)
    power = jnp.clip(jnp.floor(jnp.log2(rows)), -100.0, 126.0)
    main = jnp.floor(rows * jnp.exp2(-power) * MAIN) + 1.0
    factor = (Q_MAX * MAIN) / (main * jnp.exp2(power))
    for s in range(slots):
        codes = found[s] * to_column(factor[s : s + 1, :], diagonal)
        codes = (codes + jnp.where(codes >= 0, 0.5, -0.5)).astype(I32)
        coded_ref[s * skel : (s + 1) * skel, :] = codes.astype(jnp.int16)
        tails[s : s + 1, pair:] = owed[base + s : base + s + 1, :]
    tails[:, :pair] = jnp.concatenate([main, power], axis=1)
    coded_ref[slots * skel :, :] = tails[...].astype(I32).astype(jnp.int16)
    for copy in writes:
        copy.wait()


def solve(base, slots, most, choose, pattern, counts, dense, proxy, pieces, interp):
    unknowns, width = proxy.shape[1:]
    skel = choose.shape[0] // proxy.shape[0]
    parts, room = len(pieces), pieces[0].shape[0]
    extra = -(-slots // 16) * 16
    args = [most, choose, pattern, counts, *in_hbm(dense, proxy), *pieces] + ([] if interp is None else [interp])
    return pl.pallas_call(
        functools.partial(solve_kernel, base, slots, parts),
        name="solve",
        out_shape=[
            jax.ShapeDtypeStruct((proxy.shape[0], skel, unknowns), F32),
            jax.ShapeDtypeStruct((slots * skel + extra, unknowns), jnp.int16),
            jax.ShapeDtypeStruct((slots, skel, unknowns), F32),
        ],
        in_specs=[SMEM, VMEM, VMEM, VMEM, HBM, HBM] + [VMEM] * parts + [HBM] * (interp is not None),
        out_specs=[HBM, VMEM, VMEM],
        input_output_aliases={} if interp is None else {len(args) - 1: 0},
        scratch_shapes=[
            pltpu.VMEM((parts * room, width), BF16),
            pltpu.VMEM((slots * skel, width), BF16),
            pltpu.VMEM((slots // 2 * skel, 2 * skel), F32),
            pltpu.VMEM((slots // 2 * skel, 2 * skel), F32),
            pltpu.VMEM((extra, unknowns), F32),
            pltpu.VMEM((slots, unknowns, width), BF16),
            pltpu.VMEM((slots, 2 * skel, width), BF16),
            pltpu.VMEM((slots, unknowns, 2 * skel), F32),
            pltpu.SemaphoreType.DMA((1 + 2 * slots,)),
        ],
        compiler_params=pltpu.CompilerParams(vmem_limit_bytes=24 << 20),
        cost_estimate=pl.CostEstimate(flops=1 << 33, bytes_accessed=8 << 20, transcendentals=0),
    )(*args)


def owed_rows(counts, skel):
    mine = jnp.where(iota(counts.shape, 1) == lax.axis_index("grp"), counts, 0.0)
    return iota((counts.shape[0], skel), 1) < jnp.sum(mine, axis=1, keepdims=True).astype(I32)


def turn(rows, inverse, scale):
    skel = rows.shape[0]
    high = rows.astype(BF16)
    low = (rows - high.astype(F32)).astype(BF16)
    turned = dot(jnp.concatenate([high, low], axis=0), inverse, NT)
    turned = (turned[:skel] + turned[skel:]) * scale
    high = turned.astype(BF16)
    return jnp.concatenate([high, (turned - high.astype(F32)).astype(BF16)], axis=0)


def own_kernel(groups, near_ref, inverse_ref, counts_ref, *refs):
    own_refs = refs[:-4]
    near, part_ref, turns, sems = refs[-4:]
    slots, skel, unknowns = part_ref.shape
    copies = [pltpu.make_async_copy(near_ref.at[b], near.at[b], sems.at[b]) for b in range(slots)]
    for copy in copies:
        copy.start()
    here = lax.axis_index("grp")
    diagonal = iota((skel, skel), 0) == iota((skel, skel), 1)
    unit = (iota((groups, 2 * skel), 0) == iota((groups, 2 * skel), 1)).astype(F32).astype(BF16)
    counts = dot(counts_ref[...].astype(F32).astype(BF16), unit, TN)
    scales = owed_rows(counts, skel).astype(F32)
    b = 0
    for ref in own_refs:
        for i in range(ref.shape[0]):
            turns[b] = turn(ref[i], inverse_ref[b], to_column(scales[b : b + 1, :], diagonal))
            b += 1
    for copy in copies:
        copy.wait()
    for b in range(slots):
        both = dot(turns[b], near[b, here], NT)
        part_ref[b] = both[:skel] + both[skel:]


def own_part(near, inverse, counts, owns):
    slots, groups, unknowns = near.shape[:3]
    skel = owns[0].shape[1]
    return pl.pallas_call(
        functools.partial(own_kernel, groups),
        name="own_part",
        out_shape=[jax.ShapeDtypeStruct(near.shape, BF16), jax.ShapeDtypeStruct((slots, skel, unknowns), F32)],
        in_specs=[HBM] + [VMEM] * (2 + len(owns)),
        out_specs=[VMEM, VMEM],
        scratch_shapes=[pltpu.VMEM((slots, 2 * skel, unknowns), BF16), pltpu.SemaphoreType.DMA((slots,))],
        compiler_params=pltpu.CompilerParams(vmem_limit_bytes=24 << 20),
        cost_estimate=pl.CostEstimate(flops=1 << 31, bytes_accessed=8 << 20, transcendentals=0),
    )(*in_hbm(near), inverse, counts, *owns)


def couple_kernel(base, groups, near, inverse, part_ref, *refs):
    coded_refs = refs[: groups - 1]
    out_ref, out, turns, sems = refs[-4:]
    slots, skel, unknowns = out.shape
    here = lax.axis_index("grp")
    diagonal = iota((skel, skel), 0) == iota((skel, skel), 1)
    scales = []
    for ref in coded_refs:
        tail = ref[slots * skel :, :].astype(I32).astype(F32)
        main, power, counts = tail[:, :skel], tail[:, skel : 2 * skel], tail[:, 2 * skel :]
        scale = main * jnp.exp2(power) * (1.0 / (MAIN * Q_MAX))
        scales.append(jnp.where(owed_rows(counts, skel), scale, 0.0))
    for b in range(slots):
        for k, ref in enumerate(coded_refs):
            rows = ref[b * skel : (b + 1) * skel, :].astype(I32).astype(F32)
            turns[b, k] = turn(rows, inverse[base + b], to_column(scales[k][b : b + 1, :], diagonal))
    writes = []
    for b in range(slots):
        total = None
        for k in range(groups - 1):
            term = dot(turns[b, k], near[base + b, here ^ (k + 1)], NT)
            total = term if total is None else total + term
        out[b] = part_ref[base + b] + (total[:skel] + total[skel:])
        writes.append(pltpu.make_async_copy(out.at[b], out_ref.at[base + b], sems.at[b]))
        writes[-1].start()
    for copy in writes:
        copy.wait()


def couple(base, slots, near, inverse, part, coded, coupling):
    groups, unknowns = near.shape[1:3]
    skel = part.shape[1]
    args = [near, inverse, part, *coded] + ([] if coupling is None else [coupling])
    return pl.pallas_call(
        functools.partial(couple_kernel, base, groups),
        name="couple",
        out_shape=jax.ShapeDtypeStruct(part.shape, F32),
        in_specs=[VMEM] * (3 + len(coded)) + [HBM] * (coupling is not None),
        out_specs=HBM,
        input_output_aliases={} if coupling is None else {len(args) - 1: 0},
        scratch_shapes=[
            pltpu.VMEM((slots, skel, unknowns), F32),
            pltpu.VMEM((slots, groups - 1, 2 * skel, unknowns), BF16),
            pltpu.SemaphoreType.DMA((slots,)),
        ],
        compiler_params=pltpu.CompilerParams(vmem_limit_bytes=24 << 20),
    )(*args)


def swap(x, axis, size, k):
    return lax.ppermute(x, axis, [(i, i ^ k) for i in range(size)])


def send_all(merge, taken, pattern, proxy):
    cols = lax.axis_size("col")
    slots, skel = taken.shape
    width = proxy.shape[2]
    mask = jnp.repeat(pattern, width // pattern.shape[1], axis=1).astype(BF16)
    rows = jnp.take_along_axis(proxy, jnp.maximum(taken, 0)[:, :, None], axis=1) * mask[:, None, :]
    rows = jnp.where(taken[:, :, None] >= 0, rows, jnp.zeros_like(rows)).astype(F32)
    placed = jnp.zeros((cols // merge,) + rows.shape, F32)
    final = lax.axis_index("col") // merge
    placed = lax.dynamic_update_index_in_dim(placed, rows, final, 0)
    summed = lax.psum(placed, "col")
    rows = lax.dynamic_index_in_dim(summed, final, 0, keepdims=False).astype(BF16)
    return jnp.zeros((), bool), rows.reshape(slots * skel, width)


def local(proxy_rows, pattern, first_pivots, merge_pivots, send_counts, near_field, self_inverse):
    cols, groups = lax.axis_size("col"), lax.axis_size("grp")
    merge = 1 << min(5, cols.bit_length() - 1)
    slots, skel = first_pivots.shape[1:]
    proxy = proxy_rows[0]
    share = slots * skel // merge
    room = -(-(share * 4) // (3 * 32)) * 32
    blocks, counts = pattern[0].T, send_counts[0].T
    compact, where, taken, most, dense = route(
        merge, room, jnp.swapaxes(merge_pivots[0], 1, 2), jnp.swapaxes(first_pivots, 0, 1), blocks, proxy
    )

    pieces = {0: compact, 1: swap(compact, "col", cols, 1)}
    for k in range(2, merge, 2):
        pieces[k] = swap(compact, "col", cols, k)
    for k in range(2, merge, 2):
        pieces[k + 1] = swap(pieces[k], "col", cols, 1)
    pieces = [pieces[k] for k in range(merge)]
    choose = aim(where, merge * room)
    dense = lax.while_loop(
        lambda now: now[0], lambda now: send_all(merge, taken, pattern[0], proxy), (most[0] >= room, dense)
    )[1]
    early = slots * 2 // 3 // 2 * 2
    chunks = ((0, early), (early, slots - early))
    interp = coupling = None
    codes, owns = [], []
    for base, count in chunks:
        interp, coded, own = solve(base, count, most, choose, blocks, counts, dense, proxy, pieces, interp)
        codes.append([swap(coded, "grp", groups, k) for k in range(1, groups)])
        owns.append(own)
    near, part = own_part(near_field[0], self_inverse[0], counts, owns)
    for (base, count), coded in zip(chunks, codes):
        coupling = couple(base, count, near, self_inverse[0], part, coded, coupling)
    return (interp[None], coupling[None])


def solution(mesh):
    return jax.shard_map(
        local,
        mesh=mesh,
        in_specs=(
            P("grp", "col", None, None),
            P("grp", "col", None),
            P("grp", "col", None),
            P("grp", None, None, None, None),
            P("grp", "col", None),
            P("grp", "col", None, None, None),
            P("grp", "col", None, None),
        ),
        out_specs=(P("grp", "col", None, None), P("grp", "col", None, None)),
        check_vma=False,
    )
```

```python
import functools

import jax
import jax.numpy as jnp
from jax import lax
from jax.experimental import pallas as pl
from jax.experimental.pallas import tpu as pltpu
from jax.sharding import PartitionSpec as P


F32 = jnp.float32
BF16 = jnp.bfloat16
I32 = jnp.int32
NT = (((1,), (1,)), ((), ()))
NN = (((1,), (0,)), ((), ()))
TN = (((0,), (0,)), ((), ()))
VMEM = pl.BlockSpec(memory_space=pltpu.VMEM)
HBM = pl.BlockSpec(memory_space=pltpu.HBM)
SMEM = pl.BlockSpec(memory_space=pltpu.SMEM)
PIVOTS = 4
Q_MAX = 32000.0
MAIN = 8000.0


def dot(a, b, dims=NN, precision=None):
    return lax.dot_general(a, b, dims, preferred_element_type=F32, precision=precision)


def in_hbm(*arrays):
    return [pltpu.with_memory_space_constraint(x, pltpu.HBM) for x in arrays]


def iota(shape, dim):
    return lax.broadcasted_iota(I32, shape, dim)


def box_masks(pattern_ref, width):
    blocks = pattern_ref.shape[0]
    spread = (iota((blocks, width), 1) // (width // blocks) == iota((blocks, width), 0)).astype(F32).astype(BF16)
    return dot(pattern_ref[...].astype(F32).astype(BF16), spread, TN)


def to_column(row, diagonal):
    return jnp.sum(jnp.where(diagonal, row, 0.0), axis=1, keepdims=True)


def to_row(column, diagonal):
    return jnp.sum(jnp.where(diagonal, column, 0.0), axis=0, keepdims=True)


def thirds(x):
    high = x.astype(BF16)
    rest = x - high.astype(F32)
    middle = rest.astype(BF16)
    return high, middle, (rest - middle.astype(F32)).astype(BF16)


def exact_dot(a, b):
    a, b = thirds(a), thirds(b)
    order = ((0, 0), (0, 1), (1, 0), (0, 2), (2, 0), (1, 1))
    return dot(jnp.concatenate([a[i] for i, _ in order], axis=1), jnp.concatenate([b[j] for _, j in order], axis=1), NT)


def route_kernel(merge, only, merge_hbm, first_hbm, pattern_hbm, proxy_ref, *refs):
    compact_ref, where_ref, taken_ref, most_ref, _, merge_ref, first_ref, pattern_ref, boxes, move, sems = refs
    rounds = merge.bit_length() - 1
    slots, unknowns, width = boxes.shape
    skel = first_ref.shape[2]
    room = compact_ref.shape[0]
    tables = ((merge_hbm, merge_ref), (first_hbm, first_ref), (pattern_hbm, pattern_ref))
    tables = [pltpu.make_async_copy(a, b, sems.at[slots + i]) for i, (a, b) in enumerate(tables)]
    copies = [pltpu.make_async_copy(proxy_ref.at[s], boxes.at[s], sems.at[s]) for s in range(slots)]
    for copy in tables + copies:
        copy.start()
    for copy in tables:
        copy.wait()
    me = lax.axis_index("col")
    final, local = (0 if only else me >> rounds), me & (merge - 1)
    picked = merge_ref[rounds - 1, :, final, :]
    upper = (picked >= skel).astype(I32)
    node, row = upper, picked - upper * skel
    for section in range(rounds - 2, -1, -1):
        count = merge >> (section + 1)
        picked = jnp.zeros_like(row)
        for n in range(count):
            found = jnp.take_along_axis(merge_ref[section, :, final * count + n, :], row, axis=1)
            picked = jnp.where(node == n, found, picked)
        upper = (picked >= skel).astype(I32)
        node, row = 2 * node + upper, picked - upper * skel
    unknown = jnp.take_along_axis(first_ref[:, 0, :], row, axis=1)
    before = (iota((skel, skel), 0) < iota((skel, skel), 1)).astype(BF16)
    ones = jnp.ones((skel, skel), BF16)
    above = (iota((slots, slots), 1) < iota((slots, slots), 0)).astype(BF16)
    place = jnp.zeros((slots, skel), F32)
    for d in range(merge):
        here = (node == d).astype(F32).astype(BF16)
        rank = dot(here, before) + dot(dot(above, here).astype(BF16), ones)
        place = jnp.where(node == d, rank, place)
    place = place.astype(I32)
    most_ref[0] = jnp.max(place)
    where_ref[...] = jnp.where(place < room, (node ^ local) * room + place, -1)
    mine = jnp.where(node == local, place, -1)
    taken_ref[...] = jnp.where(node == local, unknown, -1)
    mask = box_masks(pattern_ref, width).astype(BF16)
    kind = iota((8, skel), 0)
    source = jnp.zeros((room, 8), F32)
    for s in range(slots):
        into = (iota((room, skel), 0) == mine[s : s + 1, :]).astype(F32).astype(BF16)
        facts = jnp.where(kind == 0, unknown[s : s + 1, :], jnp.where(kind == 1, s + 1, 0))
        source += dot(into, facts.astype(F32).astype(BF16), NT)
    slot = source[:, 1:2].astype(I32) - 1
    source = source[:, 0:1].astype(I32)
    for s in range(slots):
        match = iota((room, unknowns), 1) == jnp.where(slot == s, source, -1)
        move[:, s * unknowns : (s + 1) * unknowns] = match.astype(F32).astype(BF16)
    own = (iota((room, slots), 1) == slot).astype(F32).astype(BF16)
    for copy in copies:
        copy.wait()
    rows = dot(move[...], boxes[...].reshape(slots * unknowns, width)) * dot(own, mask)
    compact_ref[...] = rows.astype(BF16)


def route(merge, room, merge_pivots, first_pivots, pattern, proxy):
    slots, unknowns, width = proxy.shape
    skel = first_pivots.shape[2]
    return pl.pallas_call(
        functools.partial(route_kernel, merge, lax.axis_size("col") == merge),
        name="route",
        out_shape=[
            jax.ShapeDtypeStruct((room, width), BF16),
            jax.ShapeDtypeStruct((slots, skel), I32),
            jax.ShapeDtypeStruct((slots, skel), I32),
            jax.ShapeDtypeStruct((1,), I32),
            jax.ShapeDtypeStruct((slots * skel, width), BF16),
        ],
        in_specs=[HBM] * 4,
        out_specs=[VMEM, VMEM, VMEM, SMEM, HBM],
        scratch_shapes=[
            pltpu.VMEM(merge_pivots.shape, I32),
            pltpu.VMEM(first_pivots.shape, I32),
            pltpu.VMEM(pattern.shape, I32),
            pltpu.VMEM((slots, unknowns, width), BF16),
            pltpu.VMEM((room, slots * unknowns), BF16),
            pltpu.SemaphoreType.DMA((slots + 3,)),
        ],
        compiler_params=pltpu.CompilerParams(vmem_limit_bytes=16 << 20),
    )(*in_hbm(merge_pivots, first_pivots, pattern, proxy))


def aim_kernel(where_ref, choose_ref, picks_ref):
    slots, skel = where_ref.shape
    diagonal = iota((skel, skel), 0) == iota((skel, skel), 1)
    lanes = iota((skel, choose_ref.shape[1]), 1)
    for s in range(slots):
        spot = to_column(where_ref[s : s + 1, :].astype(F32), diagonal).astype(I32)
        choose_ref[s * skel : (s + 1) * skel, :] = (lanes == spot).astype(F32).astype(BF16)
    pair = 2 * skel
    gap = iota((pair, pair), 0) - (iota((pair, pair), 1) & skel)
    for k in range(skel):
        picks_ref[k] = (gap == k).astype(F32).astype(BF16)


def aim(where, total):
    slots, skel = where.shape
    return pl.pallas_call(
        aim_kernel,
        name="aim",
        out_shape=[
            jax.ShapeDtypeStruct((slots * skel, total), BF16),
            jax.ShapeDtypeStruct((skel, 2 * skel, 2 * skel), BF16),
        ],
        in_specs=[VMEM],
        out_specs=[VMEM, VMEM],
        compiler_params=pltpu.CompilerParams(vmem_limit_bytes=8 << 20),
        cost_estimate=pl.CostEstimate(flops=1 << 30, bytes_accessed=2 << 20, transcendentals=0),
    )(where)


def solve_kernel(base, slots, parts, most_ref, choose_ref, picks_ref, pattern_ref, counts_ref, dense_ref, proxy_ref, *refs):
    piece_refs = refs[:parts]
    interp_ref, coded_ref, found, pieces, skeleton, inverse, tails, boxes, weights, right, sems = refs[-11:]
    skel = interp_ref.shape[1]
    unknowns, width = proxy_ref.shape[1:]
    room = piece_refs[0].shape[0]
    half = slots // 2
    pair = 2 * skel
    diagonal = iota((skel, skel), 0) == iota((skel, skel), 1)
    loads = [pltpu.make_async_copy(proxy_ref.at[base + s], boxes.at[s], sems.at[1 + slots + s]) for s in range(slots)]
    for copy in loads:
        copy.start()

    @pl.when(most_ref[0] < room)
    def _():
        for k in range(parts):
            pieces[k * room : (k + 1) * room, :] = piece_refs[k][...]
        skeleton[...] = dot(choose_ref[base * skel : (base + slots) * skel, :], pieces[...]).astype(BF16)

    @pl.when(most_ref[0] >= room)
    def _():
        copy = pltpu.make_async_copy(dense_ref.at[pl.ds(base * skel, slots * skel), :], skeleton, sems.at[0])
        copy.start()
        copy.wait()

    mask = box_masks(pattern_ref, width).astype(BF16)
    for h in range(half):
        for side in range(2):
            rows = skeleton[(h + side * half) * skel : (h + side * half + 1) * skel, :]
            inverse[h * skel : (h + 1) * skel, side * skel : (side + 1) * skel] = dot(rows, rows, NT)

    side, column, sublane = iota((8, pair), 1) & skel, iota((8, pair), 1) & (skel - 1), iota((8, pair), 0)
    wide_side, wide_column = iota((skel, pair), 1) & skel, iota((skel, pair), 1) & (skel - 1)

    blank = jnp.zeros((skel, width), BF16)
    for s in range(slots):
        rows = skeleton[s * skel : (s + 1) * skel, :] * mask[base + s : base + s + 1, :]
        weights[s] = jnp.concatenate([rows, blank] if s < half else [blank, rows], axis=0)
    for copy in loads:
        copy.wait()
    steps = skel // PIVOTS
    spread = half // 2 if half > 2 else 0
    stretch = unknowns
    while slots * unknowns <= steps * stretch // 2:
        stretch //= 2
    turns = unknowns // stretch

    def line(k):
        row = jnp.broadcast_to(inverse[pl.ds(k, 1), :], (8, pair))
        for h in range(1, half):
            row = jnp.where(sublane == h, jnp.broadcast_to(inverse[pl.ds(h * skel + k, 1), :], (8, pair)), row)
        return row

    def eliminate(step, carry):
        k = PIVOTS * step
        span = range(PIVOTS)
        rows = [line(k + i) for i in span]
        small = [[jnp.take_along_axis(rows[i], side + (k + j), axis=1) for j in span] for i in span]
        for p in span:
            r = 1.0 / small[p][p]
            pivot = [r if j == p else small[p][j] * r for j in span]
            for i in span:
                if i != p:
                    f = small[i][p]
                    small[i] = [-f * r if j == p else small[i][j] - f * pivot[j] for j in span]
            small[p] = pivot
        fresh = []
        for i in span:
            row = small[i][0] * rows[0]
            for j in span[1:]:
                row = row + small[i][j] * rows[j]
            for j in span:
                row = jnp.where(column == k + j, small[i][j], row)
            fresh.append(row)
        blocks = [inverse[h * skel : (h + 1) * skel, :] for h in range(half)]
        if spread:
            each = jnp.concatenate([picks_ref[k + j] for j in span], axis=1)
            high, middle, low = thirds(jnp.concatenate(blocks[:spread], axis=0))
            columns = dot(high, each) + dot(middle, each) + dot(low, each)
        for h, block in enumerate(blocks):
            kept = jnp.where((wide_column // PIVOTS) == step, 0.0, block)
            for j in span:
                if h < spread:
                    col = columns[h * skel : (h + 1) * skel, j * pair : (j + 1) * pair]
                else:
                    col = jnp.take_along_axis(block, wide_side + (k + j), axis=1)
                kept = kept - col * fresh[j][h : h + 1, :]
            inverse[h * skel : (h + 1) * skel, :] = kept
        for h in range(half):
            for j in span:
                inverse[pl.ds(h * skel + k + j, 1), :] = fresh[j][h : h + 1, :]
        turn = jnp.minimum(step, slots * turns - 1)
        box, part = turn // turns, pl.ds(pl.multiple_of((turn % turns) * stretch, stretch), stretch)
        right[box, part, :] = dot(boxes[box, part, :], weights[box], NT)
        return carry

    lax.fori_loop(0, steps, eliminate, 0)

    groups = counts_ref.shape[0]
    unit = (iota((groups, unknowns - pair), 0) == iota((groups, unknowns - pair), 1)).astype(F32).astype(BF16)
    owed = dot(counts_ref[...].astype(F32).astype(BF16), unit, TN)
    tails[...] = jnp.zeros_like(tails)
    left = iota((skel, pair), 1) < skel
    writes = []
    for h in range(half):
        both = inverse[h * skel : (h + 1) * skel, :]
        both = jnp.concatenate([jnp.where(left, both, 0.0), jnp.where(left, 0.0, both)], axis=0)
        xs = exact_dot(both, right[h] + right[h + half])
        tops = jnp.max(jnp.abs(xs), axis=1, keepdims=True)
        for side in range(2):
            s = h + side * half
            part = slice(side * skel, (side + 1) * skel)
            found[s] = xs[part]
            writes.append(pltpu.make_async_copy(found.at[s], interp_ref.at[base + s], sems.at[1 + s]))
            writes[-1].start()
            tails[s : s + 1, :skel] = to_row(tops[part], diagonal)
    rows = jnp.maximum(tails[:, :skel], 1e-30)
    power = jnp.clip(jnp.floor(jnp.log2(rows)), -100.0, 126.0)
    main = jnp.floor(rows * jnp.exp2(-power) * MAIN) + 1.0
    factor = (Q_MAX * MAIN) / (main * jnp.exp2(power))
    for s in range(slots):
        codes = found[s] * to_column(factor[s : s + 1, :], diagonal)
        codes = (codes + jnp.where(codes >= 0, 0.5, -0.5)).astype(I32)
        coded_ref[s * skel : (s + 1) * skel, :] = codes.astype(jnp.int16)
        tails[s : s + 1, pair:] = owed[base + s : base + s + 1, :]
    tails[:, :pair] = jnp.concatenate([main, power], axis=1)
    coded_ref[slots * skel :, :] = tails[...].astype(I32).astype(jnp.int16)
    for copy in writes:
        copy.wait()


def solve(base, slots, most, choose, picks, pattern, counts, dense, proxy, pieces, interp):
    unknowns, width = proxy.shape[1:]
    skel = choose.shape[0] // proxy.shape[0]
    parts, room = len(pieces), pieces[0].shape[0]
    extra = -(-slots // 16) * 16
    args = [most, choose, picks, pattern, counts, *in_hbm(dense, proxy), *pieces] + ([] if interp is None else [interp])
    return pl.pallas_call(
        functools.partial(solve_kernel, base, slots, parts),
        name="solve",
        out_shape=[
            jax.ShapeDtypeStruct((proxy.shape[0], skel, unknowns), F32),
            jax.ShapeDtypeStruct((slots * skel + extra, unknowns), jnp.int16),
            jax.ShapeDtypeStruct((slots, skel, unknowns), F32),
        ],
        in_specs=[SMEM, VMEM, VMEM, VMEM, VMEM, HBM, HBM] + [VMEM] * parts + [HBM] * (interp is not None),
        out_specs=[HBM, VMEM, VMEM],
        input_output_aliases={} if interp is None else {len(args) - 1: 0},
        scratch_shapes=[
            pltpu.VMEM((parts * room, width), BF16),
            pltpu.VMEM((slots * skel, width), BF16),
            pltpu.VMEM((slots // 2 * skel, 2 * skel), F32),
            pltpu.VMEM((extra, unknowns), F32),
            pltpu.VMEM((slots, unknowns, width), BF16),
            pltpu.VMEM((slots, 2 * skel, width), BF16),
            pltpu.VMEM((slots, unknowns, 2 * skel), F32),
            pltpu.SemaphoreType.DMA((1 + 2 * slots,)),
        ],
        compiler_params=pltpu.CompilerParams(vmem_limit_bytes=24 << 20),
        cost_estimate=pl.CostEstimate(flops=1 << 33, bytes_accessed=8 << 20, transcendentals=0),
    )(*args)


def owed_rows(counts, skel):
    mine = jnp.where(iota(counts.shape, 1) == lax.axis_index("grp"), counts, 0.0)
    return iota((counts.shape[0], skel), 1) < jnp.sum(mine, axis=1, keepdims=True).astype(I32)


def turn(rows, inverse, scale):
    skel = rows.shape[0]
    high = rows.astype(BF16)
    low = (rows - high.astype(F32)).astype(BF16)
    turned = dot(jnp.concatenate([high, low], axis=0), inverse, NT)
    turned = (turned[:skel] + turned[skel:]) * scale
    high = turned.astype(BF16)
    return jnp.concatenate([high, (turned - high.astype(F32)).astype(BF16)], axis=0)


def own_kernel(groups, near_ref, inverse_ref, counts_ref, *refs):
    own_refs = refs[:-4]
    near, part_ref, turns, sems = refs[-4:]
    slots, skel, unknowns = part_ref.shape
    copies = [pltpu.make_async_copy(near_ref.at[b], near.at[b], sems.at[b]) for b in range(slots)]
    for copy in copies:
        copy.start()
    here = lax.axis_index("grp")
    diagonal = iota((skel, skel), 0) == iota((skel, skel), 1)
    unit = (iota((groups, 2 * skel), 0) == iota((groups, 2 * skel), 1)).astype(F32).astype(BF16)
    counts = dot(counts_ref[...].astype(F32).astype(BF16), unit, TN)
    scales = owed_rows(counts, skel).astype(F32)
    b = 0
    for ref in own_refs:
        for i in range(ref.shape[0]):
            turns[b] = turn(ref[i], inverse_ref[b], to_column(scales[b : b + 1, :], diagonal))
            b += 1
    for copy in copies:
        copy.wait()
    for b in range(slots):
        both = dot(turns[b], near[b, here], NT)
        part_ref[b] = both[:skel] + both[skel:]


def own_part(near, inverse, counts, owns):
    slots, groups, unknowns = near.shape[:3]
    skel = owns[0].shape[1]
    return pl.pallas_call(
        functools.partial(own_kernel, groups),
        name="own_part",
        out_shape=[jax.ShapeDtypeStruct(near.shape, BF16), jax.ShapeDtypeStruct((slots, skel, unknowns), F32)],
        in_specs=[HBM] + [VMEM] * (2 + len(owns)),
        out_specs=[VMEM, VMEM],
        scratch_shapes=[pltpu.VMEM((slots, 2 * skel, unknowns), BF16), pltpu.SemaphoreType.DMA((slots,))],
        compiler_params=pltpu.CompilerParams(vmem_limit_bytes=24 << 20),
        cost_estimate=pl.CostEstimate(flops=1 << 31, bytes_accessed=8 << 20, transcendentals=0),
    )(*in_hbm(near), inverse, counts, *owns)


def couple_kernel(base, groups, near, inverse, part_ref, *refs):
    coded_refs = refs[: groups - 1]
    out_ref, out, turns, sems = refs[-4:]
    slots, skel, unknowns = out.shape
    here = lax.axis_index("grp")
    diagonal = iota((skel, skel), 0) == iota((skel, skel), 1)
    scales = []
    for ref in coded_refs:
        tail = ref[slots * skel :, :].astype(I32).astype(F32)
        main, power, counts = tail[:, :skel], tail[:, skel : 2 * skel], tail[:, 2 * skel :]
        scale = main * jnp.exp2(power) * (1.0 / (MAIN * Q_MAX))
        scales.append(jnp.where(owed_rows(counts, skel), scale, 0.0))
    for b in range(slots):
        for k, ref in enumerate(coded_refs):
            rows = ref[b * skel : (b + 1) * skel, :].astype(I32).astype(F32)
            turns[b, k] = turn(rows, inverse[base + b], to_column(scales[k][b : b + 1, :], diagonal))
    writes = []
    for b in range(slots):
        total = None
        for k in range(groups - 1):
            term = dot(turns[b, k], near[base + b, here ^ (k + 1)], NT)
            total = term if total is None else total + term
        out[b] = part_ref[base + b] + (total[:skel] + total[skel:])
        writes.append(pltpu.make_async_copy(out.at[b], out_ref.at[base + b], sems.at[b]))
        writes[-1].start()
    for copy in writes:
        copy.wait()


def couple(base, slots, near, inverse, part, coded, coupling):
    groups, unknowns = near.shape[1:3]
    skel = part.shape[1]
    args = [near, inverse, part, *coded] + ([] if coupling is None else [coupling])
    return pl.pallas_call(
        functools.partial(couple_kernel, base, groups),
        name="couple",
        out_shape=jax.ShapeDtypeStruct(part.shape, F32),
        in_specs=[VMEM] * (3 + len(coded)) + [HBM] * (coupling is not None),
        out_specs=HBM,
        input_output_aliases={} if coupling is None else {len(args) - 1: 0},
        scratch_shapes=[
            pltpu.VMEM((slots, skel, unknowns), F32),
            pltpu.VMEM((slots, groups - 1, 2 * skel, unknowns), BF16),
            pltpu.SemaphoreType.DMA((slots,)),
        ],
        compiler_params=pltpu.CompilerParams(vmem_limit_bytes=24 << 20),
    )(*args)


def swap(x, axis, size, k):
    return lax.ppermute(x, axis, [(i, i ^ k) for i in range(size)])


def send_all(merge, taken, pattern, proxy):
    cols = lax.axis_size("col")
    slots, skel = taken.shape
    width = proxy.shape[2]
    mask = jnp.repeat(pattern, width // pattern.shape[1], axis=1).astype(BF16)
    rows = jnp.take_along_axis(proxy, jnp.maximum(taken, 0)[:, :, None], axis=1) * mask[:, None, :]
    rows = jnp.where(taken[:, :, None] >= 0, rows, jnp.zeros_like(rows)).astype(F32)
    placed = jnp.zeros((cols // merge,) + rows.shape, F32)
    final = lax.axis_index("col") // merge
    placed = lax.dynamic_update_index_in_dim(placed, rows, final, 0)
    summed = lax.psum(placed, "col")
    rows = lax.dynamic_index_in_dim(summed, final, 0, keepdims=False).astype(BF16)
    return jnp.zeros((), bool), rows.reshape(slots * skel, width)


def local(proxy_rows, pattern, first_pivots, merge_pivots, send_counts, near_field, self_inverse):
    cols, groups = lax.axis_size("col"), lax.axis_size("grp")
    merge = 1 << min(5, cols.bit_length() - 1)
    slots, skel = first_pivots.shape[1:]
    proxy = proxy_rows[0]
    share = slots * skel // merge
    room = -(-(share * 4) // (3 * 32)) * 32
    blocks, counts = pattern[0].T, send_counts[0].T
    compact, where, taken, most, dense = route(
        merge, room, jnp.swapaxes(merge_pivots[0], 1, 2), jnp.swapaxes(first_pivots, 0, 1), blocks, proxy
    )

    pieces = {0: compact, 1: swap(compact, "col", cols, 1)}
    for k in range(2, merge, 2):
        pieces[k] = swap(compact, "col", cols, k)
    for k in range(2, merge, 2):
        pieces[k + 1] = swap(pieces[k], "col", cols, 1)
    pieces = [pieces[k] for k in range(merge)]
    choose, picks = aim(where, merge * room)
    dense = lax.while_loop(
        lambda now: now[0], lambda now: send_all(merge, taken, pattern[0], proxy), (most[0] >= room, dense)
    )[1]
    early = slots * 2 // 3 // 2 * 2
    chunks = ((0, early), (early, slots - early))
    interp = coupling = None
    codes, owns = [], []
    for base, count in chunks:
        interp, coded, own = solve(base, count, most, choose, picks, blocks, counts, dense, proxy, pieces, interp)
        codes.append([swap(coded, "grp", groups, k) for k in range(1, groups)])
        owns.append(own)
    near, part = own_part(near_field[0], self_inverse[0], counts, owns)
    for (base, count), coded in zip(chunks, codes):
        coupling = couple(base, count, near, self_inverse[0], part, coded, coupling)
    return (interp[None], coupling[None])


def solution(mesh):
    return jax.shard_map(
        local,
        mesh=mesh,
        in_specs=(
            P("grp", "col", None, None),
            P("grp", "col", None),
            P("grp", "col", None),
            P("grp", None, None, None, None),
            P("grp", "col", None),
            P("grp", "col", None, None, None),
            P("grp", "col", None, None),
        ),
        out_specs=(P("grp", "col", None, None), P("grp", "col", None, None)),
        check_vma=False,
    )
```

```python
import functools

import jax
import jax.numpy as jnp
from jax import lax
from jax.experimental import pallas as pl
from jax.experimental.pallas import tpu as pltpu
from jax.sharding import PartitionSpec as P


F32 = jnp.float32
BF16 = jnp.bfloat16
I32 = jnp.int32
NT = (((1,), (1,)), ((), ()))
NN = (((1,), (0,)), ((), ()))
TN = (((0,), (0,)), ((), ()))
VMEM = pl.BlockSpec(memory_space=pltpu.VMEM)
HBM = pl.BlockSpec(memory_space=pltpu.HBM)
SMEM = pl.BlockSpec(memory_space=pltpu.SMEM)
PIVOTS = 4
Q_MAX = 32000.0
MAIN = 8000.0


def dot(a, b, dims=NN, precision=None):
    return lax.dot_general(a, b, dims, preferred_element_type=F32, precision=precision)


def in_hbm(*arrays):
    return [pltpu.with_memory_space_constraint(x, pltpu.HBM) for x in arrays]


def iota(shape, dim):
    return lax.broadcasted_iota(I32, shape, dim)


def box_masks(pattern_ref, width):
    blocks = pattern_ref.shape[0]
    spread = (iota((blocks, width), 1) // (width // blocks) == iota((blocks, width), 0)).astype(F32).astype(BF16)
    return dot(pattern_ref[...].astype(F32).astype(BF16), spread, TN)


def to_column(row, diagonal):
    return jnp.sum(jnp.where(diagonal, row, 0.0), axis=1, keepdims=True)


def to_row(column, diagonal):
    return jnp.sum(jnp.where(diagonal, column, 0.0), axis=0, keepdims=True)


def thirds(x):
    high = x.astype(BF16)
    rest = x - high.astype(F32)
    middle = rest.astype(BF16)
    return high, middle, (rest - middle.astype(F32)).astype(BF16)


def exact_dot(a, b):
    a, b = thirds(a), thirds(b)
    order = ((0, 0), (0, 1), (1, 0), (0, 2), (2, 0), (1, 1))
    return dot(jnp.concatenate([a[i] for i, _ in order], axis=1), jnp.concatenate([b[j] for _, j in order], axis=1), NT)


def route_kernel(merge, only, merge_hbm, first_hbm, pattern_hbm, proxy_ref, *refs):
    compact_ref, where_ref, taken_ref, most_ref, _, merge_ref, first_ref, pattern_ref, boxes, move, sems = refs
    rounds = merge.bit_length() - 1
    slots, unknowns, width = boxes.shape
    skel = first_ref.shape[2]
    room = compact_ref.shape[0]
    tables = ((merge_hbm, merge_ref), (first_hbm, first_ref), (pattern_hbm, pattern_ref))
    tables = [pltpu.make_async_copy(a, b, sems.at[slots + i]) for i, (a, b) in enumerate(tables)]
    copies = [pltpu.make_async_copy(proxy_ref.at[s], boxes.at[s], sems.at[s]) for s in range(slots)]
    for copy in tables + copies:
        copy.start()
    for copy in tables:
        copy.wait()
    me = lax.axis_index("col")
    final, local = (0 if only else me >> rounds), me & (merge - 1)
    picked = merge_ref[rounds - 1, :, final, :]
    upper = (picked >= skel).astype(I32)
    node, row = upper, picked - upper * skel
    for section in range(rounds - 2, -1, -1):
        count = merge >> (section + 1)
        picked = jnp.zeros_like(row)
        for n in range(count):
            found = jnp.take_along_axis(merge_ref[section, :, final * count + n, :], row, axis=1)
            picked = jnp.where(node == n, found, picked)
        upper = (picked >= skel).astype(I32)
        node, row = 2 * node + upper, picked - upper * skel
    unknown = jnp.take_along_axis(first_ref[:, 0, :], row, axis=1)
    before = (iota((skel, skel), 0) < iota((skel, skel), 1)).astype(BF16)
    ones = jnp.ones((skel, skel), BF16)
    above = (iota((slots, slots), 1) < iota((slots, slots), 0)).astype(BF16)
    place = jnp.zeros((slots, skel), F32)
    for d in range(merge):
        here = (node == d).astype(F32).astype(BF16)
        rank = dot(here, before) + dot(dot(above, here).astype(BF16), ones)
        place = jnp.where(node == d, rank, place)
    place = place.astype(I32)
    most_ref[0] = jnp.max(place)
    where_ref[...] = jnp.where(place < room, (node ^ local) * room + place, -1)
    mine = jnp.where(node == local, place, -1)
    taken_ref[...] = jnp.where(node == local, unknown, -1)
    mask = box_masks(pattern_ref, width).astype(BF16)
    kind = iota((8, skel), 0)
    source = jnp.zeros((room, 8), F32)
    for s in range(slots):
        into = (iota((room, skel), 0) == mine[s : s + 1, :]).astype(F32).astype(BF16)
        facts = jnp.where(kind == 0, unknown[s : s + 1, :], jnp.where(kind == 1, s + 1, 0))
        source += dot(into, facts.astype(F32).astype(BF16), NT)
    slot = source[:, 1:2].astype(I32) - 1
    key = jnp.broadcast_to(slot * unknowns + source[:, 0:1].astype(I32), (room, unknowns))
    for s in range(slots):
        match = iota((room, unknowns), 1) + s * unknowns == key
        move[:, s * unknowns : (s + 1) * unknowns] = match.astype(F32).astype(BF16)
    own = (iota((room, slots), 1) == slot).astype(F32).astype(BF16)
    for copy in copies:
        copy.wait()
    rows = dot(move[...], boxes[...].reshape(slots * unknowns, width)) * dot(own, mask)
    compact_ref[...] = rows.astype(BF16)


def route(merge, room, merge_pivots, first_pivots, pattern, proxy):
    slots, unknowns, width = proxy.shape
    skel = first_pivots.shape[2]
    return pl.pallas_call(
        functools.partial(route_kernel, merge, lax.axis_size("col") == merge),
        name="route",
        out_shape=[
            jax.ShapeDtypeStruct((room, width), BF16),
            jax.ShapeDtypeStruct((slots, skel), I32),
            jax.ShapeDtypeStruct((slots, skel), I32),
            jax.ShapeDtypeStruct((1,), I32),
            jax.ShapeDtypeStruct((slots * skel, width), BF16),
        ],
        in_specs=[HBM] * 4,
        out_specs=[VMEM, VMEM, VMEM, SMEM, HBM],
        scratch_shapes=[
            pltpu.VMEM(merge_pivots.shape, I32),
            pltpu.VMEM(first_pivots.shape, I32),
            pltpu.VMEM(pattern.shape, I32),
            pltpu.VMEM((slots, unknowns, width), BF16),
            pltpu.VMEM((room, slots * unknowns), BF16),
            pltpu.SemaphoreType.DMA((slots + 3,)),
        ],
        compiler_params=pltpu.CompilerParams(vmem_limit_bytes=16 << 20),
    )(*in_hbm(merge_pivots, first_pivots, pattern, proxy))


def aim_kernel(where_ref, choose_ref, picks_ref):
    slots, skel = where_ref.shape
    diagonal = iota((skel, skel), 0) == iota((skel, skel), 1)
    lanes = iota((skel, choose_ref.shape[1]), 1)
    for s in range(slots):
        spot = to_column(where_ref[s : s + 1, :].astype(F32), diagonal).astype(I32)
        choose_ref[s * skel : (s + 1) * skel, :] = (lanes == spot).astype(F32).astype(BF16)
    pair = 2 * skel
    gap = iota((pair, pair), 0) - (iota((pair, pair), 1) & skel)
    for k in range(skel):
        picks_ref[k] = (gap == k).astype(F32).astype(BF16)


def aim(where, total):
    slots, skel = where.shape
    return pl.pallas_call(
        aim_kernel,
        name="aim",
        out_shape=[
            jax.ShapeDtypeStruct((slots * skel, total), BF16),
            jax.ShapeDtypeStruct((skel, 2 * skel, 2 * skel), BF16),
        ],
        in_specs=[VMEM],
        out_specs=[VMEM, VMEM],
        compiler_params=pltpu.CompilerParams(vmem_limit_bytes=8 << 20),
        cost_estimate=pl.CostEstimate(flops=1 << 30, bytes_accessed=2 << 20, transcendentals=0),
    )(where)


def solve_kernel(base, slots, parts, most_ref, choose_ref, picks_ref, pattern_ref, counts_ref, dense_ref, proxy_ref, *refs):
    piece_refs = refs[:parts]
    interp_ref, coded_ref, found, pieces, skeleton, inverse, tails, boxes, weights, right, sems = refs[-11:]
    skel = interp_ref.shape[1]
    unknowns, width = proxy_ref.shape[1:]
    room = piece_refs[0].shape[0]
    half = slots // 2
    pair = 2 * skel
    diagonal = iota((skel, skel), 0) == iota((skel, skel), 1)
    loads = [pltpu.make_async_copy(proxy_ref.at[base + s], boxes.at[s], sems.at[1 + slots + s]) for s in range(slots)]
    for copy in loads:
        copy.start()

    @pl.when(most_ref[0] < room)
    def _():
        for k in range(parts):
            pieces[k * room : (k + 1) * room, :] = piece_refs[k][...]
        skeleton[...] = dot(choose_ref[base * skel : (base + slots) * skel, :], pieces[...]).astype(BF16)

    @pl.when(most_ref[0] >= room)
    def _():
        copy = pltpu.make_async_copy(dense_ref.at[pl.ds(base * skel, slots * skel), :], skeleton, sems.at[0])
        copy.start()
        copy.wait()

    mask = box_masks(pattern_ref, width).astype(BF16)
    for h in range(half):
        for side in range(2):
            rows = skeleton[(h + side * half) * skel : (h + side * half + 1) * skel, :]
            inverse[h * skel : (h + 1) * skel, side * skel : (side + 1) * skel] = dot(rows, rows, NT)

    side, column, sublane = iota((8, pair), 1) & skel, iota((8, pair), 1) & (skel - 1), iota((8, pair), 0)
    wide_side, wide_column = iota((skel, pair), 1) & skel, iota((skel, pair), 1) & (skel - 1)

    blank = jnp.zeros((skel, width), BF16)
    for s in range(slots):
        rows = skeleton[s * skel : (s + 1) * skel, :] * mask[base + s : base + s + 1, :]
        weights[s] = jnp.concatenate([rows, blank] if s < half else [blank, rows], axis=0)
    for copy in loads:
        copy.wait()
    steps = skel // PIVOTS
    spread = half // 2 if half > 2 else 0
    stretch = unknowns
    while slots * unknowns <= steps * stretch // 2:
        stretch //= 2
    turns = unknowns // stretch

    def line(k):
        row = jnp.broadcast_to(inverse[pl.ds(k, 1), :], (8, pair))
        for h in range(1, half):
            row = jnp.where(sublane == h, jnp.broadcast_to(inverse[pl.ds(h * skel + k, 1), :], (8, pair)), row)
        return row

    def eliminate(step, carry):
        k = PIVOTS * step
        span = range(PIVOTS)
        rows = [line(k + i) for i in span]
        small = [[jnp.take_along_axis(rows[i], side + (k + j), axis=1) for j in span] for i in span]
        for p in span:
            r = 1.0 / small[p][p]
            pivot = [r if j == p else small[p][j] * r for j in span]
            for i in span:
                if i != p:
                    f = small[i][p]
                    small[i] = [-f * r if j == p else small[i][j] - f * pivot[j] for j in span]
            small[p] = pivot
        fresh = []
        for i in span:
            row = small[i][0] * rows[0]
            for j in span[1:]:
                row = row + small[i][j] * rows[j]
            for j in span:
                row = jnp.where(column == k + j, small[i][j], row)
            fresh.append(row)
        blocks = [inverse[h * skel : (h + 1) * skel, :] for h in range(half)]
        if spread:
            each = jnp.concatenate([picks_ref[k + j] for j in span], axis=1)
            high, middle, low = thirds(jnp.concatenate(blocks[:spread], axis=0))
            columns = dot(high, each) + dot(middle, each) + dot(low, each)
        for h, block in enumerate(blocks):
            kept = jnp.where((wide_column // PIVOTS) == step, 0.0, block)
            for j in span:
                if h < spread:
                    col = columns[h * skel : (h + 1) * skel, j * pair : (j + 1) * pair]
                else:
                    col = jnp.take_along_axis(block, wide_side + (k + j), axis=1)
                kept = kept - col * fresh[j][h : h + 1, :]
            inverse[h * skel : (h + 1) * skel, :] = kept
        for h in range(half):
            for j in span:
                inverse[pl.ds(h * skel + k + j, 1), :] = fresh[j][h : h + 1, :]
        turn = jnp.minimum(step, slots * turns - 1)
        box, part = turn // turns, pl.ds(pl.multiple_of((turn % turns) * stretch, stretch), stretch)
        right[box, part, :] = dot(boxes[box, part, :], weights[box], NT)
        return carry

    lax.fori_loop(0, steps, eliminate, 0)

    groups = counts_ref.shape[0]
    unit = (iota((groups, unknowns - pair), 0) == iota((groups, unknowns - pair), 1)).astype(F32).astype(BF16)
    owed = dot(counts_ref[...].astype(F32).astype(BF16), unit, TN)
    tails[...] = jnp.zeros_like(tails)
    left = iota((skel, pair), 1) < skel
    writes = []
    for h in range(half):
        both = inverse[h * skel : (h + 1) * skel, :]
        both = jnp.concatenate([jnp.where(left, both, 0.0), jnp.where(left, 0.0, both)], axis=0)
        xs = exact_dot(both, right[h] + right[h + half])
        tops = jnp.max(jnp.abs(xs), axis=1, keepdims=True)
        for side in range(2):
            s = h + side * half
            part = slice(side * skel, (side + 1) * skel)
            found[s] = xs[part]
            writes.append(pltpu.make_async_copy(found.at[s], interp_ref.at[base + s], sems.at[1 + s]))
            writes[-1].start()
            tails[s : s + 1, :skel] = to_row(tops[part], diagonal)
    rows = jnp.maximum(tails[:, :skel], 1e-30)
    power = jnp.clip(jnp.floor(jnp.log2(rows)), -100.0, 126.0)
    main = jnp.floor(rows * jnp.exp2(-power) * MAIN) + 1.0
    factor = (Q_MAX * MAIN) / (main * jnp.exp2(power))
    for s in range(slots):
        codes = found[s] * to_column(factor[s : s + 1, :], diagonal)
        codes = (codes + jnp.where(codes >= 0, 0.5, -0.5)).astype(I32)
        coded_ref[s * skel : (s + 1) * skel, :] = codes.astype(jnp.int16)
        tails[s : s + 1, pair:] = owed[base + s : base + s + 1, :]
    tails[:, :pair] = jnp.concatenate([main, power], axis=1)
    coded_ref[slots * skel :, :] = tails[...].astype(I32).astype(jnp.int16)
    for copy in writes:
        copy.wait()


def solve(base, slots, most, choose, picks, pattern, counts, dense, proxy, pieces, interp):
    unknowns, width = proxy.shape[1:]
    skel = choose.shape[0] // proxy.shape[0]
    parts, room = len(pieces), pieces[0].shape[0]
    extra = -(-slots // 8) * 8
    args = [most, choose, picks, pattern, counts, *in_hbm(dense, proxy), *pieces] + ([] if interp is None else [interp])
    return pl.pallas_call(
        functools.partial(solve_kernel, base, slots, parts),
        name="solve",
        out_shape=[
            jax.ShapeDtypeStruct((proxy.shape[0], skel, unknowns), F32),
            jax.ShapeDtypeStruct((slots * skel + extra, unknowns), jnp.int16),
            jax.ShapeDtypeStruct((slots, skel, unknowns), F32),
        ],
        in_specs=[SMEM, VMEM, VMEM, VMEM, VMEM, HBM, HBM] + [VMEM] * parts + [HBM] * (interp is not None),
        out_specs=[HBM, VMEM, VMEM],
        input_output_aliases={} if interp is None else {len(args) - 1: 0},
        scratch_shapes=[
            pltpu.VMEM((parts * room, width), BF16),
            pltpu.VMEM((slots * skel, width), BF16),
            pltpu.VMEM((slots // 2 * skel, 2 * skel), F32),
            pltpu.VMEM((extra, unknowns), F32),
            pltpu.VMEM((slots, unknowns, width), BF16),
            pltpu.VMEM((slots, 2 * skel, width), BF16),
            pltpu.VMEM((slots, unknowns, 2 * skel), F32),
            pltpu.SemaphoreType.DMA((1 + 2 * slots,)),
        ],
        compiler_params=pltpu.CompilerParams(vmem_limit_bytes=24 << 20),
        cost_estimate=pl.CostEstimate(flops=1 << 33, bytes_accessed=8 << 20, transcendentals=0),
    )(*args)


def owed_rows(counts, skel):
    mine = jnp.where(iota(counts.shape, 1) == lax.axis_index("grp"), counts, 0.0)
    return iota((counts.shape[0], skel), 1) < jnp.sum(mine, axis=1, keepdims=True).astype(I32)


def turn(rows, inverse, scale):
    skel = rows.shape[0]
    high = rows.astype(BF16)
    low = (rows - high.astype(F32)).astype(BF16)
    turned = dot(jnp.concatenate([high, low], axis=0), inverse, NT)
    turned = (turned[:skel] + turned[skel:]) * scale
    high = turned.astype(BF16)
    return jnp.concatenate([high, (turned - high.astype(F32)).astype(BF16)], axis=0)


def own_kernel(groups, near_ref, inverse_ref, counts_ref, *refs):
    own_refs = refs[:-4]
    near, part_ref, turns, sems = refs[-4:]
    slots, skel, unknowns = part_ref.shape
    copies = [pltpu.make_async_copy(near_ref.at[b], near.at[b], sems.at[b]) for b in range(slots)]
    for copy in copies:
        copy.start()
    here = lax.axis_index("grp")
    diagonal = iota((skel, skel), 0) == iota((skel, skel), 1)
    unit = (iota((groups, 2 * skel), 0) == iota((groups, 2 * skel), 1)).astype(F32).astype(BF16)
    counts = dot(counts_ref[...].astype(F32).astype(BF16), unit, TN)
    scales = owed_rows(counts, skel).astype(F32)
    b = 0
    for ref in own_refs:
        for i in range(ref.shape[0]):
            turns[b] = turn(ref[i], inverse_ref[b], to_column(scales[b : b + 1, :], diagonal))
            b += 1
    for copy in copies:
        copy.wait()
    for b in range(slots):
        both = dot(turns[b], near[b, here], NT)
        part_ref[b] = both[:skel] + both[skel:]


def own_part(near, inverse, counts, owns):
    slots, groups, unknowns = near.shape[:3]
    skel = owns[0].shape[1]
    return pl.pallas_call(
        functools.partial(own_kernel, groups),
        name="own_part",
        out_shape=[jax.ShapeDtypeStruct(near.shape, BF16), jax.ShapeDtypeStruct((slots, skel, unknowns), F32)],
        in_specs=[HBM] + [VMEM] * (2 + len(owns)),
        out_specs=[VMEM, VMEM],
        scratch_shapes=[pltpu.VMEM((slots, 2 * skel, unknowns), BF16), pltpu.SemaphoreType.DMA((slots,))],
        compiler_params=pltpu.CompilerParams(vmem_limit_bytes=24 << 20),
        cost_estimate=pl.CostEstimate(flops=1 << 31, bytes_accessed=8 << 20, transcendentals=0),
    )(*in_hbm(near), inverse, counts, *owns)


def couple_kernel(base, groups, near, inverse, part_ref, *refs):
    coded_refs = refs[: groups - 1]
    out_ref, out, turns, sems = refs[-4:]
    slots, skel, unknowns = out.shape
    here = lax.axis_index("grp")
    diagonal = iota((skel, skel), 0) == iota((skel, skel), 1)
    scales = []
    for ref in coded_refs:
        tail = ref[slots * skel :, :].astype(I32).astype(F32)
        main, power, counts = tail[:, :skel], tail[:, skel : 2 * skel], tail[:, 2 * skel :]
        scale = main * jnp.exp2(power) * (1.0 / (MAIN * Q_MAX))
        scales.append(jnp.where(owed_rows(counts, skel), scale, 0.0))
    for b in range(slots):
        for k, ref in enumerate(coded_refs):
            rows = ref[b * skel : (b + 1) * skel, :].astype(I32).astype(F32)
            turns[b, k] = turn(rows, inverse[base + b], to_column(scales[k][b : b + 1, :], diagonal))
    writes = []
    for b in range(slots):
        total = None
        for k in range(groups - 1):
            term = dot(turns[b, k], near[base + b, here ^ (k + 1)], NT)
            total = term if total is None else total + term
        out[b] = part_ref[base + b] + (total[:skel] + total[skel:])
        writes.append(pltpu.make_async_copy(out.at[b], out_ref.at[base + b], sems.at[b]))
        writes[-1].start()
    for copy in writes:
        copy.wait()


def couple(base, slots, near, inverse, part, coded, coupling):
    groups, unknowns = near.shape[1:3]
    skel = part.shape[1]
    args = [near, inverse, part, *coded] + ([] if coupling is None else [coupling])
    return pl.pallas_call(
        functools.partial(couple_kernel, base, groups),
        name="couple",
        out_shape=jax.ShapeDtypeStruct(part.shape, F32),
        in_specs=[VMEM] * (3 + len(coded)) + [HBM] * (coupling is not None),
        out_specs=HBM,
        input_output_aliases={} if coupling is None else {len(args) - 1: 0},
        scratch_shapes=[
            pltpu.VMEM((slots, skel, unknowns), F32),
            pltpu.VMEM((slots, groups - 1, 2 * skel, unknowns), BF16),
            pltpu.SemaphoreType.DMA((slots,)),
        ],
        compiler_params=pltpu.CompilerParams(vmem_limit_bytes=24 << 20),
    )(*args)


def swap(x, axis, size, k):
    return lax.ppermute(x, axis, [(i, i ^ k) for i in range(size)])


def send_all(merge, taken, pattern, proxy):
    cols = lax.axis_size("col")
    slots, skel = taken.shape
    width = proxy.shape[2]
    mask = jnp.repeat(pattern, width // pattern.shape[1], axis=1).astype(BF16)
    rows = jnp.take_along_axis(proxy, jnp.maximum(taken, 0)[:, :, None], axis=1) * mask[:, None, :]
    rows = jnp.where(taken[:, :, None] >= 0, rows, jnp.zeros_like(rows)).astype(F32)
    placed = jnp.zeros((cols // merge,) + rows.shape, F32)
    final = lax.axis_index("col") // merge
    placed = lax.dynamic_update_index_in_dim(placed, rows, final, 0)
    summed = lax.psum(placed, "col")
    rows = lax.dynamic_index_in_dim(summed, final, 0, keepdims=False).astype(BF16)
    return jnp.zeros((), bool), rows.reshape(slots * skel, width)


def local(proxy_rows, pattern, first_pivots, merge_pivots, send_counts, near_field, self_inverse):
    cols, groups = lax.axis_size("col"), lax.axis_size("grp")
    merge = 1 << min(5, cols.bit_length() - 1)
    slots, skel = first_pivots.shape[1:]
    proxy = proxy_rows[0]
    share = slots * skel // merge
    room = -(-(share * 4) // (3 * 32)) * 32
    blocks, counts = pattern[0].T, send_counts[0].T
    compact, where, taken, most, dense = route(
        merge, room, jnp.swapaxes(merge_pivots[0], 1, 2), jnp.swapaxes(first_pivots, 0, 1), blocks, proxy
    )

    pieces = {0: compact, 1: swap(compact, "col", cols, 1)}
    for k in range(2, merge, 2):
        pieces[k] = swap(compact, "col", cols, k)
    for k in range(2, merge, 2):
        pieces[k + 1] = swap(pieces[k], "col", cols, 1)
    pieces = [pieces[k] for k in range(merge)]
    choose, picks = aim(where, merge * room)
    dense = lax.while_loop(
        lambda now: now[0], lambda now: send_all(merge, taken, pattern[0], proxy), (most[0] >= room, dense)
    )[1]
    early = slots * 2 // 3 // 2 * 2
    chunks = ((0, early), (early, slots - early))
    interp = coupling = None
    codes, owns = [], []
    for base, count in chunks:
        interp, coded, own = solve(base, count, most, choose, picks, blocks, counts, dense, proxy, pieces, interp)
        codes.append([swap(coded, "grp", groups, k) for k in range(1, groups)])
        owns.append(own)
    near, part = own_part(near_field[0], self_inverse[0], counts, owns)
    for (base, count), coded in zip(chunks, codes):
        coupling = couple(base, count, near, self_inverse[0], part, coded, coupling)
    return (interp[None], coupling[None])


def solution(mesh):
    return jax.shard_map(
        local,
        mesh=mesh,
        in_specs=(
            P("grp", "col", None, None),
            P("grp", "col", None),
            P("grp", "col", None),
            P("grp", None, None, None, None),
            P("grp", "col", None),
            P("grp", "col", None, None, None),
            P("grp", "col", None, None),
        ),
        out_specs=(P("grp", "col", None, None), P("grp", "col", None, None)),
        check_vma=False,
    )
```

```python
import functools

import jax
import jax.numpy as jnp
from jax import lax
from jax.experimental import pallas as pl
from jax.experimental.pallas import tpu as pltpu
from jax.sharding import PartitionSpec as P


F32 = jnp.float32
BF16 = jnp.bfloat16
I32 = jnp.int32
NT = (((1,), (1,)), ((), ()))
NN = (((1,), (0,)), ((), ()))
TN = (((0,), (0,)), ((), ()))
VMEM = pl.BlockSpec(memory_space=pltpu.VMEM)
HBM = pl.BlockSpec(memory_space=pltpu.HBM)
SMEM = pl.BlockSpec(memory_space=pltpu.SMEM)
PIVOTS = 4
Q_MAX = 32000.0
MAIN = 8000.0


def dot(a, b, dims=NN, precision=None):
    return lax.dot_general(a, b, dims, preferred_element_type=F32, precision=precision)


def in_hbm(*arrays):
    return [pltpu.with_memory_space_constraint(x, pltpu.HBM) for x in arrays]


def iota(shape, dim):
    return lax.broadcasted_iota(I32, shape, dim)


def box_masks(pattern_ref, width):
    blocks = pattern_ref.shape[0]
    spread = (iota((blocks, width), 1) // (width // blocks) == iota((blocks, width), 0)).astype(F32).astype(BF16)
    return dot(pattern_ref[...].astype(F32).astype(BF16), spread, TN)


def to_column(row, diagonal):
    return jnp.sum(jnp.where(diagonal, row, 0.0), axis=1, keepdims=True)


def to_row(column, diagonal):
    return jnp.sum(jnp.where(diagonal, column, 0.0), axis=0, keepdims=True)


def thirds(x):
    high = x.astype(BF16)
    rest = x - high.astype(F32)
    middle = rest.astype(BF16)
    return high, middle, (rest - middle.astype(F32)).astype(BF16)


def exact_dot(a, b):
    a, b = thirds(a), thirds(b)
    order = ((0, 0), (0, 1), (1, 0), (0, 2), (2, 0), (1, 1))
    return dot(jnp.concatenate([a[i] for i, _ in order], axis=1), jnp.concatenate([b[j] for _, j in order], axis=1), NT)


def route_kernel(merge, only, merge_hbm, first_hbm, pattern_hbm, proxy_ref, *refs):
    compact_ref, where_ref, taken_ref, most_ref, _, merge_ref, first_ref, pattern_ref, boxes, move, sems = refs
    rounds = merge.bit_length() - 1
    slots, unknowns, width = boxes.shape
    skel = first_ref.shape[2]
    room = compact_ref.shape[0]
    tables = ((merge_hbm, merge_ref), (first_hbm, first_ref), (pattern_hbm, pattern_ref))
    tables = [pltpu.make_async_copy(a, b, sems.at[slots + i]) for i, (a, b) in enumerate(tables)]
    copies = [pltpu.make_async_copy(proxy_ref.at[s], boxes.at[s], sems.at[s]) for s in range(slots)]
    for copy in tables + copies:
        copy.start()
    for copy in tables:
        copy.wait()
    me = lax.axis_index("col")
    final, local = (0 if only else me >> rounds), me & (merge - 1)
    picked = merge_ref[rounds - 1, :, final, :]
    upper = (picked >= skel).astype(I32)
    node, row = upper, picked - upper * skel
    for section in range(rounds - 2, -1, -1):
        count = merge >> (section + 1)
        picked = jnp.zeros_like(row)
        for n in range(count):
            found = jnp.take_along_axis(merge_ref[section, :, final * count + n, :], row, axis=1)
            picked = jnp.where(node == n, found, picked)
        upper = (picked >= skel).astype(I32)
        node, row = 2 * node + upper, picked - upper * skel
    unknown = jnp.take_along_axis(first_ref[:, 0, :], row, axis=1)
    before = (iota((skel, skel), 0) < iota((skel, skel), 1)).astype(BF16)
    ones = jnp.ones((skel, skel), BF16)
    above = (iota((slots, slots), 1) < iota((slots, slots), 0)).astype(BF16)
    place = jnp.zeros((slots, skel), F32)
    for d in range(merge):
        here = (node == d).astype(F32).astype(BF16)
        rank = dot(here, before) + dot(dot(above, here).astype(BF16), ones)
        place = jnp.where(node == d, rank, place)
    place = place.astype(I32)
    most_ref[0] = jnp.max(place)
    where_ref[...] = jnp.where(place < room, (node ^ local) * room + place, -1)
    mine = jnp.where(node == local, place, -1)
    taken_ref[...] = jnp.where(node == local, unknown, -1)
    mask = box_masks(pattern_ref, width).astype(BF16)
    kind = iota((8, skel), 0)
    source = jnp.zeros((room, 8), F32)
    for s in range(slots):
        into = (iota((room, skel), 0) == mine[s : s + 1, :]).astype(F32).astype(BF16)
        facts = jnp.where(kind == 0, unknown[s : s + 1, :], jnp.where(kind == 1, s + 1, 0))
        source += dot(into, facts.astype(F32).astype(BF16), NT)
    slot = source[:, 1:2].astype(I32) - 1
    key = jnp.broadcast_to(slot * unknowns + source[:, 0:1].astype(I32), (room, unknowns))
    for s in range(slots):
        match = iota((room, unknowns), 1) + s * unknowns == key
        move[:, s * unknowns : (s + 1) * unknowns] = match.astype(F32).astype(BF16)
    own = (iota((room, slots), 1) == slot).astype(F32).astype(BF16)
    for copy in copies:
        copy.wait()
    rows = dot(move[...], boxes[...].reshape(slots * unknowns, width)) * dot(own, mask)
    compact_ref[...] = rows.astype(BF16)


def route(merge, room, merge_pivots, first_pivots, pattern, proxy):
    slots, unknowns, width = proxy.shape
    skel = first_pivots.shape[2]
    return pl.pallas_call(
        functools.partial(route_kernel, merge, lax.axis_size("col") == merge),
        name="route",
        out_shape=[
            jax.ShapeDtypeStruct((room, width), BF16),
            jax.ShapeDtypeStruct((slots, skel), I32),
            jax.ShapeDtypeStruct((slots, skel), I32),
            jax.ShapeDtypeStruct((1,), I32),
            jax.ShapeDtypeStruct((slots * skel, width), BF16),
        ],
        in_specs=[HBM] * 4,
        out_specs=[VMEM, VMEM, VMEM, SMEM, HBM],
        scratch_shapes=[
            pltpu.VMEM(merge_pivots.shape, I32),
            pltpu.VMEM(first_pivots.shape, I32),
            pltpu.VMEM(pattern.shape, I32),
            pltpu.VMEM((slots, unknowns, width), BF16),
            pltpu.VMEM((room, slots * unknowns), BF16),
            pltpu.SemaphoreType.DMA((slots + 3,)),
        ],
        compiler_params=pltpu.CompilerParams(vmem_limit_bytes=16 << 20),
    )(*in_hbm(merge_pivots, first_pivots, pattern, proxy))


def aim_kernel(where_ref, choose_ref, picks_ref):
    slots, skel = where_ref.shape
    diagonal = iota((skel, skel), 0) == iota((skel, skel), 1)
    lanes = iota((skel, choose_ref.shape[1]), 1)
    for s in range(slots):
        spot = to_column(where_ref[s : s + 1, :].astype(F32), diagonal).astype(I32)
        choose_ref[s * skel : (s + 1) * skel, :] = (lanes == spot).astype(F32).astype(BF16)
    pair = 2 * skel
    gap = iota((pair, pair), 0) - (iota((pair, pair), 1) & skel)
    for k in range(skel):
        picks_ref[k] = (gap == k).astype(F32).astype(BF16)


def aim(where, total):
    slots, skel = where.shape
    return pl.pallas_call(
        aim_kernel,
        name="aim",
        out_shape=[
            jax.ShapeDtypeStruct((slots * skel, total), BF16),
            jax.ShapeDtypeStruct((skel, 2 * skel, 2 * skel), BF16),
        ],
        in_specs=[VMEM],
        out_specs=[VMEM, VMEM],
        compiler_params=pltpu.CompilerParams(vmem_limit_bytes=8 << 20),
        cost_estimate=pl.CostEstimate(flops=1 << 30, bytes_accessed=2 << 20, transcendentals=0),
    )(where)


def solve_kernel(base, slots, parts, most_ref, choose_ref, picks_ref, pattern_ref, counts_ref, dense_ref, proxy_ref, *refs):
    piece_refs = refs[:parts]
    interp_ref, coded_ref, found, pieces, skeleton, inverse, tails, boxes, weights, right, sems = refs[-11:]
    skel = interp_ref.shape[1]
    unknowns, width = proxy_ref.shape[1:]
    room = piece_refs[0].shape[0]
    half = slots // 2
    pair = 2 * skel
    diagonal = iota((skel, skel), 0) == iota((skel, skel), 1)
    loads = [pltpu.make_async_copy(proxy_ref.at[base + s], boxes.at[s], sems.at[1 + slots + s]) for s in range(slots)]
    for copy in loads:
        copy.start()

    @pl.when(most_ref[0] < room)
    def _():
        for k in range(parts):
            pieces[k * room : (k + 1) * room, :] = piece_refs[k][...]
        skeleton[...] = dot(choose_ref[base * skel : (base + slots) * skel, :], pieces[...]).astype(BF16)

    @pl.when(most_ref[0] >= room)
    def _():
        copy = pltpu.make_async_copy(dense_ref.at[pl.ds(base * skel, slots * skel), :], skeleton, sems.at[0])
        copy.start()
        copy.wait()

    mask = box_masks(pattern_ref, width).astype(BF16)
    for h in range(half):
        for side in range(2):
            rows = skeleton[(h + side * half) * skel : (h + side * half + 1) * skel, :]
            inverse[h * skel : (h + 1) * skel, side * skel : (side + 1) * skel] = dot(rows, rows, NT)

    side, column, sublane = iota((8, pair), 1) & skel, iota((8, pair), 1) & (skel - 1), iota((8, pair), 0)
    wide_side, wide_column = iota((skel, pair), 1) & skel, iota((skel, pair), 1) & (skel - 1)

    blank = jnp.zeros((skel, width), BF16)
    for s in range(slots):
        rows = skeleton[s * skel : (s + 1) * skel, :] * mask[base + s : base + s + 1, :]
        weights[s] = jnp.concatenate([rows, blank] if s < half else [blank, rows], axis=0)
    for copy in loads:
        copy.wait()
    steps = skel // PIVOTS
    spread = half // 2 if half > 2 else 0
    stretch = unknowns
    while slots * unknowns <= steps * stretch // 2:
        stretch //= 2
    turns = unknowns // stretch

    def line(k):
        row = jnp.broadcast_to(inverse[pl.ds(k, 1), :], (8, pair))
        for h in range(1, half):
            row = jnp.where(sublane == h, jnp.broadcast_to(inverse[pl.ds(h * skel + k, 1), :], (8, pair)), row)
        return row

    def eliminate(step, carry):
        k = PIVOTS * step
        span = range(PIVOTS)
        rows = [line(k + i) for i in span]
        small = [[jnp.take_along_axis(rows[i], side + (k + j), axis=1) for j in span] for i in span]
        for p in span:
            r = 1.0 / small[p][p]
            pivot = [r if j == p else small[p][j] * r for j in span]
            for i in span:
                if i != p:
                    f = small[i][p]
                    small[i] = [-f * r if j == p else small[i][j] - f * pivot[j] for j in span]
            small[p] = pivot
        fresh = []
        for i in span:
            row = small[i][0] * rows[0]
            for j in span[1:]:
                row = row + small[i][j] * rows[j]
            for j in span:
                row = jnp.where(column == k + j, small[i][j], row)
            fresh.append(row)
        blocks = [inverse[h * skel : (h + 1) * skel, :] for h in range(half)]
        if spread:
            each = jnp.concatenate([picks_ref[k + j] for j in span], axis=1)
            high, middle, low = thirds(jnp.concatenate(blocks[:spread], axis=0))
            columns = dot(high, each) + dot(middle, each) + dot(low, each)
        for h, block in enumerate(blocks):
            kept = jnp.where((wide_column // PIVOTS) == step, 0.0, block)
            for j in span:
                if h < spread:
                    col = columns[h * skel : (h + 1) * skel, j * pair : (j + 1) * pair]
                else:
                    col = jnp.take_along_axis(block, wide_side + (k + j), axis=1)
                kept = kept - col * fresh[j][h : h + 1, :]
            inverse[h * skel : (h + 1) * skel, :] = kept
        for h in range(half):
            for j in span:
                inverse[pl.ds(h * skel + k + j, 1), :] = fresh[j][h : h + 1, :]
        turn = jnp.minimum(step, slots * turns - 1)
        box, part = turn // turns, pl.ds(pl.multiple_of((turn % turns) * stretch, stretch), stretch)
        right[box, part, :] = dot(boxes[box, part, :], weights[box], NT)
        return carry

    lax.fori_loop(0, steps, eliminate, 0)

    groups = counts_ref.shape[0]
    unit = (iota((groups, unknowns - pair), 0) == iota((groups, unknowns - pair), 1)).astype(F32).astype(BF16)
    owed = dot(counts_ref[...].astype(F32).astype(BF16), unit, TN)
    tails[...] = jnp.zeros_like(tails)
    left = iota((skel, pair), 1) < skel
    writes = []
    for h in range(half):
        both = inverse[h * skel : (h + 1) * skel, :]
        both = jnp.concatenate([jnp.where(left, both, 0.0), jnp.where(left, 0.0, both)], axis=0)
        xs = exact_dot(both, right[h] + right[h + half])
        tops = jnp.max(jnp.abs(xs), axis=1, keepdims=True)
        for side in range(2):
            s = h + side * half
            part = slice(side * skel, (side + 1) * skel)
            found[s] = xs[part]
            writes.append(pltpu.make_async_copy(found.at[s], interp_ref.at[base + s], sems.at[1 + s]))
            writes[-1].start()
            tails[s : s + 1, :skel] = to_row(tops[part], diagonal)
    rows = jnp.maximum(tails[:, :skel], 1e-30)
    power = jnp.clip(jnp.floor(jnp.log2(rows)), -100.0, 126.0)
    main = jnp.floor(rows * jnp.exp2(-power) * MAIN) + 1.0
    factor = (Q_MAX * MAIN) / (main * jnp.exp2(power))
    for s in range(slots):
        codes = found[s] * to_column(factor[s : s + 1, :], diagonal)
        codes = jnp.floor(codes + 0.5).astype(I32)
        coded_ref[s * skel : (s + 1) * skel, :] = codes.astype(jnp.int16)
        tails[s : s + 1, pair:] = owed[base + s : base + s + 1, :]
    tails[:, :pair] = jnp.concatenate([main, power], axis=1)
    coded_ref[slots * skel :, :] = tails[...].astype(I32).astype(jnp.int16)
    for copy in writes:
        copy.wait()


def solve(base, slots, most, choose, picks, pattern, counts, dense, proxy, pieces, interp):
    unknowns, width = proxy.shape[1:]
    skel = choose.shape[0] // proxy.shape[0]
    parts, room = len(pieces), pieces[0].shape[0]
    extra = -(-slots // 8) * 8
    args = [most, choose, picks, pattern, counts, *in_hbm(dense, proxy), *pieces] + ([] if interp is None else [interp])
    return pl.pallas_call(
        functools.partial(solve_kernel, base, slots, parts),
        name="solve",
        out_shape=[
            jax.ShapeDtypeStruct((proxy.shape[0], skel, unknowns), F32),
            jax.ShapeDtypeStruct((slots * skel + extra, unknowns), jnp.int16),
            jax.ShapeDtypeStruct((slots, skel, unknowns), F32),
        ],
        in_specs=[SMEM, VMEM, VMEM, VMEM, VMEM, HBM, HBM] + [VMEM] * parts + [HBM] * (interp is not None),
        out_specs=[HBM, VMEM, VMEM],
        input_output_aliases={} if interp is None else {len(args) - 1: 0},
        scratch_shapes=[
            pltpu.VMEM((parts * room, width), BF16),
            pltpu.VMEM((slots * skel, width), BF16),
            pltpu.VMEM((slots // 2 * skel, 2 * skel), F32),
            pltpu.VMEM((extra, unknowns), F32),
            pltpu.VMEM((slots, unknowns, width), BF16),
            pltpu.VMEM((slots, 2 * skel, width), BF16),
            pltpu.VMEM((slots, unknowns, 2 * skel), F32),
            pltpu.SemaphoreType.DMA((1 + 2 * slots,)),
        ],
        compiler_params=pltpu.CompilerParams(vmem_limit_bytes=24 << 20),
        cost_estimate=pl.CostEstimate(flops=1 << 33, bytes_accessed=8 << 20, transcendentals=0),
    )(*args)


def owed_rows(counts, skel):
    mine = jnp.where(iota(counts.shape, 1) == lax.axis_index("grp"), counts, 0.0)
    return iota((counts.shape[0], skel), 1) < jnp.sum(mine, axis=1, keepdims=True).astype(I32)


def turn(rows, inverse, scale):
    skel = rows.shape[0]
    high = rows.astype(BF16)
    low = (rows - high.astype(F32)).astype(BF16)
    turned = dot(jnp.concatenate([high, low], axis=0), inverse, NT)
    turned = (turned[:skel] + turned[skel:]) * scale
    high = turned.astype(BF16)
    return jnp.concatenate([high, (turned - high.astype(F32)).astype(BF16)], axis=0)


def own_kernel(groups, near_ref, inverse_ref, counts_ref, *refs):
    own_refs = refs[:-4]
    near, part_ref, turns, sems = refs[-4:]
    slots, skel, unknowns = part_ref.shape
    copies = [pltpu.make_async_copy(near_ref.at[b], near.at[b], sems.at[b]) for b in range(slots)]
    for copy in copies:
        copy.start()
    here = lax.axis_index("grp")
    diagonal = iota((skel, skel), 0) == iota((skel, skel), 1)
    unit = (iota((groups, 2 * skel), 0) == iota((groups, 2 * skel), 1)).astype(F32).astype(BF16)
    counts = dot(counts_ref[...].astype(F32).astype(BF16), unit, TN)
    scales = owed_rows(counts, skel).astype(F32)
    b = 0
    for ref in own_refs:
        for i in range(ref.shape[0]):
            turns[b] = turn(ref[i], inverse_ref[b], to_column(scales[b : b + 1, :], diagonal))
            b += 1
    for copy in copies:
        copy.wait()
    for b in range(slots):
        both = dot(turns[b], near[b, here], NT)
        part_ref[b] = both[:skel] + both[skel:]


def own_part(near, inverse, counts, owns):
    slots, groups, unknowns = near.shape[:3]
    skel = owns[0].shape[1]
    return pl.pallas_call(
        functools.partial(own_kernel, groups),
        name="own_part",
        out_shape=[jax.ShapeDtypeStruct(near.shape, BF16), jax.ShapeDtypeStruct((slots, skel, unknowns), F32)],
        in_specs=[HBM] + [VMEM] * (2 + len(owns)),
        out_specs=[VMEM, VMEM],
        scratch_shapes=[pltpu.VMEM((slots, 2 * skel, unknowns), BF16), pltpu.SemaphoreType.DMA((slots,))],
        compiler_params=pltpu.CompilerParams(vmem_limit_bytes=24 << 20),
        cost_estimate=pl.CostEstimate(flops=1 << 31, bytes_accessed=8 << 20, transcendentals=0),
    )(*in_hbm(near), inverse, counts, *owns)


def couple_kernel(base, groups, near, inverse, part_ref, *refs):
    coded_refs = refs[: groups - 1]
    out_ref, out, turns, sems = refs[-4:]
    slots, skel, unknowns = out.shape
    here = lax.axis_index("grp")
    diagonal = iota((skel, skel), 0) == iota((skel, skel), 1)
    scales = []
    for ref in coded_refs:
        tail = ref[slots * skel :, :].astype(I32).astype(F32)
        main, power, counts = tail[:, :skel], tail[:, skel : 2 * skel], tail[:, 2 * skel :]
        scale = main * jnp.exp2(power) * (1.0 / (MAIN * Q_MAX))
        scales.append(jnp.where(owed_rows(counts, skel), scale, 0.0))
    for b in range(slots):
        for k, ref in enumerate(coded_refs):
            rows = ref[b * skel : (b + 1) * skel, :].astype(I32).astype(F32)
            turns[b, k] = turn(rows, inverse[base + b], to_column(scales[k][b : b + 1, :], diagonal))
    writes = []
    for b in range(slots):
        total = None
        for k in range(groups - 1):
            term = dot(turns[b, k], near[base + b, here ^ (k + 1)], NT)
            total = term if total is None else total + term
        out[b] = part_ref[base + b] + (total[:skel] + total[skel:])
        writes.append(pltpu.make_async_copy(out.at[b], out_ref.at[base + b], sems.at[b]))
        writes[-1].start()
    for copy in writes:
        copy.wait()


def couple(base, slots, near, inverse, part, coded, coupling):
    groups, unknowns = near.shape[1:3]
    skel = part.shape[1]
    args = [near, inverse, part, *coded] + ([] if coupling is None else [coupling])
    return pl.pallas_call(
        functools.partial(couple_kernel, base, groups),
        name="couple",
        out_shape=jax.ShapeDtypeStruct(part.shape, F32),
        in_specs=[VMEM] * (3 + len(coded)) + [HBM] * (coupling is not None),
        out_specs=HBM,
        input_output_aliases={} if coupling is None else {len(args) - 1: 0},
        scratch_shapes=[
            pltpu.VMEM((slots, skel, unknowns), F32),
            pltpu.VMEM((slots, groups - 1, 2 * skel, unknowns), BF16),
            pltpu.SemaphoreType.DMA((slots,)),
        ],
        compiler_params=pltpu.CompilerParams(vmem_limit_bytes=24 << 20),
    )(*args)


def swap(x, axis, size, k):
    return lax.ppermute(x, axis, [(i, i ^ k) for i in range(size)])


def send_all(merge, taken, pattern, proxy):
    cols = lax.axis_size("col")
    slots, skel = taken.shape
    width = proxy.shape[2]
    mask = jnp.repeat(pattern, width // pattern.shape[1], axis=1).astype(BF16)
    rows = jnp.take_along_axis(proxy, jnp.maximum(taken, 0)[:, :, None], axis=1) * mask[:, None, :]
    rows = jnp.where(taken[:, :, None] >= 0, rows, jnp.zeros_like(rows)).astype(F32)
    placed = jnp.zeros((cols // merge,) + rows.shape, F32)
    final = lax.axis_index("col") // merge
    placed = lax.dynamic_update_index_in_dim(placed, rows, final, 0)
    summed = lax.psum(placed, "col")
    rows = lax.dynamic_index_in_dim(summed, final, 0, keepdims=False).astype(BF16)
    return jnp.zeros((), bool), rows.reshape(slots * skel, width)


def local(proxy_rows, pattern, first_pivots, merge_pivots, send_counts, near_field, self_inverse):
    cols, groups = lax.axis_size("col"), lax.axis_size("grp")
    merge = 1 << min(5, cols.bit_length() - 1)
    slots, skel = first_pivots.shape[1:]
    proxy = proxy_rows[0]
    share = slots * skel // merge
    room = -(-(share * 4) // (3 * 32)) * 32
    blocks, counts = pattern[0].T, send_counts[0].T
    compact, where, taken, most, dense = route(
        merge, room, jnp.swapaxes(merge_pivots[0], 1, 2), jnp.swapaxes(first_pivots, 0, 1), blocks, proxy
    )

    pieces = {0: compact, 1: swap(compact, "col", cols, 1)}
    for k in range(2, merge, 2):
        pieces[k] = swap(compact, "col", cols, k)
    for k in range(2, merge, 2):
        pieces[k + 1] = swap(pieces[k], "col", cols, 1)
    pieces = [pieces[k] for k in range(merge)]
    choose, picks = aim(where, merge * room)
    dense = lax.while_loop(
        lambda now: now[0], lambda now: send_all(merge, taken, pattern[0], proxy), (most[0] >= room, dense)
    )[1]
    early = slots * 2 // 3 // 2 * 2
    chunks = ((0, early), (early, slots - early))
    interp = coupling = None
    codes, owns = [], []
    for base, count in chunks:
        interp, coded, own = solve(base, count, most, choose, picks, blocks, counts, dense, proxy, pieces, interp)
        codes.append([swap(coded, "grp", groups, k) for k in range(1, groups)])
        owns.append(own)
    near, part = own_part(near_field[0], self_inverse[0], counts, owns)
    for (base, count), coded in zip(chunks, codes):
        coupling = couple(base, count, near, self_inverse[0], part, coded, coupling)
    return (interp[None], coupling[None])


def solution(mesh):
    return jax.shard_map(
        local,
        mesh=mesh,
        in_specs=(
            P("grp", "col", None, None),
            P("grp", "col", None),
            P("grp", "col", None),
            P("grp", None, None, None, None),
            P("grp", "col", None),
            P("grp", "col", None, None, None),
            P("grp", "col", None, None),
        ),
        out_specs=(P("grp", "col", None, None), P("grp", "col", None, None)),
        check_vma=False,
    )
```
